32 devices in a mesh: dp: 8 (over z, x), tensor: 4 (over y, core).
Axes of the slice: x: 2, y: 2, z: 4, core: 2. Of those that a mesh axis runs over, the one named last changes fastest.
Arguments:
- token_ids: int32 [48, 512], P('dp'), may hold values from 0 to 50431
- lengths: int32 [48], P('dp'), may hold values from 128 to 512, as said below
- partners: int32 [48], replicated, may hold values from 0 to 47, as said below
- embedding: float32 [50432, 1024], P('dp', 'tensor'), may hold values from -0.18 to 0.18
- positions: float32 [514, 1024], P(None, 'tensor'), may hold values from -0.18 to 0.18
- attn_weights: float32 [4, 1024, 1024], P(None, None, 'tensor')
- ffn_weights: float32 [2, 1024, 4096], P(None, None, 'tensor')
- bias_qv: float32 [2, 1024], P(None, 'tensor'), may hold values from -1.8 to 1.8
- bias_up: float32 [4096], P('tensor'), may hold values from -1.8 to 1.8
- norms: float32 [8, 1024], replicated
- head_first: float32 [1024, 256], replicated, may hold values from -0.1875 to 0.1875
- head_second: float32 [256, 64], replicated, may hold values from -0.375 to 0.375
- head_bias: float32 [256], replicated, may hold values from -1.8 to 1.8
- mom_embedding: float32 [50432, 1024], P('dp', 'tensor'), may hold values from -5.9604645e-07 to 5.9604645e-07
- mom_positions: float32 [514, 1024], P(None, 'tensor'), may hold values from -5.9604645e-07 to 5.9604645e-07
- mom_attn: float32 [4, 1024, 1024], P(None, None, 'tensor'), may hold values from -5.9604645e-07 to 5.9604645e-07
- ffn_momentum: float32 [2, 1024, 4096], P(None, None, 'tensor'), may hold values from -5.9604645e-07 to 5.9604645e-07
- mom_bias_qv: float32 [2, 1024], P(None, 'tensor'), may hold values from -2.861023e-06 to 2.861023e-06
- mom_bias_up: float32 [4096], P('tensor'), may hold values from -2.861023e-06 to 2.861023e-06
- mom_norms: float32 [8, 1024], replicated, may hold values from -2.861023e-06 to 2.861023e-06
- mom_head_first: float32 [1024, 256], replicated, may hold values from -5.9604645e-07 to 5.9604645e-07
- mom_head_second: float32 [256, 64], replicated, may hold values from -5.9604645e-07 to 5.9604645e-07
- mom_head_bias: float32 [256], replicated, may hold values from -2.861023e-06 to 2.861023e-06
Outputs:
- new_embedding: float32 [50432, 1024], P('dp', 'tensor')
- new_positions: float32 [514, 1024], P(None, 'tensor')
- new_attn: float32 [4, 1024, 1024], P(None, None, 'tensor')
- new_ffn: float32 [2, 1024, 4096], P(None, None, 'tensor')
- new_bias_qv: float32 [2, 1024], P(None, 'tensor')
- new_bias_up: float32 [4096], P('tensor')
- new_norms: float32 [8, 1024], replicated
- new_head_first: float32 [1024, 256], replicated
- new_head_second: float32 [256, 64], replicated
- new_head_bias: float32 [256], replicated
- next_embedding: float32 [50432, 1024], P('dp', 'tensor')
- next_positions: float32 [514, 1024], P(None, 'tensor')
- next_attn: float32 [4, 1024, 1024], P(None, None, 'tensor')
- next_ffn: float32 [2, 1024, 4096], P(None, None, 'tensor')
- next_bias_qv: float32 [2, 1024], P(None, 'tensor')
- next_bias_up: float32 [4096], P('tensor')
- next_norms: float32 [8, 1024], replicated
- next_head_first: float32 [1024, 256], replicated
- next_head_second: float32 [256, 64], replicated
- next_head_bias: float32 [256], replicated
- loss: float32 [], replicated
- grad_norm: float32 [], replicated
The draws below stay inside these ranges and needn't reach their ends.
Inputs may be any that keep to these rules, and one draw needn't show every extreme that they name: `lengths`: every length is at least 128, and some sequence has exactly 512. partners pair the sequences: partners[partners[i]] = i and partners[i] != i.
All inputs are finite; a program needn't handle non-finite values.
Results may differ from the reference program's by a relative error of at most 0.0003.
Values sent between devices are 32-bit elements; how exact they have to be, the bound alone decides.
A program may use at most 384 MiB of HBM per device.

```python
import math
import jax
import jax.numpy as jnp
import numpy as np
from jax import lax

D = 1024
HEADS = 16
HEAD_DIM = 64
FF = 4096
POSITIONS = 514
VOCAB = 50432
HEAD_MID = 256
HEAD_OUT = 64
SEQ_LEN = 512
MIN_LEN = 128
SEQS = 48
PARAMS = 65044736


def draw_lengths(key, part):
    key_len, key_pick = jax.random.split(jax.random.fold_in(key, 11))
    drawn = jax.random.randint(key_len, (SEQS,), MIN_LEN, SEQ_LEN + 1)
    picked_rows = jax.random.randint(key_pick, (), 0, SEQS)
    return jnp.where(jnp.arange(SEQS) == picked_rows, SEQ_LEN, drawn).astype(jnp.int32)


def draw_partners(key, part):
    order = jax.random.permutation(jax.random.fold_in(key, 23), SEQS).astype(jnp.int32)
    even_slots = order[0::2]
    odd_slots = order[1::2]
    paired_rows = jnp.zeros((SEQS,), jnp.int32).at[even_slots].set(odd_slots).at[odd_slots].set(even_slots)
    return paired_rows.astype(jnp.int32)


def draw_norms(key, part):
    noise = jax.random.normal(jax.random.fold_in(key, 37), (8, D), jnp.float32)
    rows = jnp.arange(8)[:, None]
    is_gain = (rows % 2 == 0) & (rows < 6)
    return jnp.where(is_gain, 1.0 + 0.1 * noise, 0.2 * noise).astype(jnp.float32)


def draw_attn_weights(key, part):
    noise = jax.random.normal(jax.random.fold_in(key, 41), (4, D, D), jnp.float32)
    scale = jnp.where(jnp.arange(4) == 3, 16.0, 1.0)[:, None, None] / math.sqrt(D)
    return (noise * scale).astype(jnp.float32)


def draw_ffn_weights(key, part):
    noise = jax.random.normal(jax.random.fold_in(key, 43), (2, D, FF), jnp.float32)
    scale = jnp.where(jnp.arange(2) == 0, 1.0 / math.sqrt(D), 1.0 / math.sqrt(FF))[:, None, None]
    return (noise * scale).astype(jnp.float32)


def place_ends(result, stream_key, low, high):
    index_at = [jax.random.randint(jax.random.fold_in(stream_key, axis), (), 0, length) for axis, length in enumerate(result.shape)]
    longest = result.shape.index(max(result.shape))
    next_to = index_at[:longest] + [(index_at[longest] + 1) % result.shape[longest]] + index_at[longest + 1:]
    return result.at[tuple(index_at)].set(low).at[tuple(next_to)].set(high)


def steps_of(stream_key, extent, shards, low, largest):
    loudness = 1.0
    for dim, parts in shards:
        steps = jax.random.uniform(jax.random.fold_in(jax.random.fold_in(stream_key, 6), dim), (parts,), jnp.float32, low / len(shards), largest / len(shards))
        loudness = loudness * jnp.repeat(jnp.exp(steps), extent[dim] // parts).reshape((-1,) + (1,) * (len(extent) - 1 - dim))
    return loudness


def cumulative_ranks(amount, lean):
    loads = [(1 << 20) // math.isqrt(standing ** lean) + 1 for standing in range(1, amount + 1)]
    deviation = 1 + sum(loads) // (1 << 30)
    return np.cumsum(np.array([max(1, weight // deviation) for weight in loads]))


def ranked(rng, extent, number_of, skew):
    grid = cumulative_ranks(number_of, skew)
    ticket = jax.random.randint(jax.random.fold_in(rng, 1), extent, 0, int(grid[number_of - 1]))
    standing = jnp.searchsorted(jnp.asarray(grid, jnp.int32), ticket, side="right")
    return jax.random.permutation(jax.random.fold_in(rng, 2), number_of)[standing].astype(jnp.int32)


def scatter_about(stream_key, shape, scale, limit, pieces=(), held_as=jnp.bfloat16):
    entries = jax.random.normal(stream_key, shape, jnp.float32) * scale
    if len(pieces) > 0:
        entries = steps_of(stream_key, shape, pieces, -0.22, 0.18) * entries
    return jnp.clip(entries, min=-limit, max=limit).astype(held_as)


def setup_inputs(seed: int = 0) -> dict:
    splits = jax.random.split(jax.random.key(seed), 24)
    return {
        "token_ids": place_ends(ranked(splits[0], (SEQS, SEQ_LEN), VOCAB, 2), jax.random.fold_in(splits[0], 3), 0, VOCAB - 1).astype(jnp.int32),
        "lengths": draw_lengths(jax.random.fold_in(splits[23], 71), 0),
        "partners": draw_partners(jax.random.fold_in(splits[23], 71), 0),
        "embedding": scatter_about(splits[3], (VOCAB, D), 0.03, 0.18, ((0, 8), (1, 4)), jnp.float32),
        "positions": scatter_about(splits[4], (POSITIONS, D), 0.03, 0.18, ((1, 4),), jnp.float32),
        "attn_weights": draw_attn_weights(jax.random.fold_in(splits[23], 71), 0),
        "ffn_weights": draw_ffn_weights(jax.random.fold_in(splits[23], 71), 0),
        "bias_qv": scatter_about(splits[7], (2, D), 0.3, 1.8, ((1, 4),), jnp.float32),
        "bias_up": scatter_about(splits[8], (FF,), 0.3, 1.8, ((0, 4),), jnp.float32),
        "norms": draw_norms(jax.random.fold_in(splits[23], 71), 0),
        "head_first": scatter_about(splits[10], (D, HEAD_MID), D ** -0.5, 0.1875, (), jnp.float32),
        "head_second": scatter_about(splits[11], (HEAD_MID, HEAD_OUT), HEAD_MID ** -0.5, 0.375, (), jnp.float32),
        "head_bias": scatter_about(splits[12], (HEAD_MID,), 0.3, 1.8, (), jnp.float32),
        "mom_embedding": scatter_about(splits[13], (VOCAB, D), 0.00000011, 5.960464477539062e-07, ((0, 8), (1, 4)), jnp.float32),
        "mom_positions": scatter_about(splits[14], (POSITIONS, D), 0.00000011, 5.960464477539062e-07, ((1, 4),), jnp.float32),
        "mom_attn": scatter_about(splits[15], (4, D, D), 0.00000011, 5.960464477539062e-07, ((2, 4),), jnp.float32),
        "ffn_momentum": scatter_about(splits[16], (2, D, FF), 0.00000011, 5.960464477539062e-07, ((2, 4),), jnp.float32),
        "mom_bias_qv": scatter_about(splits[17], (2, D), 0.0000005, 2.86102294921875e-06, ((1, 4),), jnp.float32),
        "mom_bias_up": scatter_about(splits[18], (FF,), 0.0000005, 2.86102294921875e-06, ((0, 4),), jnp.float32),
        "mom_norms": scatter_about(splits[19], (8, D), 0.0000005, 2.86102294921875e-06, (), jnp.float32),
        "mom_head_first": scatter_about(splits[20], (D, HEAD_MID), 0.00000011, 5.960464477539062e-07, (), jnp.float32),
        "mom_head_second": scatter_about(splits[21], (HEAD_MID, HEAD_OUT), 0.00000011, 5.960464477539062e-07, (), jnp.float32),
        "mom_head_bias": scatter_about(splits[22], (HEAD_MID,), 0.0000005, 2.86102294921875e-06, (), jnp.float32),
    }


@jax.custom_vjp
def low(v):
    return lax.optimization_barrier(v.astype(jnp.bfloat16)).astype(jnp.float32)

@jax.custom_vjp
def low_back(v):
    return v

def lowered_keep(v):
    return (low(v), None)

def low_pass(kept, grad):
    return (grad,)

def back_keep(v):
    return (v, None)

def back_low(kept, grad):
    return (low(grad),)
low.defvjp(lowered_keep, low_pass)
low_back.defvjp(back_keep, back_low)
EPS = 1e-05
SOFTMAX_TEMP = 0.1
DECAY = 0.9
RATE = 100000.0
CLIP_SCALE = 1e-06
HIGH = lax.Precision.HIGHEST

def precise_product(left, right):
    return jnp.dot(left, right, precision=HIGH)

def norm_rows(values, gain, shift):
    center = values - lax.optimization_barrier(jnp.mean(values, axis=-1, keepdims=True))
    spread = lax.optimization_barrier(jnp.mean(center * center, axis=-1, keepdims=True))
    return center * lax.rsqrt(spread + EPS) * gain + shift

def encode(embedded, length, attn, ffn, bias_qv, bias_up, norms):
    h_zero = norm_rows(embedded, norms[0], norms[1])
    queries = (precise_product(h_zero, attn[0]) + bias_qv[0]).reshape(SEQ_LEN, HEADS, HEAD_DIM)
    keys_all = precise_product(h_zero, attn[1]).reshape(SEQ_LEN, HEADS, HEAD_DIM)
    values = (precise_product(h_zero, attn[2]) + bias_qv[1]).reshape(SEQ_LEN, HEADS, HEAD_DIM)
    scores = jnp.einsum('qhd,khd->hqk', queries, keys_all, precision=HIGH) / math.sqrt(HEAD_DIM)
    valid = jnp.arange(SEQ_LEN) < length
    scores = jnp.where(valid[None, None, :], scores, -1e+30)
    probs = jax.nn.softmax(scores, axis=-1)
    mixed = jnp.einsum('hqk,khd->qhd', probs, values, precision=HIGH).reshape(SEQ_LEN, D)
    x_one = h_zero + precise_product(mixed, attn[3].T) + norms[6]
    h_one = norm_rows(x_one, norms[2], norms[3])
    hidden = jax.nn.gelu(precise_product(h_one, ffn[0]) + bias_up, approximate=False)
    x_two = h_one + precise_product(hidden, ffn[1].T) + norms[7]
    h_two = norm_rows(x_two, norms[4], norms[5])
    keep = valid.astype(jnp.float32)
    return lax.optimization_barrier(jnp.sum(h_two * keep[:, None], axis=0)) / length.astype(jnp.float32)

def contrast(pooled, head_first, head_second, head_bias, partners):
    middle = jax.nn.gelu(precise_product(pooled, head_first) + head_bias, approximate=False)
    output = precise_product(middle, head_second)
    unit_vectors = output * lax.rsqrt(lax.optimization_barrier(jnp.sum(output * output, axis=-1, keepdims=True)) + 1e-06)
    similarity_scores = precise_product(unit_vectors, unit_vectors.T) / SOFTMAX_TEMP
    count = similarity_scores.shape[0]
    index = jnp.arange(count)
    similarity_scores = jnp.where(index[:, None] == index[None, :], -1e+30, similarity_scores)
    totals = jax.nn.logsumexp(similarity_scores, axis=-1)
    paired_rows = lax.optimization_barrier(jnp.sum(jnp.where(index[None, :] == partners[:, None], similarity_scores, 0.0), axis=-1))
    return jnp.sum(totals - paired_rows)

def forward(token_ids, lengths, partners, embedding, positions, attn, ffn, bias_qv, bias_up, norms, head_first, head_second, head_bias):
    embedded = jnp.take(embedding, token_ids, axis=0) + positions[2:SEQ_LEN + 2][None]
    encoder = jax.checkpoint(encode)

    def one_seq(item):
        return encoder(item[0], item[1], attn, ffn, bias_qv, bias_up, norms)
    pooled = lax.map(one_seq, (embedded, lengths))
    return contrast(pooled, head_first, head_second, head_bias, partners)

def reference(token_ids, lengths, partners, embedding, positions, attn_weights, ffn_weights, bias_qv, bias_up, norms, head_first, head_second, head_bias, mom_embedding, mom_positions, mom_attn, ffn_momentum, mom_bias_qv, mom_bias_up, mom_norms, mom_head_first, mom_head_second, mom_head_bias):
    weights = (embedding, positions, attn_weights, ffn_weights, bias_qv, bias_up, norms, head_first, head_second, head_bias)
    moments = (mom_embedding, mom_positions, mom_attn, ffn_momentum, mom_bias_qv, mom_bias_up, mom_norms, mom_head_first, mom_head_second, mom_head_bias)

    def loss_of(*params):
        return forward(token_ids, lengths, partners, *params)
    loss, pull = jax.vjp(loss_of, *weights)
    grads = pull(jnp.ones_like(loss))
    total = jnp.sum(jnp.stack([jnp.sum(grad * grad) for grad in grads]))
    grad_norm = jnp.sqrt(total)
    factor = jnp.minimum(1.0, CLIP_SCALE * math.sqrt(PARAMS) / (grad_norm + 1e-06))
    new_weights = []
    new_moments = []
    for weight, moment, grad in zip(weights, moments, grads):
        clipped = factor * grad
        moment_new = DECAY * moment + (1.0 - DECAY) * clipped
        new_weights.append(weight - RATE * (DECAY * moment_new + (1.0 - DECAY) * clipped))
        new_moments.append(moment_new)
    return (new_weights[0], new_weights[1], new_weights[2], new_weights[3], new_weights[4], new_weights[5], new_weights[6], new_weights[7], new_weights[8], new_weights[9], new_moments[0], new_moments[1], new_moments[2], new_moments[3], new_moments[4], new_moments[5], new_moments[6], new_moments[7], new_moments[8], new_moments[9], loss, grad_norm)
```

```python
import functools
import math

import jax
import jax.numpy as jnp
from jax import lax
from jax.sharding import PartitionSpec as P

HEAD_DIM = 64
PARAMS = 65044736


EPS = 1e-05
SOFTMAX_TEMP = 0.1
DECAY = 0.9
RATE = 100000.0
CLIP_SCALE = 1e-06
HIGH = lax.Precision.HIGHEST
PRODUCT = lax.Precision.HIGH
CAPACITY = 96


def precise_product(left, right):
    return jnp.matmul(left, right, precision=HIGH)


def norm_rows(values, gain, shift):
    center = values - jnp.mean(values, axis=-1, keepdims=True)
    spread = jnp.mean(center * center, axis=-1, keepdims=True)
    return center * lax.rsqrt(spread + EPS) * gain + shift


def attend(normed, lengths, attn, bias_qv):
    seqs, slots, width = normed.shape
    cols = attn.shape[2]
    heads = cols // HEAD_DIM
    queries = (precise_product(normed, attn[0]) + bias_qv[0]).reshape(seqs, slots, heads, HEAD_DIM)
    keys_all = precise_product(normed, attn[1]).reshape(seqs, slots, heads, HEAD_DIM)
    values = (precise_product(normed, attn[2]) + bias_qv[1]).reshape(seqs, slots, heads, HEAD_DIM)
    scores = jnp.einsum("sqhd,skhd->shqk", queries, keys_all, precision=HIGH) / math.sqrt(HEAD_DIM)
    valid = lax.broadcasted_iota(jnp.int32, (seqs, slots), 1) < lengths[:, None]
    scores = jnp.where(valid[:, None, None, :], scores, -1e30)
    probs = jax.nn.softmax(scores, axis=-1)
    mixed = jnp.einsum("shqk,skhd->sqhd", probs, values, precision=HIGH).reshape(seqs, slots, cols)
    return precise_product(mixed, attn[3].T)


def expand(normed, ffn, bias_up):
    hidden = jax.nn.gelu(precise_product(normed, ffn[0]) + bias_up, approximate=False)
    return precise_product(hidden, ffn[1].T)


def contrast(pooled, head_first, head_second, head_bias, partners):
    middle = jax.nn.gelu(precise_product(pooled, head_first) + head_bias, approximate=False)
    output = precise_product(middle, head_second)
    unit_vectors = output * lax.rsqrt(jnp.sum(output * output, axis=-1, keepdims=True) + 1e-06)
    similarity_scores = precise_product(unit_vectors, unit_vectors.T) / SOFTMAX_TEMP
    count = similarity_scores.shape[0]
    index = lax.broadcasted_iota(jnp.int32, (count,), 0)
    similarity_scores = jnp.where(index[:, None] == index[None, :], -1e30, similarity_scores)
    totals = jax.nn.logsumexp(similarity_scores, axis=-1)
    paired_rows = jnp.sum(
        jnp.where(index[None, :] == partners[:, None], similarity_scores, 0.0), axis=-1
    )
    return jnp.sum(totals - paired_rows)


def owner_rows(ids_part, base, vocab_rows):
    local_ids = ids_part - base
    inside = (local_ids >= 0) & (local_ids < vocab_rows)
    return jnp.where(inside, local_ids, vocab_rows)


def advance(weight, moment, grad, factor):
    clipped = factor * grad
    moment_new = DECAY * moment + (1.0 - DECAY) * clipped
    return (weight - RATE * (DECAY * moment_new + (1.0 - DECAY) * clipped), moment_new)


def squares(array):
    return jnp.sum(array * array)


def on_device(
    token_ids,
    lengths,
    partners,
    embedding,
    positions,
    attn_weights,
    ffn_weights,
    bias_qv,
    bias_up,
    norms,
    head_first,
    head_second,
    head_bias,
    mom_embedding,
    mom_positions,
    mom_attn,
    ffn_momentum,
    mom_bias_qv,
    mom_bias_up,
    mom_norms,
    mom_head_first,
    mom_head_second,
    mom_head_bias,
):
    seqs, slots = token_ids.shape
    vocab_rows, cols = embedding.shape
    dp_rank = lax.axis_index("dp")
    tp_rank = lax.axis_index("tensor")
    base = dp_rank * vocab_rows
    all_ids = lax.all_gather(token_ids, "dp", axis=0, tiled=True).reshape(-1)
    padded_table = jnp.concatenate([embedding, jnp.zeros((1, cols), jnp.float32)], axis=0)
    rows_ids = owner_rows(all_ids, base, vocab_rows)
    token_rows = lax.psum_scatter(
        jnp.take(padded_table, rows_ids, axis=0), "dp", scatter_dimension=0, tiled=True
    )
    token_cols = token_rows.reshape(seqs, slots, cols) + positions[2 : slots + 2][None]
    embedded = lax.all_gather(token_cols, "tensor", axis=2, tiled=True)
    h_zero, ln_zero_pull = jax.vjp(norm_rows, embedded, norms[0], norms[1])
    attn_part, attn_pull = jax.vjp(
        lambda normed, weights, biases: attend(normed, lengths, weights, biases),
        h_zero,
        attn_weights,
        bias_qv,
    )
    x_one = h_zero + lax.psum(attn_part, "tensor") + norms[6]
    h_one, ln_one_pull = jax.vjp(norm_rows, x_one, norms[2], norms[3])
    ffn_part, ffn_pull = jax.vjp(expand, h_one, ffn_weights, bias_up)
    x_two = h_one + lax.psum(ffn_part, "tensor") + norms[7]
    h_two, ln_two_pull = jax.vjp(norm_rows, x_two, norms[4], norms[5])
    valid = (lax.broadcasted_iota(jnp.int32, (seqs, slots), 1) < lengths[:, None]).astype(
        jnp.float32
    )
    len_float = lengths.astype(jnp.float32)
    pooled = jnp.sum(h_two * valid[:, :, None], axis=1) / len_float[:, None]
    all_pooled = lax.all_gather(pooled, "dp", axis=0, tiled=True)
    loss, head_pull = jax.vjp(
        lambda rows, first_w, second_w, bias_w: contrast(rows, first_w, second_w, bias_w, partners),
        all_pooled,
        head_first,
        head_second,
        head_bias,
    )
    back_pooled_all, grad_head_first, grad_head_second, grad_head_bias = head_pull(
        jnp.ones_like(loss)
    )
    back_pooled = lax.dynamic_slice_in_dim(back_pooled_all, dp_rank * seqs, seqs)
    back_h_two = valid[:, :, None] * (back_pooled / len_float[:, None])[:, None, :]
    back_x_two, grad_gain_two, grad_shift_two = ln_two_pull(back_h_two)
    back_h_one_part, grad_ffn, grad_bias_up = ffn_pull(back_x_two)
    back_h_one = back_x_two + lax.psum(back_h_one_part, "tensor")
    back_x_one, grad_gain_one, grad_shift_one = ln_one_pull(back_h_one)
    back_h_zero_part, grad_attn, grad_bias_qv = attn_pull(back_x_one)
    back_h_zero = back_x_one + lax.psum(back_h_zero_part, "tensor")
    back_embedded, grad_gain_zero, grad_shift_zero = ln_zero_pull(back_h_zero)
    back_cols = lax.dynamic_slice_in_dim(back_embedded, tp_rank * cols, cols, 2)
    grad_positions = jnp.pad(
        jnp.sum(back_cols, axis=0), ((2, positions.shape[0] - slots - 2), (0, 0))
    )
    grad_norms = jnp.stack(
        [
            grad_gain_zero,
            grad_shift_zero,
            grad_gain_one,
            grad_shift_one,
            grad_gain_two,
            grad_shift_two,
            jnp.sum(back_x_one, axis=(0, 1)),
            jnp.sum(back_x_two, axis=(0, 1)),
        ]
    )
    back_flat = back_cols.reshape(seqs * slots, cols)
    target = owner_rows(all_ids, base, vocab_rows)
    grad_embedding = jax.ops.segment_sum(
        lax.all_gather(back_flat, "dp", axis=0, tiled=True), target, num_segments=vocab_rows + 1
    )[:vocab_rows]
    first_dp = (dp_rank == 0).astype(jnp.float32)
    first_all = first_dp * (tp_rank == 0).astype(jnp.float32)
    grad_attn, grad_ffn, grad_positions, grad_bias_qv, grad_bias_up, grad_norms = lax.psum(
        (grad_attn, grad_ffn, grad_positions, grad_bias_qv, grad_bias_up, grad_norms), "dp"
    )
    big_squares = first_dp * (squares(grad_attn) + squares(grad_ffn))
    local_squares = (
        big_squares
        + squares(grad_embedding)
        + first_dp * (squares(grad_positions) + squares(grad_bias_qv) + squares(grad_bias_up))
        + first_all
        * (
            squares(grad_norms)
            + squares(grad_head_first)
            + squares(grad_head_second)
            + squares(grad_head_bias)
        )
    )
    total_squares = lax.psum(local_squares, ("dp", "tensor"))
    grad_norm = jnp.sqrt(total_squares)
    factor = jnp.minimum(1.0, CLIP_SCALE * math.sqrt(PARAMS) / (grad_norm + 1e-06))
    new_attn, next_attn = advance(attn_weights, mom_attn, grad_attn, factor)
    new_ffn, next_ffn = advance(ffn_weights, ffn_momentum, grad_ffn, factor)
    new_embedding, next_embedding = advance(embedding, mom_embedding, grad_embedding, factor)
    new_positions, next_positions = advance(positions, mom_positions, grad_positions, factor)
    new_bias_qv, next_bias_qv = advance(bias_qv, mom_bias_qv, grad_bias_qv, factor)
    new_bias_up, next_bias_up = advance(bias_up, mom_bias_up, grad_bias_up, factor)
    new_norms, next_norms = advance(norms, mom_norms, grad_norms, factor)
    new_head_first, next_head_first = advance(head_first, mom_head_first, grad_head_first, factor)
    new_head_second, next_head_second = advance(
        head_second, mom_head_second, grad_head_second, factor
    )
    new_head_bias, next_head_bias = advance(head_bias, mom_head_bias, grad_head_bias, factor)
    return (
        new_embedding,
        new_positions,
        new_attn,
        new_ffn,
        new_bias_qv,
        new_bias_up,
        new_norms,
        new_head_first,
        new_head_second,
        new_head_bias,
        next_embedding,
        next_positions,
        next_attn,
        next_ffn,
        next_bias_qv,
        next_bias_up,
        next_norms,
        next_head_first,
        next_head_second,
        next_head_bias,
        loss,
        grad_norm,
    )


def normalise(values):
    center = values - jnp.mean(values, axis=-1, keepdims=True)
    scale = lax.rsqrt(jnp.mean(center * center, axis=-1, keepdims=True) + EPS)
    return center * scale, scale


def normalise_back(back, gain, unit, scale):
    inner = back * gain
    grad = scale * (
        inner
        - jnp.mean(inner, axis=-1, keepdims=True)
        - unit * jnp.mean(inner * unit, axis=-1, keepdims=True)
    )
    return grad, jnp.sum(back * unit, axis=0), jnp.sum(back, axis=0)


def gelu_both(values):
    cdf = 0.5 * (1.0 + lax.erf(values * math.sqrt(0.5)))
    pdf = jnp.exp(-0.5 * values * values) * (1.0 / math.sqrt(2.0 * math.pi))
    return values * cdf, cdf + values * pdf


def product(subscripts, left, right):
    return jnp.einsum(subscripts, left, right, precision=PRODUCT)


def request_lists(ids, vocab_rows, owners):
    count = ids.shape[0]
    index = lax.broadcasted_iota(jnp.int32, (count,), 0)
    earlier = index[None, :] < index[:, None]
    same = (ids[None, :] == ids[:, None]) & earlier
    first = jnp.logical_not(jnp.any(same, axis=1))
    owner = ids // vocab_rows
    ahead = (owner[None, :] == owner[:, None]) & earlier & first[None, :]
    rank = jnp.sum(ahead.astype(jnp.int32), axis=1)
    return owner, jnp.where(first, rank, -1)


def round_list(ids, owner, rank, round_index, owners):
    place = rank - round_index * CAPACITY
    inside = (rank >= 0) & (place >= 0) & (place < CAPACITY)
    place = jnp.where(inside, owner * CAPACITY + place, -1)
    wanted = lax.broadcasted_iota(jnp.int32, (owners * CAPACITY, 1), 0)
    return jnp.sum(jnp.where(place[None, :] == wanted, ids[None, :] + 1, 0), axis=1) - 1


def trade(block):
    return lax.all_to_all(block, ("dp", "tensor"), 0, 0, tiled=True)


def fast_on_device(
    token_ids, lengths, partners, embedding, positions, attn_weights, ffn_weights, bias_qv, bias_up, norms,
    head_first, head_second, head_bias, mom_embedding, mom_positions, mom_attn, ffn_momentum, mom_bias_qv,
    mom_bias_up, mom_norms, mom_head_first, mom_head_second, mom_head_bias, *, groups, shards
):
    seqs, slots = token_ids.shape
    half = slots // 2
    vocab_rows, cols = embedding.shape
    width = cols * shards
    devices = groups * shards
    hidden = bias_up.shape[0]
    heads = width // HEAD_DIM
    dp_rank = lax.axis_index("dp")
    tp_rank = lax.axis_index("tensor")
    pair = tp_rank // 2
    side = tp_rank % 2
    base = dp_rank * vocab_rows

    whole_seq = 3 * pair + 2 * side
    split_seq = 3 * pair + 1
    whole_ids = lax.dynamic_index_in_dim(token_ids, whole_seq, 0, keepdims=False)
    split_ids = lax.dynamic_index_in_dim(token_ids, split_seq, 0, keepdims=False)
    ids = jnp.concatenate([whole_ids, lax.dynamic_slice_in_dim(split_ids, side * half, half)])
    count = ids.shape[0]
    whole_length = lax.dynamic_index_in_dim(lengths, whole_seq, 0, keepdims=False)
    split_length = lax.dynamic_index_in_dim(lengths, split_seq, 0, keepdims=False)

    all_attn = lax.all_gather(attn_weights, "tensor")
    all_ffn_up = lax.all_gather(ffn_weights[0], "tensor")
    all_ffn_down = lax.all_gather(ffn_weights[1], "tensor")
    small = jnp.concatenate([positions[2 : slots + 2], bias_qv, bias_up.reshape(-1, cols)], axis=0)
    all_small = lax.all_gather(small, "tensor")
    all_positions = all_small[:, :slots].transpose(1, 0, 2).reshape(slots, width)
    all_bias_qv = all_small[:, slots : slots + 2].transpose(1, 0, 2).reshape(2, width)
    all_bias_up = all_small[:, slots + 2 :].reshape(-1)

    owner, rank = request_lists(ids, vocab_rows, groups)
    rounds_here = jnp.max(rank) // CAPACITY + 1

    def serve(round_index):
        wanted = round_list(ids, owner, rank, round_index, groups)
        lists = jnp.broadcast_to(wanted.reshape(groups, 1, CAPACITY), (groups, shards, CAPACITY))
        lists = lists.reshape(devices, CAPACITY)
        tail = jnp.broadcast_to(rounds_here, (devices, 1)).astype(jnp.int32)
        lists = jnp.concatenate([lists, tail, jnp.zeros((devices, 127 - CAPACITY % 128), jnp.int32)], axis=1)
        asked = trade(lists)
        rows = asked[:, :CAPACITY].reshape(-1) - base
        rounds = jnp.max(asked[:, CAPACITY])
        return wanted, rows, rounds

    def fetch(wanted, rows):
        found = jnp.take(embedding, rows, axis=0, mode="clip")
        landed = trade(found).reshape(groups, shards, CAPACITY, cols)
        landed = landed.transpose(0, 2, 1, 3).reshape(groups * CAPACITY, width)
        chosen = (ids[:, None] == wanted[None, :]).astype(jnp.float32)
        return jnp.matmul(chosen, landed, precision=HIGH)

    wanted_first, rows_first, rounds = serve(0)
    tokens = fetch(wanted_first, rows_first)

    def more(state):
        return state[0] < rounds

    def fetch_more(state):
        round_index, total = state
        wanted, rows, _ = serve(round_index)
        return round_index + 1, total + fetch(wanted, rows)

    _, tokens = lax.while_loop(more, fetch_more, (jnp.int32(1), tokens))
    own_positions = jnp.concatenate(
        [all_positions, lax.dynamic_slice_in_dim(all_positions, side * half, half)], axis=0
    )
    embedded = tokens + own_positions
    unit_zero, scale_zero = normalise(embedded)
    h_zero = unit_zero * norms[0] + norms[1]

    swap = [(i, i ^ 1) for i in range(shards)]
    h_other = lax.ppermute(h_zero[slots:], "tensor", swap)
    h_keys = jnp.concatenate([h_zero, h_other], axis=0)
    queries = product("td,jdc->tjc", h_zero, all_attn[:, 0]).reshape(count, width) + all_bias_qv[0]
    keys_all = product("td,jdc->tjc", h_keys, all_attn[:, 1]).reshape(count + half, width)
    values = product("td,jdc->tjc", h_keys, all_attn[:, 2]).reshape(count + half, width) + all_bias_qv[1]
    key_index = lax.broadcasted_iota(jnp.int32, (slots,), 0)
    own_first = jnp.where(
        key_index < half, side * half + key_index, (1 - side) * half + key_index - half
    )
    root = 1.0 / math.sqrt(HEAD_DIM)

    def split_heads(array):
        return array.reshape(-1, heads, HEAD_DIM)

    def attend_block(q, k, v, valid):
        scores = product("qhd,khd->hqk", q, k) * root
        scores = jnp.where(valid[None, None, :], scores, -1e30)
        probs = jnp.exp(scores - jnp.max(scores, axis=-1, keepdims=True))
        probs = probs / jnp.sum(probs, axis=-1, keepdims=True)
        return probs, product("hqk,khd->qhd", probs, v)

    q_whole, q_split = split_heads(queries[:slots]), split_heads(queries[slots:])
    k_whole, k_split = split_heads(keys_all[:slots]), split_heads(keys_all[slots:])
    v_whole, v_split = split_heads(values[:slots]), split_heads(values[slots:])
    p_whole, a_whole = attend_block(q_whole, k_whole, v_whole, key_index < whole_length)
    p_split, a_split = attend_block(q_split, k_split, v_split, own_first < split_length)
    mixed = jnp.concatenate([a_whole.reshape(slots, width), a_split.reshape(half, width)], axis=0)
    mixed_parts = mixed.reshape(count, shards, cols)
    x_one = h_zero + product("tjc,jdc->td", mixed_parts, all_attn[:, 3]) + norms[6]
    unit_one, scale_one = normalise(x_one)
    h_one = unit_one * norms[2] + norms[3]

    up = product("td,jdc->tjc", h_one, all_ffn_up) + all_bias_up.reshape(shards, hidden)
    act, act_slope = gelu_both(up)
    x_two = h_one + product("tjc,jdc->td", act, all_ffn_down) + norms[7]
    unit_two, scale_two = normalise(x_two)
    h_two = unit_two * norms[4] + norms[5]

    slot = lax.broadcasted_iota(jnp.int32, (count,), 0)
    in_whole = slot < slots
    place = jnp.where(in_whole, slot, slot - slots + side * half)
    keep = place < jnp.where(in_whole, whole_length, split_length)
    weight_whole = jnp.where(keep & in_whole, 1.0 / whole_length.astype(jnp.float32), 0.0)
    weight_split = jnp.where(keep & ~in_whole, 1.0 / split_length.astype(jnp.float32), 0.0)
    sums = jnp.stack(
        [jnp.sum(h_two * weight_whole[:, None], axis=0), jnp.sum(h_two * weight_split[:, None], axis=0)]
    )
    all_sums = lax.all_gather(sums, ("dp", "tensor")).reshape(groups * shards // 2, 2, 2, width)
    all_pooled = jnp.stack(
        [all_sums[:, 0, 0], all_sums[:, 0, 1] + all_sums[:, 1, 1], all_sums[:, 1, 0]], axis=1
    ).reshape(groups * seqs, width)
    loss, head_pull = jax.vjp(
        lambda rows, first_w, second_w, bias_w: contrast(rows, first_w, second_w, bias_w, partners),
        all_pooled,
        head_first,
        head_second,
        head_bias,
    )
    back_pooled, grad_head_first, grad_head_second, grad_head_bias = head_pull(jnp.ones_like(loss))
    first_row = dp_rank * seqs
    back_whole = lax.dynamic_index_in_dim(back_pooled, first_row + whole_seq, 0, keepdims=False)
    back_split = lax.dynamic_index_in_dim(back_pooled, first_row + split_seq, 0, keepdims=False)
    back_h_two = weight_whole[:, None] * back_whole[None, :] + weight_split[:, None] * back_split[None, :]

    back_x_two, grad_gain_two, grad_shift_two = normalise_back(back_h_two, norms[4], unit_two, scale_two)
    grad_down = product("td,tjc->jdc", back_x_two, act)
    sum_down = lax.psum_scatter(grad_down, "tensor", scatter_dimension=0, tiled=False)
    back_up = product("td,jdc->tjc", back_x_two, all_ffn_down) * act_slope
    grad_up = product("td,tjc->jdc", h_one, back_up)
    sum_up = lax.psum_scatter(grad_up, "tensor", scatter_dimension=0, tiled=False)
    grad_bias_up = jnp.sum(back_up, axis=0)
    back_h_one = back_x_two + product("tjc,jdc->td", back_up, all_ffn_up)
    back_x_one, grad_gain_one, grad_shift_one = normalise_back(back_h_one, norms[2], unit_one, scale_one)

    back_mixed_parts = product("td,jdc->tjc", back_x_one, all_attn[:, 3])
    grad_out = product("td,tjc->jdc", back_x_one, mixed_parts)
    back_mixed = back_mixed_parts.reshape(count, width)

    def attend_back(q, k, v, probs, mixed_block, back):
        back_v = product("hqk,qhd->khd", probs, back)
        back_p = product("qhd,khd->hqk", back, v)
        inner = jnp.sum(back * mixed_block, axis=-1).T
        back_s = probs * (back_p - inner[:, :, None]) * root
        return product("hqk,khd->qhd", back_s, k), product("hqk,qhd->khd", back_s, q), back_v

    dq_whole, dk_whole, dv_whole = attend_back(
        q_whole, k_whole, v_whole, p_whole, a_whole, split_heads(back_mixed[:slots])
    )
    dq_split, dk_split, dv_split = attend_back(
        q_split, k_split, v_split, p_split, a_split, split_heads(back_mixed[slots:])
    )
    back_q = jnp.concatenate([dq_whole, dq_split], axis=0).reshape(count, shards, cols)
    back_k = jnp.concatenate([dk_whole, dk_split], axis=0).reshape(count + half, shards, cols)
    back_v = jnp.concatenate([dv_whole, dv_split], axis=0).reshape(count + half, shards, cols)
    back_keys = product("tjc,jdc->td", back_k, all_attn[:, 1]) + product("tjc,jdc->td", back_v, all_attn[:, 2])
    back_other = lax.ppermute(back_keys[count:], "tensor", swap)
    grad_q = product("td,tjc->jdc", h_zero, back_q)
    grad_k = product("td,tjc->jdc", h_keys, back_k)
    grad_v = product("td,tjc->jdc", h_keys, back_v)
    back_h_zero = back_x_one + product("tjc,jdc->td", back_q, all_attn[:, 0]) + back_keys[:count]
    back_h_zero = back_h_zero + jnp.pad(back_other, ((slots, 0), (0, 0)))
    back_embedded, grad_gain_zero, grad_shift_zero = normalise_back(back_h_zero, norms[0], unit_zero, scale_zero)

    def give_back(wanted, rows, listed, total):
        chosen = (wanted[:, None] == ids[None, :]).astype(jnp.float32)
        summed = jnp.matmul(chosen, back_embedded, precision=HIGH)
        parts = summed.reshape(groups, CAPACITY, shards, cols).transpose(0, 2, 1, 3)
        landed = trade(parts.reshape(devices * CAPACITY, cols))
        target = jnp.where(rows >= 0, rows, vocab_rows)
        return total.at[target].add(landed, mode="drop")

    zero_table = jnp.zeros((vocab_rows, cols), jnp.float32)
    grad_embedding = give_back(wanted_first, rows_first, None, zero_table)

    def give_more(state):
        round_index, total = state
        wanted, rows, _ = serve(round_index)
        return round_index + 1, give_back(wanted, rows, None, total)

    _, grad_embedding = lax.while_loop(more, give_more, (jnp.int32(1), grad_embedding))

    half_rows = jnp.where(side == 0, 1.0, 0.0) * back_embedded[slots:]
    other_rows = back_embedded[slots:] - half_rows
    grad_pos_full = back_embedded[:slots] + jnp.concatenate([half_rows, other_rows], axis=0)
    grad_pos_parts = grad_pos_full.reshape(slots, shards, cols).transpose(1, 0, 2)
    grad_attn_parts = jnp.concatenate([grad_q, grad_k, grad_v, grad_out, grad_pos_parts], axis=1)
    sum_attn = lax.psum_scatter(grad_attn_parts, "tensor", scatter_dimension=0, tiled=False)
    with jax.named_scope("sum_ffn_down"):
        sum_down = lax.psum(sum_down, "dp")
    sum_down, sum_up = lax.optimization_barrier((sum_down, sum_up))
    sum_up = lax.psum(sum_up, "dp")
    sum_up, sum_attn = lax.optimization_barrier((sum_up, sum_attn))
    sum_attn = lax.psum(sum_attn, "dp")
    grad_small = jnp.concatenate(
        [
            jnp.stack(
                [
                    grad_gain_zero,
                    grad_shift_zero,
                    grad_gain_one,
                    grad_shift_one,
                    grad_gain_two,
                    grad_shift_two,
                    jnp.sum(back_x_one, axis=0),
                    jnp.sum(back_x_two, axis=0),
                    jnp.sum(back_q, axis=0).reshape(-1),
                    jnp.sum(back_v, axis=0).reshape(-1),
                ]
            ),
            grad_bias_up.reshape(-1, width),
        ],
        axis=0,
    )
    sum_small = lax.psum(grad_small, ("dp", "tensor"))
    grad_norms = sum_small[:8]
    grad_bias_qv = lax.dynamic_slice_in_dim(sum_small[8:10], tp_rank * cols, cols, 1)
    grad_bias_up = lax.dynamic_slice_in_dim(sum_small[10:].reshape(-1), tp_rank * hidden, hidden)
    grad_attn = sum_attn[: 4 * width].reshape(4, width, cols)
    grad_ffn_up, grad_ffn_down = sum_up, sum_down
    grad_pos = sum_attn[4 * width :]

    first_dp = (dp_rank == 0).astype(jnp.float32)
    first_all = first_dp * (tp_rank == 0).astype(jnp.float32)
    local_squares = (
        squares(grad_embedding)
        + first_dp
        * (
            squares(sum_attn)
            + squares(grad_ffn_up)
            + squares(grad_ffn_down)
            + squares(grad_bias_qv)
            + squares(grad_bias_up)
        )
        + first_all
        * (
            squares(grad_norms)
            + squares(grad_head_first)
            + squares(grad_head_second)
            + squares(grad_head_bias)
        )
    )
    grad_norm = jnp.sqrt(lax.psum(local_squares, ("dp", "tensor")))
    factor = jnp.minimum(1.0, CLIP_SCALE * math.sqrt(PARAMS) / (grad_norm + 1e-06))
    grad_positions = jnp.pad(grad_pos, ((2, positions.shape[0] - slots - 2), (0, 0)))
    grad_ffn = jnp.stack([grad_ffn_up, grad_ffn_down])
    new_embedding, next_embedding = advance(embedding, mom_embedding, grad_embedding, factor)
    new_positions, next_positions = advance(positions, mom_positions, grad_positions, factor)
    new_attn, next_attn = advance(attn_weights, mom_attn, grad_attn, factor)
    new_ffn, next_ffn = advance(ffn_weights, ffn_momentum, grad_ffn, factor)
    new_bias_qv, next_bias_qv = advance(bias_qv, mom_bias_qv, grad_bias_qv, factor)
    new_bias_up, next_bias_up = advance(bias_up, mom_bias_up, grad_bias_up, factor)
    new_norms, next_norms = advance(norms, mom_norms, grad_norms, factor)
    new_head_first, next_head_first = advance(head_first, mom_head_first, grad_head_first, factor)
    new_head_second, next_head_second = advance(head_second, mom_head_second, grad_head_second, factor)
    new_head_bias, next_head_bias = advance(head_bias, mom_head_bias, grad_head_bias, factor)
    return (
        new_embedding, new_positions, new_attn, new_ffn, new_bias_qv, new_bias_up, new_norms, new_head_first,
        new_head_second, new_head_bias, next_embedding, next_positions, next_attn, next_ffn, next_bias_qv,
        next_bias_up, next_norms, next_head_first, next_head_second, next_head_bias, loss, grad_norm,
    )


def solution(mesh):
    in_specs = (
        P("dp", None),
        P("dp"),
        P(),
        P("dp", "tensor"),
        P(None, "tensor"),
        P(None, None, "tensor"),
        P(None, None, "tensor"),
        P(None, "tensor"),
        P("tensor"),
        P(),
        P(),
        P(),
        P(),
        P("dp", "tensor"),
        P(None, "tensor"),
        P(None, None, "tensor"),
        P(None, None, "tensor"),
        P(None, "tensor"),
        P("tensor"),
        P(),
        P(),
        P(),
        P(),
    )
    out_specs = (
        P("dp", "tensor"),
        P(None, "tensor"),
        P(None, None, "tensor"),
        P(None, None, "tensor"),
        P(None, "tensor"),
        P("tensor"),
        P(),
        P(),
        P(),
        P(),
        P("dp", "tensor"),
        P(None, "tensor"),
        P(None, None, "tensor"),
        P(None, None, "tensor"),
        P(None, "tensor"),
        P("tensor"),
        P(),
        P(),
        P(),
        P(),
        P(),
        P(),
    )
    groups, shards = mesh.shape["dp"], mesh.shape["tensor"]

    def run(*arrays):
        body = on_device
        if 2 * (arrays[0].shape[0] // groups) == 3 * shards:
            body = functools.partial(fast_on_device, groups=groups, shards=shards)
        return jax.shard_map(
            body, mesh=mesh, in_specs=in_specs, out_specs=out_specs, check_vma=False
        )(*arrays)

    return run
```

```python
import functools
import math

import jax
import jax.numpy as jnp
from jax import lax
from jax.experimental import pallas as pl
from jax.experimental.pallas import tpu as pltpu
from jax.sharding import PartitionSpec as P

HEAD_DIM = 64
PARAMS = 65044736


EPS = 1e-05
SOFTMAX_TEMP = 0.1
DECAY = 0.9
RATE = 100000.0
CLIP_SCALE = 1e-06
HIGH = lax.Precision.HIGHEST
PRODUCT = lax.Precision.HIGH
CAPACITY = 88


def precise_product(left, right):
    return jnp.matmul(left, right, precision=HIGH)


def norm_rows(values, gain, shift):
    center = values - jnp.mean(values, axis=-1, keepdims=True)
    spread = jnp.mean(center * center, axis=-1, keepdims=True)
    return center * lax.rsqrt(spread + EPS) * gain + shift


def attend(normed, lengths, attn, bias_qv):
    seqs, slots, width = normed.shape
    cols = attn.shape[2]
    heads = cols // HEAD_DIM
    queries = (precise_product(normed, attn[0]) + bias_qv[0]).reshape(seqs, slots, heads, HEAD_DIM)
    keys_all = precise_product(normed, attn[1]).reshape(seqs, slots, heads, HEAD_DIM)
    values = (precise_product(normed, attn[2]) + bias_qv[1]).reshape(seqs, slots, heads, HEAD_DIM)
    scores = jnp.einsum("sqhd,skhd->shqk", queries, keys_all, precision=HIGH) / math.sqrt(HEAD_DIM)
    valid = lax.broadcasted_iota(jnp.int32, (seqs, slots), 1) < lengths[:, None]
    scores = jnp.where(valid[:, None, None, :], scores, -1e30)
    probs = jax.nn.softmax(scores, axis=-1)
    mixed = jnp.einsum("shqk,skhd->sqhd", probs, values, precision=HIGH).reshape(seqs, slots, cols)
    return precise_product(mixed, attn[3].T)


def expand(normed, ffn, bias_up):
    hidden = jax.nn.gelu(precise_product(normed, ffn[0]) + bias_up, approximate=False)
    return precise_product(hidden, ffn[1].T)


def contrast(pooled, head_first, head_second, head_bias, partners):
    middle = jax.nn.gelu(precise_product(pooled, head_first) + head_bias, approximate=False)
    output = precise_product(middle, head_second)
    unit_vectors = output * lax.rsqrt(jnp.sum(output * output, axis=-1, keepdims=True) + 1e-06)
    similarity_scores = precise_product(unit_vectors, unit_vectors.T) / SOFTMAX_TEMP
    count = similarity_scores.shape[0]
    index = lax.broadcasted_iota(jnp.int32, (count,), 0)
    similarity_scores = jnp.where(index[:, None] == index[None, :], -1e30, similarity_scores)
    totals = jax.nn.logsumexp(similarity_scores, axis=-1)
    paired_rows = jnp.sum(
        jnp.where(index[None, :] == partners[:, None], similarity_scores, 0.0), axis=-1
    )
    return jnp.sum(totals - paired_rows)


def owner_rows(ids_part, base, vocab_rows):
    local_ids = ids_part - base
    inside = (local_ids >= 0) & (local_ids < vocab_rows)
    return jnp.where(inside, local_ids, vocab_rows)


def advance(weight, moment, grad, factor):
    clipped = factor * grad
    moment_new = DECAY * moment + (1.0 - DECAY) * clipped
    return (weight - RATE * (DECAY * moment_new + (1.0 - DECAY) * clipped), moment_new)


def squares(array):
    return jnp.sum(array * array)


def on_device(
    token_ids,
    lengths,
    partners,
    embedding,
    positions,
    attn_weights,
    ffn_weights,
    bias_qv,
    bias_up,
    norms,
    head_first,
    head_second,
    head_bias,
    mom_embedding,
    mom_positions,
    mom_attn,
    ffn_momentum,
    mom_bias_qv,
    mom_bias_up,
    mom_norms,
    mom_head_first,
    mom_head_second,
    mom_head_bias,
):
    seqs, slots = token_ids.shape
    vocab_rows, cols = embedding.shape
    dp_rank = lax.axis_index("dp")
    tp_rank = lax.axis_index("tensor")
    base = dp_rank * vocab_rows
    all_ids = lax.all_gather(token_ids, "dp", axis=0, tiled=True).reshape(-1)
    padded_table = jnp.concatenate([embedding, jnp.zeros((1, cols), jnp.float32)], axis=0)
    rows_ids = owner_rows(all_ids, base, vocab_rows)
    token_rows = lax.psum_scatter(
        jnp.take(padded_table, rows_ids, axis=0), "dp", scatter_dimension=0, tiled=True
    )
    token_cols = token_rows.reshape(seqs, slots, cols) + positions[2 : slots + 2][None]
    embedded = lax.all_gather(token_cols, "tensor", axis=2, tiled=True)
    h_zero, ln_zero_pull = jax.vjp(norm_rows, embedded, norms[0], norms[1])
    attn_part, attn_pull = jax.vjp(
        lambda normed, weights, biases: attend(normed, lengths, weights, biases),
        h_zero,
        attn_weights,
        bias_qv,
    )
    x_one = h_zero + lax.psum(attn_part, "tensor") + norms[6]
    h_one, ln_one_pull = jax.vjp(norm_rows, x_one, norms[2], norms[3])
    ffn_part, ffn_pull = jax.vjp(expand, h_one, ffn_weights, bias_up)
    x_two = h_one + lax.psum(ffn_part, "tensor") + norms[7]
    h_two, ln_two_pull = jax.vjp(norm_rows, x_two, norms[4], norms[5])
    valid = (lax.broadcasted_iota(jnp.int32, (seqs, slots), 1) < lengths[:, None]).astype(
        jnp.float32
    )
    len_float = lengths.astype(jnp.float32)
    pooled = jnp.sum(h_two * valid[:, :, None], axis=1) / len_float[:, None]
    all_pooled = lax.all_gather(pooled, "dp", axis=0, tiled=True)
    loss, head_pull = jax.vjp(
        lambda rows, first_w, second_w, bias_w: contrast(rows, first_w, second_w, bias_w, partners),
        all_pooled,
        head_first,
        head_second,
        head_bias,
    )
    back_pooled_all, grad_head_first, grad_head_second, grad_head_bias = head_pull(
        jnp.ones_like(loss)
    )
    back_pooled = lax.dynamic_slice_in_dim(back_pooled_all, dp_rank * seqs, seqs)
    back_h_two = valid[:, :, None] * (back_pooled / len_float[:, None])[:, None, :]
    back_x_two, grad_gain_two, grad_shift_two = ln_two_pull(back_h_two)
    back_h_one_part, grad_ffn, grad_bias_up = ffn_pull(back_x_two)
    back_h_one = back_x_two + lax.psum(back_h_one_part, "tensor")
    back_x_one, grad_gain_one, grad_shift_one = ln_one_pull(back_h_one)
    back_h_zero_part, grad_attn, grad_bias_qv = attn_pull(back_x_one)
    back_h_zero = back_x_one + lax.psum(back_h_zero_part, "tensor")
    back_embedded, grad_gain_zero, grad_shift_zero = ln_zero_pull(back_h_zero)
    back_cols = lax.dynamic_slice_in_dim(back_embedded, tp_rank * cols, cols, 2)
    grad_positions = jnp.pad(
        jnp.sum(back_cols, axis=0), ((2, positions.shape[0] - slots - 2), (0, 0))
    )
    grad_norms = jnp.stack(
        [
            grad_gain_zero,
            grad_shift_zero,
            grad_gain_one,
            grad_shift_one,
            grad_gain_two,
            grad_shift_two,
            jnp.sum(back_x_one, axis=(0, 1)),
            jnp.sum(back_x_two, axis=(0, 1)),
        ]
    )
    back_flat = back_cols.reshape(seqs * slots, cols)
    target = owner_rows(all_ids, base, vocab_rows)
    grad_embedding = jax.ops.segment_sum(
        lax.all_gather(back_flat, "dp", axis=0, tiled=True), target, num_segments=vocab_rows + 1
    )[:vocab_rows]
    first_dp = (dp_rank == 0).astype(jnp.float32)
    first_all = first_dp * (tp_rank == 0).astype(jnp.float32)
    grad_attn, grad_ffn, grad_positions, grad_bias_qv, grad_bias_up, grad_norms = lax.psum(
        (grad_attn, grad_ffn, grad_positions, grad_bias_qv, grad_bias_up, grad_norms), "dp"
    )
    big_squares = first_dp * (squares(grad_attn) + squares(grad_ffn))
    local_squares = (
        big_squares
        + squares(grad_embedding)
        + first_dp * (squares(grad_positions) + squares(grad_bias_qv) + squares(grad_bias_up))
        + first_all
        * (
            squares(grad_norms)
            + squares(grad_head_first)
            + squares(grad_head_second)
            + squares(grad_head_bias)
        )
    )
    total_squares = lax.psum(local_squares, ("dp", "tensor"))
    grad_norm = jnp.sqrt(total_squares)
    factor = jnp.minimum(1.0, CLIP_SCALE * math.sqrt(PARAMS) / (grad_norm + 1e-06))
    new_attn, next_attn = advance(attn_weights, mom_attn, grad_attn, factor)
    new_ffn, next_ffn = advance(ffn_weights, ffn_momentum, grad_ffn, factor)
    new_embedding, next_embedding = advance(embedding, mom_embedding, grad_embedding, factor)
    new_positions, next_positions = advance(positions, mom_positions, grad_positions, factor)
    new_bias_qv, next_bias_qv = advance(bias_qv, mom_bias_qv, grad_bias_qv, factor)
    new_bias_up, next_bias_up = advance(bias_up, mom_bias_up, grad_bias_up, factor)
    new_norms, next_norms = advance(norms, mom_norms, grad_norms, factor)
    new_head_first, next_head_first = advance(head_first, mom_head_first, grad_head_first, factor)
    new_head_second, next_head_second = advance(
        head_second, mom_head_second, grad_head_second, factor
    )
    new_head_bias, next_head_bias = advance(head_bias, mom_head_bias, grad_head_bias, factor)
    return (
        new_embedding,
        new_positions,
        new_attn,
        new_ffn,
        new_bias_qv,
        new_bias_up,
        new_norms,
        new_head_first,
        new_head_second,
        new_head_bias,
        next_embedding,
        next_positions,
        next_attn,
        next_ffn,
        next_bias_qv,
        next_bias_up,
        next_norms,
        next_head_first,
        next_head_second,
        next_head_bias,
        loss,
        grad_norm,
    )


MESH = pl.DeviceIdType.MESH
VMEM = pl.BlockSpec(memory_space=pltpu.VMEM)


def cube_partners(groups, shards):
    dp, tp = lax.axis_index("dp"), lax.axis_index("tensor")
    partners = []
    for size, at in ((shards, 1), (groups, 0)):
        bit = 1
        while bit < size:
            here = (dp, tp)[at]
            there = here + bit * (1 - 2 * ((here // bit) % 2))
            partners.append((dp, there) if at else (there, tp))
            bit *= 2
    return partners


def greet(partners):
    barrier = pltpu.get_barrier_semaphore()
    for partner in partners:
        pl.semaphore_signal(barrier, inc=1, device_id=partner, device_id_type=MESH)
    pl.semaphore_wait(barrier, len(partners))


def cube_sum_kernel(groups, shards, x_ref, o_ref, sent, landed, send_sem, recv_sem):
    partners = cube_partners(groups, shards)
    greet(partners)
    sent[0] = x_ref[...]
    for stage, partner in enumerate(partners):
        copy = pltpu.make_async_remote_copy(
            src_ref=sent.at[stage],
            dst_ref=landed.at[stage],
            send_sem=send_sem.at[stage],
            recv_sem=recv_sem.at[stage],
            device_id=partner,
            device_id_type=MESH,
        )
        copy.start()
        copy.wait()
        sent[stage + 1] = sent[stage] + landed[stage]
    o_ref[...] = sent[len(partners)]


def cube_stages(groups, shards):
    return (groups * shards).bit_length() - 1


def cube_sum(block, groups, shards, collective_id):
    stages = cube_stages(groups, shards)
    return pl.pallas_call(
        functools.partial(cube_sum_kernel, groups, shards),
        out_shape=jax.ShapeDtypeStruct(block.shape, block.dtype),
        in_specs=[VMEM],
        out_specs=VMEM,
        scratch_shapes=[
            pltpu.VMEM((stages + 1, *block.shape), block.dtype),
            pltpu.VMEM((stages, *block.shape), block.dtype),
            pltpu.SemaphoreType.DMA((stages,)),
            pltpu.SemaphoreType.DMA((stages,)),
        ],
        compiler_params=pltpu.CompilerParams(collective_id=collective_id, has_side_effects=True),
    )(block)


def cube_gather_kernel(groups, shards, x_ref, o_ref, held, send_sem, recv_sem):
    partners = cube_partners(groups, shards)
    greet(partners)
    me = lax.axis_index("dp") * shards + lax.axis_index("tensor")
    held[pl.ds(me, 1)] = x_ref[...][None]
    for stage, partner in enumerate(partners):
        size = 1 << stage
        mine = pl.ds((me // size) * size, size)
        copy = pltpu.make_async_remote_copy(
            src_ref=held.at[mine],
            dst_ref=held.at[mine],
            send_sem=send_sem.at[stage],
            recv_sem=recv_sem.at[stage],
            device_id=partner,
            device_id_type=MESH,
        )
        copy.start()
        copy.wait()
    o_ref[...] = held[...]


def cube_gather(block, groups, shards, collective_id):
    stages = cube_stages(groups, shards)
    shape = (groups * shards, *block.shape)
    return pl.pallas_call(
        functools.partial(cube_gather_kernel, groups, shards),
        out_shape=jax.ShapeDtypeStruct(shape, block.dtype),
        in_specs=[VMEM],
        out_specs=VMEM,
        scratch_shapes=[
            pltpu.VMEM(shape, block.dtype),
            pltpu.SemaphoreType.DMA((stages,)),
            pltpu.SemaphoreType.DMA((stages,)),
        ],
        compiler_params=pltpu.CompilerParams(collective_id=collective_id, has_side_effects=True),
    )(block)


def ring_kernel(groups, parts, arrays, *refs):
    inputs, outputs, slots = refs[:arrays], refs[arrays : 2 * arrays], refs[2 * arrays : 3 * arrays]
    send_sem, recv_sem = refs[3 * arrays :]
    depth = groups // 2
    dp, tp = lax.axis_index("dp"), lax.axis_index("tensor")
    side, level = dp % 2, dp // 2
    place = level * (1 - side) + (groups - 1 - level) * side

    def device_at(spot):
        spot = (spot + groups) % groups
        far = spot // depth
        return (2 * (spot * (1 - far) + (groups - 1 - spot) * far) + far, tp)

    greet([device_at(place + 1), device_at(place - 1)])
    streams = []
    for array in range(arrays):
        rows = inputs[array].shape[1] // (2 * parts)
        for part in range(2 * parts):
            streams.append((array, 1 - 2 * (part % 2), pl.ds(part * rows, rows)))

    def chunk(step, way):
        return (place + groups * 2 - way * step) % groups

    copies = []

    def send(index, step, source, target):
        copy = pltpu.make_async_remote_copy(
            src_ref=source,
            dst_ref=target,
            send_sem=send_sem.at[index, step],
            recv_sem=recv_sem.at[index, step],
            device_id=device_at(place + streams[index][1]),
            device_id_type=MESH,
        )
        copy.start()
        copies.append(copy)
        return copy

    flying = [None] * len(streams)
    for step in range(groups - 1):
        for index, (array, way, rows) in enumerate(streams):
            if step == 0:
                source = inputs[array].at[chunk(0, way), rows]
            else:
                flying[index].wait_recv()
                source = slots[array].at[step - 1, rows]
                source[...] = source[...] + inputs[array][chunk(step, way), rows]
            flying[index] = send(index, step, source, slots[array].at[step, rows])
    for step in range(groups - 1):
        for index, (array, way, rows) in enumerate(streams):
            flying[index].wait_recv()
            now = chunk(groups - 1 + step, way)
            if step == 0:
                outputs[array][now, rows] = slots[array][groups - 2, rows] + inputs[array][now, rows]
            place_out = outputs[array].at[now, rows]
            flying[index] = send(index, groups - 1 + step, place_out, place_out)
    for copy in flying:
        copy.wait_recv()
    for copy in copies:
        copy.wait_send()


def ring_sum(arrays, groups, parts, collective_id):
    blocks = [array.reshape(groups, array.shape[0] // groups, array.shape[1]) for array in arrays]
    streams = 2 * parts * len(blocks)
    steps = 2 * (groups - 1)
    moved = sum(2 * block.size * 4 for block in blocks)
    sums = pl.pallas_call(
        functools.partial(ring_kernel, groups, parts, len(blocks)),
        out_shape=[jax.ShapeDtypeStruct(block.shape, block.dtype) for block in blocks],
        in_specs=[VMEM] * len(blocks),
        out_specs=[VMEM] * len(blocks),
        scratch_shapes=[
            *[pltpu.VMEM((groups - 1, *block.shape[1:]), block.dtype) for block in blocks],
            pltpu.SemaphoreType.DMA((streams, steps)),
            pltpu.SemaphoreType.DMA((streams, steps)),
        ],
        compiler_params=pltpu.CompilerParams(
            collective_id=collective_id, has_side_effects=True, vmem_limit_bytes=48 << 20
        ),
        cost_estimate=pl.CostEstimate(flops=moved, bytes_accessed=60 * moved, transcendentals=0),
    )(*blocks)
    return [total.reshape(array.shape) for total, array in zip(sums, arrays)]


def spread_kernel(groups, w_ref, o_ref, local_sem, pair_send, pair_recv, ring_send, ring_recv, core_send, core_recv):
    depth = groups // 2
    dp, tp = lax.axis_index("dp"), lax.axis_index("tensor")
    far = tp + 2 - 4 * (tp // 2)
    core = (dp, tp + 1 - 2 * (tp % 2))
    side, level = dp % 2, dp // 2
    place = level * (1 - side) + (groups - 1 - level) * side

    def index_at(spot):
        spot = (spot + groups) % groups
        back = spot // depth
        return 2 * (spot * (1 - back) + (groups - 1 - spot) * back) + back

    def send(source, target, send_sem, recv_sem, device):
        copy = pltpu.make_async_remote_copy(
            src_ref=source,
            dst_ref=target,
            send_sem=send_sem,
            recv_sem=recv_sem,
            device_id=device,
            device_id_type=MESH,
        )
        copy.start()
        return copy

    greet([(index_at(place + 1), tp), (index_at(place - 1), tp), core, (dp, far)])
    cross = send(w_ref.at[dp], o_ref.at[tp, dp], pair_send.at[0], pair_recv.at[0], (dp, far))
    near = send(w_ref, o_ref.at[tp], pair_send.at[1], pair_recv.at[1], core)
    local = pltpu.make_async_copy(w_ref, o_ref.at[tp], local_sem)
    local.start()
    cross.wait_recv()
    lanes = ring_send.shape[0]
    size = w_ref.shape[1] // lanes
    flying = [None] * lanes
    started = [cross]
    handed = [near]
    for step in range(groups):
        for lane in range(lanes):
            way = 1 - 2 * (lane % 2)
            block = o_ref.at[far, index_at(place + groups - way * step), pl.ds(lane * size, size)]
            if step > 0:
                flying[lane].wait_recv()
            if step < groups - 1:
                flying[lane] = send(
                    block, block, ring_send.at[lane, step], ring_recv.at[lane, step], (index_at(place + way), tp)
                )
                started.append(flying[lane])
            handed.append(send(block, block, core_send.at[lane, step], core_recv.at[lane, step], core))
    for copy in handed:
        copy.wait_recv()
        copy.wait_send()
    for copy in started:
        copy.wait_send()
    local.wait()


def spread(weight, groups, collective_id):
    rows = weight.shape[0] // groups
    lanes = 4
    moved = 4 * weight.size
    gathered = pl.pallas_call(
        functools.partial(spread_kernel, groups),
        out_shape=jax.ShapeDtypeStruct((4, groups, rows, weight.shape[1]), weight.dtype),
        in_specs=[pl.BlockSpec(memory_space=pl.ANY)],
        out_specs=VMEM,
        scratch_shapes=[
            pltpu.SemaphoreType.DMA,
            pltpu.SemaphoreType.DMA((2,)),
            pltpu.SemaphoreType.DMA((2,)),
            pltpu.SemaphoreType.DMA((lanes, groups - 1)),
            pltpu.SemaphoreType.DMA((lanes, groups - 1)),
            pltpu.SemaphoreType.DMA((lanes, groups)),
            pltpu.SemaphoreType.DMA((lanes, groups)),
        ],
        compiler_params=pltpu.CompilerParams(
            collective_id=collective_id, has_side_effects=True, vmem_limit_bytes=32 << 20
        ),
        cost_estimate=pl.CostEstimate(flops=moved, bytes_accessed=30 * moved, transcendentals=0),
    )(weight.reshape(groups, rows, weight.shape[1]))
    return gathered.reshape(4, *weight.shape)


def halves(array):
    high = array.astype(jnp.bfloat16)
    return high, (array - high.astype(jnp.float32)).astype(jnp.bfloat16)


def dot_rows(left, right):
    return lax.dot_general(left, right, (((1,), (1,)), ((), ())), preferred_element_type=jnp.float32)


def dot_plain(left, right):
    return lax.dot_general(left, right, (((1,), (0,)), ((), ())), preferred_element_type=jnp.float32)


def one_head(array, head):
    lane = lax.broadcasted_iota(jnp.int32, array.shape, 1)
    return jnp.where(lane // HEAD_DIM == head, array, 0.0)


def score_tile(twice_k, low_k, high_q, low_q, bias):
    wide = dot_rows(twice_k, jnp.concatenate([high_q, low_q], axis=1))
    return wide + dot_rows(low_k, high_q) + bias


def attend_kernel(slots, tile, q_ref, k_ref, v_ref, bias_ref, o_ref, lse_ref):
    scale = 1.0 / math.sqrt(HEAD_DIM)
    high_k, low_k = halves(k_ref[0])
    twice_k = jnp.concatenate([high_k, high_k], axis=1)
    high_v, low_v = halves(v_ref[0].T)
    for start in range(0, q_ref.shape[1], tile):
        rows = pl.ds(start, tile)
        first = 0 if start < slots else slots
        keys = slice(first, first + slots)
        found = []
        for head in range(2):
            high_q, low_q = halves(one_head(q_ref[0, rows] * scale, head))
            scores = score_tile(twice_k[keys], low_k[keys], high_q, low_q, bias_ref[pl.ds(first, slots)])
            peak = jnp.max(scores, axis=0, keepdims=True)
            probs = jnp.exp(scores - peak)
            total = jnp.sum(probs, axis=0, keepdims=True)
            lse_ref[0, pl.ds(head, 1), rows] = peak + jnp.log(total)
            high_p, low_p = halves(probs)
            lanes = slice(head * HEAD_DIM, (head + 1) * HEAD_DIM)
            both = jnp.concatenate([high_v[lanes, keys], low_v[lanes, keys]], axis=0)
            wide = dot_plain(both, high_p)
            mixed = wide[:HEAD_DIM] + wide[HEAD_DIM:] + dot_plain(high_v[lanes, keys], low_p)
            found.append(mixed / total)
        o_ref[0, rows] = jnp.concatenate(found, axis=0).T


def attend_back_kernel(slots, tile, q_ref, k_ref, v_ref, bias_ref, o_ref, lse_ref, d_ref, dq_ref, dk_ref, dv_ref):
    scale = 1.0 / math.sqrt(HEAD_DIM)
    high_k, low_k = halves(k_ref[0])
    twice_k = jnp.concatenate([high_k, high_k], axis=1)
    high_v, low_v = halves(v_ref[0])
    twice_v = jnp.concatenate([high_v, high_v], axis=1)
    high_kt, low_kt = halves(k_ref[0].T)
    ones = jnp.ones((8, 2 * HEAD_DIM), jnp.bfloat16)
    lanes = 2 * HEAD_DIM
    for first in (0, slots):
        keys = slice(first, first + slots)
        key_rows = pl.ds(first, slots)
        for start in range(first, min(first + slots, q_ref.shape[1]), tile):
            rows = pl.ds(start, tile)
            back_qt = []
            for head in range(2):
                high_q, low_q = halves(one_head(q_ref[0, rows] * scale, head))
                back = one_head(d_ref[0, rows], head)
                high_d, low_d = halves(back)
                scores = score_tile(twice_k[keys], low_k[keys], high_q, low_q, bias_ref[key_rows])
                probs = jnp.exp(scores - lse_ref[0, pl.ds(head, 1), rows])
                high_x, low_x = halves(back * o_ref[0, rows])
                inner = (dot_rows(ones, high_x) + dot_rows(ones, low_x))[:1]
                back_s = probs * (score_tile(twice_v[keys], low_v[keys], high_d, low_d, 0.0) - inner)
                high_p, low_p = halves(probs)
                high_s, low_s = halves(back_s)
                wide = dot_plain(high_p, jnp.concatenate([high_d, low_d], axis=1))
                back_v = wide[:, :lanes] + wide[:, lanes:] + dot_plain(low_p, high_d)
                wide = dot_plain(high_s, jnp.concatenate([high_q, low_q], axis=1))
                back_k = wide[:, :lanes] + wide[:, lanes:] + dot_plain(low_s, high_q)
                if start == first and head == 0:
                    dv_ref[0, key_rows] = back_v
                    dk_ref[0, key_rows] = back_k
                else:
                    dv_ref[0, key_rows] += back_v
                    dk_ref[0, key_rows] += back_k
                mine = slice(head * HEAD_DIM, (head + 1) * HEAD_DIM)
                both = jnp.concatenate([high_kt[mine, keys], low_kt[mine, keys]], axis=0)
                wide = dot_plain(both, high_s)
                back_qt.append(wide[:HEAD_DIM] + wide[HEAD_DIM:] + dot_plain(high_kt[mine, keys], low_s))
            dq_ref[0, rows] = jnp.concatenate(back_qt, axis=0).T * scale


def attend_call(kernel, slots, inputs, outputs):
    lanes = 2 * HEAD_DIM
    queries = inputs[0]
    per_shard = queries.shape[2] // lanes
    pairs = queries.shape[0] * per_shard

    def spec(shape):
        if shape[1] == 1:
            return pl.BlockSpec(shape, lambda i: (0, 0))
        if shape[1] == 2:
            return pl.BlockSpec((1, *shape[1:]), lambda i: (i, 0, 0))
        return pl.BlockSpec((1, shape[1], lanes), lambda i: (i // per_shard, 0, i % per_shard))

    work = 7 * 2 * pairs * 2 * queries.shape[1] * slots * HEAD_DIM * 3
    return pl.pallas_call(
        functools.partial(kernel, slots, slots // 2),
        grid=(pairs,),
        in_specs=[spec(x.shape) for x in inputs],
        out_specs=[spec(shape) for shape in outputs],
        out_shape=[jax.ShapeDtypeStruct(shape, jnp.float32) for shape in outputs],
        compiler_params=pltpu.CompilerParams(vmem_limit_bytes=48 << 20),
        cost_estimate=pl.CostEstimate(flops=4 * work, bytes_accessed=20 << 20, transcendentals=0),
    )(*inputs)


def normalise(values):
    center = values - jnp.mean(values, axis=-1, keepdims=True)
    scale = lax.rsqrt(jnp.mean(center * center, axis=-1, keepdims=True) + EPS)
    return center * scale, scale


def normalise_back(back, gain, unit, scale):
    inner = back * gain
    grad = scale * (
        inner
        - jnp.mean(inner, axis=-1, keepdims=True)
        - unit * jnp.mean(inner * unit, axis=-1, keepdims=True)
    )
    return grad, jnp.sum(back * unit, axis=0), jnp.sum(back, axis=0)


def gelu_both(values):
    cdf = 0.5 * (1.0 + lax.erf(values * math.sqrt(0.5)))
    pdf = jnp.exp(-0.5 * values * values) * (1.0 / math.sqrt(2.0 * math.pi))
    return values * cdf, cdf + values * pdf


def product(subscripts, left, right):
    return jnp.einsum(subscripts, left, right, precision=PRODUCT)


def request_lists(ids, vocab_rows, owners):
    count = ids.shape[0]
    index = lax.broadcasted_iota(jnp.int32, (count,), 0)
    earlier = index[None, :] < index[:, None]
    same = (ids[None, :] == ids[:, None]) & earlier
    first = jnp.logical_not(jnp.any(same, axis=1))
    owner = ids // vocab_rows
    ahead = (owner[None, :] == owner[:, None]) & earlier & first[None, :]
    rank = jnp.sum(ahead.astype(jnp.int32), axis=1)
    return owner, jnp.where(first, rank, -1)


def round_list(ids, owner, rank, round_index, owners):
    place = rank - round_index * CAPACITY
    inside = (rank >= 0) & (place >= 0) & (place < CAPACITY)
    place = jnp.where(inside, owner * CAPACITY + place, -1)
    wanted = lax.broadcasted_iota(jnp.int32, (owners * CAPACITY, 1), 0)
    return jnp.sum(jnp.where(place[None, :] == wanted, ids[None, :] + 1, 0), axis=1) - 1


def trade(block):
    return lax.all_to_all(block, ("dp", "tensor"), 0, 0, tiled=True)


def fast_on_device(
    token_ids, lengths, partners, embedding, positions, attn_weights, ffn_weights, bias_qv, bias_up, norms,
    head_first, head_second, head_bias, mom_embedding, mom_positions, mom_attn, ffn_momentum, mom_bias_qv,
    mom_bias_up, mom_norms, mom_head_first, mom_head_second, mom_head_bias, *, groups, shards
):
    seqs, slots = token_ids.shape
    half = slots // 2
    vocab_rows, cols = embedding.shape
    width = cols * shards
    devices = groups * shards
    hidden = bias_up.shape[0]
    heads = width // HEAD_DIM
    dp_rank = lax.axis_index("dp")
    tp_rank = lax.axis_index("tensor")
    pair = tp_rank // 2
    side = tp_rank % 2
    base = dp_rank * vocab_rows

    whole_seq = 3 * pair + 2 * side
    split_seq = 3 * pair + 1
    whole_ids = lax.dynamic_index_in_dim(token_ids, whole_seq, 0, keepdims=False)
    split_ids = lax.dynamic_index_in_dim(token_ids, split_seq, 0, keepdims=False)
    ids = jnp.concatenate([whole_ids, lax.dynamic_slice_in_dim(split_ids, side * half, half)])
    count = ids.shape[0]
    whole_length = lax.dynamic_index_in_dim(lengths, whole_seq, 0, keepdims=False)
    split_length = lax.dynamic_index_in_dim(lengths, split_seq, 0, keepdims=False)

    all_attn = lax.all_gather(attn_weights, "tensor")
    all_ffn_down = lax.all_gather(ffn_weights[1], "tensor")
    small = jnp.concatenate([positions[2 : slots + 2], bias_qv, bias_up.reshape(-1, cols)], axis=0)
    swap = [(i, i ^ 1) for i in range(shards)]
    swap_pair = [(i, i ^ 2) for i in range(shards)]
    far_small = lax.ppermute(small, "tensor", swap_pair)
    rows_small = jnp.stack([small, lax.ppermute(small, "tensor", swap), far_small, lax.ppermute(far_small, "tensor", swap)])
    all_small = jnp.concatenate(
        [
            lax.dynamic_index_in_dim(rows_small, 2 * ((j // 2 + pair) % 2) + (j + side) % 2, 0)
            for j in range(shards)
        ]
    )
    all_positions = all_small[:, :slots].transpose(1, 0, 2).reshape(slots, width)
    all_bias_up = all_small[:, slots + 2 :].reshape(-1)

    owner, rank = request_lists(ids, vocab_rows, groups)
    rounds_here = jnp.max(rank) // CAPACITY + 1

    def serve(round_index):
        wanted = round_list(ids, owner, rank, round_index, groups)
        lists = jnp.broadcast_to(wanted.reshape(groups, 1, CAPACITY), (groups, shards, CAPACITY))
        lists = lists.reshape(devices, CAPACITY)
        tail = jnp.broadcast_to(rounds_here, (devices, 1)).astype(jnp.int32)
        lists = jnp.concatenate([lists, tail, jnp.zeros((devices, 127 - CAPACITY), jnp.int32)], axis=1)
        asked = trade(lists)
        rows = asked[:, :CAPACITY].reshape(-1) - base
        rounds = jnp.max(asked[:, CAPACITY])
        return wanted, rows, rounds

    def ask(rows):
        return trade(jnp.take(embedding, rows, axis=0, mode="clip"))

    def expand(wanted, landed):
        landed = landed.reshape(groups, shards, CAPACITY, cols)
        landed = landed.transpose(0, 2, 1, 3).reshape(groups * CAPACITY, width)
        chosen = (ids[:, None] == wanted[None, :]).astype(jnp.float32)
        return jnp.matmul(chosen, landed, precision=HIGH)

    wanted_first, rows_first, rounds = serve(0)
    landed, up_weights = lax.optimization_barrier((ask(rows_first), ffn_weights[0]))
    all_ffn_up = spread(up_weights, groups, 6)
    tokens = expand(wanted_first, landed)

    def more(state):
        return state[0] < rounds

    def fetch_more(state):
        round_index, total = state
        wanted, rows, _ = serve(round_index)
        return round_index + 1, total + expand(wanted, ask(rows))

    _, tokens = lax.while_loop(more, fetch_more, (jnp.int32(1), tokens))
    own_positions = jnp.concatenate(
        [all_positions, lax.dynamic_slice_in_dim(all_positions, side * half, half)], axis=0
    )
    embedded = tokens + own_positions
    unit_zero, scale_zero = normalise(embedded)
    h_zero = unit_zero * norms[0] + norms[1]

    h_other = lax.ppermute(h_zero[slots:], "tensor", swap)
    h_keys = jnp.concatenate([h_zero, h_other], axis=0)
    bias_q, bias_v = all_small[:, slots], all_small[:, slots + 1]
    queries = product("td,jdc->jtc", h_zero, all_attn[:, 0]) + bias_q[:, None, :]
    keys_all = product("td,jdc->jtc", h_keys, all_attn[:, 1])
    values = product("td,jdc->jtc", h_keys, all_attn[:, 2]) + bias_v[:, None, :]
    key_index = lax.broadcasted_iota(jnp.int32, (slots,), 0)
    own_first = jnp.where(
        key_index < half, side * half + key_index, (1 - side) * half + key_index - half
    )
    counted = jnp.concatenate([key_index < whole_length, own_first < split_length])
    key_bias = jnp.where(counted, 0.0, -1e30).astype(jnp.float32)[:, None]
    mixed, lse = attend_call(
        attend_kernel,
        slots,
        (queries, keys_all, values, key_bias),
        (queries.shape, (heads // 2, 2, count)),
    )
    x_one = h_zero + product("jtc,jdc->td", mixed, all_attn[:, 3]) + norms[6]
    unit_one, scale_one = normalise(x_one)
    h_one = unit_one * norms[2] + norms[3]

    up = product("td,jdc->tjc", h_one, all_ffn_up) + all_bias_up.reshape(shards, hidden)
    act, act_slope = lax.optimization_barrier(gelu_both(up))
    x_two = h_one + product("tjc,jdc->td", act, all_ffn_down) + norms[7]
    unit_two, scale_two = normalise(x_two)
    h_two = unit_two * norms[4] + norms[5]

    slot = lax.broadcasted_iota(jnp.int32, (count,), 0)
    in_whole = slot < slots
    place = jnp.where(in_whole, slot, slot - slots + side * half)
    keep = place < jnp.where(in_whole, whole_length, split_length)
    weight_whole = jnp.where(keep & in_whole, 1.0 / whole_length.astype(jnp.float32), 0.0)
    weight_split = jnp.where(keep & ~in_whole, 1.0 / split_length.astype(jnp.float32), 0.0)
    sums = jnp.stack(
        [jnp.sum(h_two * weight_whole[:, None], axis=0), jnp.sum(h_two * weight_split[:, None], axis=0)]
    )
    all_sums = cube_gather(sums.reshape(-1, 128), groups, shards, 5).reshape(groups * shards // 2, 2, 2, width)
    all_pooled = jnp.stack(
        [all_sums[:, 0, 0], all_sums[:, 0, 1] + all_sums[:, 1, 1], all_sums[:, 1, 0]], axis=1
    ).reshape(groups * seqs, width)
    loss, head_pull = jax.vjp(
        lambda rows, first_w, second_w, bias_w: contrast(rows, first_w, second_w, bias_w, partners),
        all_pooled,
        head_first,
        head_second,
        head_bias,
    )
    back_pooled, grad_head_first, grad_head_second, grad_head_bias = head_pull(jnp.ones_like(loss))
    first_row = dp_rank * seqs
    back_whole = lax.dynamic_index_in_dim(back_pooled, first_row + whole_seq, 0, keepdims=False)
    back_split = lax.dynamic_index_in_dim(back_pooled, first_row + split_seq, 0, keepdims=False)
    back_h_two = weight_whole[:, None] * back_whole[None, :] + weight_split[:, None] * back_split[None, :]

    back_x_two, grad_gain_two, grad_shift_two = normalise_back(back_h_two, norms[4], unit_two, scale_two)
    grad_down = product("td,tjc->jdc", back_x_two, act)
    sum_down = lax.psum_scatter(grad_down, "tensor", scatter_dimension=0, tiled=False)
    back_up = product("td,jdc->jtc", back_x_two, all_ffn_down) * act_slope.transpose(1, 0, 2)
    grad_up = product("td,jtc->jdc", h_one, back_up)
    back_up, grad_up = lax.optimization_barrier((back_up, grad_up))
    sum_up = lax.psum_scatter(grad_up, "tensor", scatter_dimension=0, tiled=False)
    grad_bias_up = jnp.sum(back_up, axis=1)
    back_h_one = back_x_two + product("jtc,jdc->td", back_up, all_ffn_up)
    back_x_one, grad_gain_one, grad_shift_one = normalise_back(back_h_one, norms[2], unit_one, scale_one)

    back_mixed = product("td,jdc->jtc", back_x_one, all_attn[:, 3])
    grad_out = product("td,jtc->jdc", back_x_one, mixed)
    back_q, back_k, back_v = attend_call(
        attend_back_kernel,
        slots,
        (queries, keys_all, values, key_bias, mixed, lse, back_mixed),
        (queries.shape, keys_all.shape, values.shape),
    )
    back_keys = product("jtc,jdc->td", back_k, all_attn[:, 1]) + product("jtc,jdc->td", back_v, all_attn[:, 2])
    back_other = lax.ppermute(back_keys[count:], "tensor", swap)
    grad_q = product("td,jtc->jdc", h_zero, back_q)
    grad_k = product("td,jtc->jdc", h_keys, back_k)
    grad_v = product("td,jtc->jdc", h_keys, back_v)
    back_h_zero = back_x_one + product("jtc,jdc->td", back_q, all_attn[:, 0]) + back_keys[:count]
    back_h_zero = back_h_zero + jnp.pad(back_other, ((slots, 0), (0, 0)))
    back_embedded, grad_gain_zero, grad_shift_zero = normalise_back(back_h_zero, norms[0], unit_zero, scale_zero)

    def send_back(wanted):
        chosen = (wanted[:, None] == ids[None, :]).astype(jnp.float32)
        summed = jnp.matmul(chosen, back_embedded, precision=HIGH)
        parts = summed.reshape(groups, CAPACITY, shards, cols).transpose(0, 2, 1, 3)
        return trade(parts.reshape(devices * CAPACITY, cols))

    def add_rows(landed, rows, total):
        target = jnp.where(rows >= 0, rows, vocab_rows)
        return total.at[target].add(landed, mode="drop")

    landed_first = send_back(wanted_first)

    grad_small = jnp.concatenate(
        [
            jnp.stack(
                [
                    grad_gain_zero,
                    grad_shift_zero,
                    grad_gain_one,
                    grad_shift_one,
                    grad_gain_two,
                    grad_shift_two,
                    jnp.sum(back_x_one, axis=0),
                    jnp.sum(back_x_two, axis=0),
                    jnp.sum(back_q, axis=1).reshape(-1),
                    jnp.sum(back_v, axis=1).reshape(-1),
                ]
            ),
            grad_bias_up.reshape(-1, width),
        ],
        axis=0,
    )
    half_rows = jnp.where(side == 0, 1.0, 0.0) * back_embedded[slots:]
    other_rows = back_embedded[slots:] - half_rows
    grad_pos_full = back_embedded[:slots] + jnp.concatenate([half_rows, other_rows], axis=0)
    grad_pos_parts = grad_pos_full.reshape(slots, shards, cols)
    grad_pos_parts = grad_pos_parts.transpose(1, 0, 2)
    small_size = grad_small.size
    small_rows = jnp.pad(grad_small.reshape(-1), (0, 256 * cols - small_size)).reshape(1, 256, cols)
    small_rows = jnp.broadcast_to(small_rows, (shards, 256, cols))
    parts_attn = jnp.concatenate([grad_q, grad_k, grad_v, grad_out, grad_pos_parts, small_rows], axis=1)
    sum_attn = lax.psum_scatter(parts_attn, "tensor", scatter_dimension=0, tiled=False)
    sum_down, sum_up = ring_sum([sum_down, sum_up], groups, 2, 1)
    landed_first, sum_up = lax.optimization_barrier((landed_first, sum_up))
    zero_table = jnp.zeros((vocab_rows, cols), jnp.float32)
    grad_embedding = add_rows(landed_first, rows_first, zero_table)

    def give_more(state):
        round_index, total = state
        wanted, rows, _ = serve(round_index)
        return round_index + 1, add_rows(send_back(wanted), rows, total)

    _, grad_embedding = lax.while_loop(more, give_more, (jnp.int32(1), grad_embedding))

    sum_attn, grad_embedding = lax.optimization_barrier((sum_attn, grad_embedding))
    (sum_attn,) = ring_sum([sum_attn], groups, 2, 2)
    sum_small = sum_attn[-256:].reshape(-1)[:small_size].reshape(grad_small.shape)
    grad_norms = sum_small[:8]
    grad_bias_qv = lax.dynamic_slice_in_dim(sum_small[8:10], tp_rank * cols, cols, 1)
    grad_bias_up = lax.dynamic_slice_in_dim(sum_small[10:].reshape(-1), tp_rank * hidden, hidden)
    grad_attn = sum_attn[: 4 * width].reshape(4, width, cols)
    grad_ffn_up, grad_ffn_down = sum_up, sum_down
    grad_pos = sum_attn[4 * width : -256]

    first_dp = (dp_rank == 0).astype(jnp.float32)
    first_all = first_dp * (tp_rank == 0).astype(jnp.float32)
    local_squares = (
        squares(grad_embedding)
        + first_dp
        * (
            squares(sum_attn[:-256])
            + squares(grad_ffn_up)
            + squares(grad_ffn_down)
            + squares(grad_bias_qv)
            + squares(grad_bias_up)
        )
        + first_all
        * (
            squares(grad_norms)
            + squares(grad_head_first)
            + squares(grad_head_second)
            + squares(grad_head_bias)
        )
    )
    total_squares = cube_sum(jnp.broadcast_to(local_squares, (8, 128)), groups, shards, 4)[0, 0]
    grad_norm = jnp.sqrt(total_squares)
    factor = jnp.minimum(1.0, CLIP_SCALE * math.sqrt(PARAMS) / (grad_norm + 1e-06))
    grad_positions = jnp.pad(grad_pos, ((2, positions.shape[0] - slots - 2), (0, 0)))
    grad_ffn = jnp.stack([grad_ffn_up, grad_ffn_down])
    new_embedding, next_embedding = advance(embedding, mom_embedding, grad_embedding, factor)
    new_positions, next_positions = advance(positions, mom_positions, grad_positions, factor)
    new_attn, next_attn = advance(attn_weights, mom_attn, grad_attn, factor)
    new_ffn, next_ffn = advance(ffn_weights, ffn_momentum, grad_ffn, factor)
    new_bias_qv, next_bias_qv = advance(bias_qv, mom_bias_qv, grad_bias_qv, factor)
    new_bias_up, next_bias_up = advance(bias_up, mom_bias_up, grad_bias_up, factor)
    new_norms, next_norms = advance(norms, mom_norms, grad_norms, factor)
    new_head_first, next_head_first = advance(head_first, mom_head_first, grad_head_first, factor)
    new_head_second, next_head_second = advance(head_second, mom_head_second, grad_head_second, factor)
    new_head_bias, next_head_bias = advance(head_bias, mom_head_bias, grad_head_bias, factor)
    return (
        new_embedding, new_positions, new_attn, new_ffn, new_bias_qv, new_bias_up, new_norms, new_head_first,
        new_head_second, new_head_bias, next_embedding, next_positions, next_attn, next_ffn, next_bias_qv,
        next_bias_up, next_norms, next_head_first, next_head_second, next_head_bias, loss, grad_norm,
    )


def solution(mesh):
    in_specs = (
        P("dp", None),
        P("dp"),
        P(),
        P("dp", "tensor"),
        P(None, "tensor"),
        P(None, None, "tensor"),
        P(None, None, "tensor"),
        P(None, "tensor"),
        P("tensor"),
        P(),
        P(),
        P(),
        P(),
        P("dp", "tensor"),
        P(None, "tensor"),
        P(None, None, "tensor"),
        P(None, None, "tensor"),
        P(None, "tensor"),
        P("tensor"),
        P(),
        P(),
        P(),
        P(),
    )
    out_specs = (
        P("dp", "tensor"),
        P(None, "tensor"),
        P(None, None, "tensor"),
        P(None, None, "tensor"),
        P(None, "tensor"),
        P("tensor"),
        P(),
        P(),
        P(),
        P(),
        P("dp", "tensor"),
        P(None, "tensor"),
        P(None, None, "tensor"),
        P(None, None, "tensor"),
        P(None, "tensor"),
        P("tensor"),
        P(),
        P(),
        P(),
        P(),
        P(),
        P(),
    )
    groups, shards = mesh.shape["dp"], mesh.shape["tensor"]

    def run(*arrays):
        body = on_device
        if 2 * (arrays[0].shape[0] // groups) == 3 * shards:
            body = functools.partial(fast_on_device, groups=groups, shards=shards)
        return jax.shard_map(
            body, mesh=mesh, in_specs=in_specs, out_specs=out_specs, check_vma=False
        )(*arrays)

    return run
```

```python
import functools
import math

import jax
import jax.numpy as jnp
from jax import lax
from jax.experimental import pallas as pl
from jax.experimental.pallas import tpu as pltpu
from jax.sharding import PartitionSpec as P

HEAD_DIM = 64
PARAMS = 65044736


EPS = 1e-05
SOFTMAX_TEMP = 0.1
DECAY = 0.9
RATE = 100000.0
CLIP_SCALE = 1e-06
HIGH = lax.Precision.HIGHEST
PRODUCT = lax.Precision.HIGH
CAPACITY = 88


def precise_product(left, right):
    return jnp.matmul(left, right, precision=HIGH)


def norm_rows(values, gain, shift):
    center = values - jnp.mean(values, axis=-1, keepdims=True)
    spread = jnp.mean(center * center, axis=-1, keepdims=True)
    return center * lax.rsqrt(spread + EPS) * gain + shift


def attend(normed, lengths, attn, bias_qv):
    seqs, slots, width = normed.shape
    cols = attn.shape[2]
    heads = cols // HEAD_DIM
    queries = (precise_product(normed, attn[0]) + bias_qv[0]).reshape(seqs, slots, heads, HEAD_DIM)
    keys_all = precise_product(normed, attn[1]).reshape(seqs, slots, heads, HEAD_DIM)
    values = (precise_product(normed, attn[2]) + bias_qv[1]).reshape(seqs, slots, heads, HEAD_DIM)
    scores = jnp.einsum("sqhd,skhd->shqk", queries, keys_all, precision=HIGH) / math.sqrt(HEAD_DIM)
    valid = lax.broadcasted_iota(jnp.int32, (seqs, slots), 1) < lengths[:, None]
    scores = jnp.where(valid[:, None, None, :], scores, -1e30)
    probs = jax.nn.softmax(scores, axis=-1)
    mixed = jnp.einsum("shqk,skhd->sqhd", probs, values, precision=HIGH).reshape(seqs, slots, cols)
    return precise_product(mixed, attn[3].T)


def expand(normed, ffn, bias_up):
    hidden = jax.nn.gelu(precise_product(normed, ffn[0]) + bias_up, approximate=False)
    return precise_product(hidden, ffn[1].T)


def contrast(pooled, head_first, head_second, head_bias, partners):
    middle = jax.nn.gelu(precise_product(pooled, head_first) + head_bias, approximate=False)
    output = precise_product(middle, head_second)
    unit_vectors = output * lax.rsqrt(jnp.sum(output * output, axis=-1, keepdims=True) + 1e-06)
    similarity_scores = precise_product(unit_vectors, unit_vectors.T) / SOFTMAX_TEMP
    count = similarity_scores.shape[0]
    index = lax.broadcasted_iota(jnp.int32, (count,), 0)
    similarity_scores = jnp.where(index[:, None] == index[None, :], -1e30, similarity_scores)
    totals = jax.nn.logsumexp(similarity_scores, axis=-1)
    paired_rows = jnp.sum(
        jnp.where(index[None, :] == partners[:, None], similarity_scores, 0.0), axis=-1
    )
    return jnp.sum(totals - paired_rows)


def owner_rows(ids_part, base, vocab_rows):
    local_ids = ids_part - base
    inside = (local_ids >= 0) & (local_ids < vocab_rows)
    return jnp.where(inside, local_ids, vocab_rows)


def advance(weight, moment, grad, factor):
    clipped = factor * grad
    moment_new = DECAY * moment + (1.0 - DECAY) * clipped
    return (weight - RATE * (DECAY * moment_new + (1.0 - DECAY) * clipped), moment_new)


def squares(array):
    return jnp.sum(array * array)


def on_device(
    token_ids,
    lengths,
    partners,
    embedding,
    positions,
    attn_weights,
    ffn_weights,
    bias_qv,
    bias_up,
    norms,
    head_first,
    head_second,
    head_bias,
    mom_embedding,
    mom_positions,
    mom_attn,
    ffn_momentum,
    mom_bias_qv,
    mom_bias_up,
    mom_norms,
    mom_head_first,
    mom_head_second,
    mom_head_bias,
):
    seqs, slots = token_ids.shape
    vocab_rows, cols = embedding.shape
    dp_rank = lax.axis_index("dp")
    tp_rank = lax.axis_index("tensor")
    base = dp_rank * vocab_rows
    all_ids = lax.all_gather(token_ids, "dp", axis=0, tiled=True).reshape(-1)
    padded_table = jnp.concatenate([embedding, jnp.zeros((1, cols), jnp.float32)], axis=0)
    rows_ids = owner_rows(all_ids, base, vocab_rows)
    token_rows = lax.psum_scatter(
        jnp.take(padded_table, rows_ids, axis=0), "dp", scatter_dimension=0, tiled=True
    )
    token_cols = token_rows.reshape(seqs, slots, cols) + positions[2 : slots + 2][None]
    embedded = lax.all_gather(token_cols, "tensor", axis=2, tiled=True)
    h_zero, ln_zero_pull = jax.vjp(norm_rows, embedded, norms[0], norms[1])
    attn_part, attn_pull = jax.vjp(
        lambda normed, weights, biases: attend(normed, lengths, weights, biases),
        h_zero,
        attn_weights,
        bias_qv,
    )
    x_one = h_zero + lax.psum(attn_part, "tensor") + norms[6]
    h_one, ln_one_pull = jax.vjp(norm_rows, x_one, norms[2], norms[3])
    ffn_part, ffn_pull = jax.vjp(expand, h_one, ffn_weights, bias_up)
    x_two = h_one + lax.psum(ffn_part, "tensor") + norms[7]
    h_two, ln_two_pull = jax.vjp(norm_rows, x_two, norms[4], norms[5])
    valid = (lax.broadcasted_iota(jnp.int32, (seqs, slots), 1) < lengths[:, None]).astype(
        jnp.float32
    )
    len_float = lengths.astype(jnp.float32)
    pooled = jnp.sum(h_two * valid[:, :, None], axis=1) / len_float[:, None]
    all_pooled = lax.all_gather(pooled, "dp", axis=0, tiled=True)
    loss, head_pull = jax.vjp(
        lambda rows, first_w, second_w, bias_w: contrast(rows, first_w, second_w, bias_w, partners),
        all_pooled,
        head_first,
        head_second,
        head_bias,
    )
    back_pooled_all, grad_head_first, grad_head_second, grad_head_bias = head_pull(
        jnp.ones_like(loss)
    )
    back_pooled = lax.dynamic_slice_in_dim(back_pooled_all, dp_rank * seqs, seqs)
    back_h_two = valid[:, :, None] * (back_pooled / len_float[:, None])[:, None, :]
    back_x_two, grad_gain_two, grad_shift_two = ln_two_pull(back_h_two)
    back_h_one_part, grad_ffn, grad_bias_up = ffn_pull(back_x_two)
    back_h_one = back_x_two + lax.psum(back_h_one_part, "tensor")
    back_x_one, grad_gain_one, grad_shift_one = ln_one_pull(back_h_one)
    back_h_zero_part, grad_attn, grad_bias_qv = attn_pull(back_x_one)
    back_h_zero = back_x_one + lax.psum(back_h_zero_part, "tensor")
    back_embedded, grad_gain_zero, grad_shift_zero = ln_zero_pull(back_h_zero)
    back_cols = lax.dynamic_slice_in_dim(back_embedded, tp_rank * cols, cols, 2)
    grad_positions = jnp.pad(
        jnp.sum(back_cols, axis=0), ((2, positions.shape[0] - slots - 2), (0, 0))
    )
    grad_norms = jnp.stack(
        [
            grad_gain_zero,
            grad_shift_zero,
            grad_gain_one,
            grad_shift_one,
            grad_gain_two,
            grad_shift_two,
            jnp.sum(back_x_one, axis=(0, 1)),
            jnp.sum(back_x_two, axis=(0, 1)),
        ]
    )
    back_flat = back_cols.reshape(seqs * slots, cols)
    target = owner_rows(all_ids, base, vocab_rows)
    grad_embedding = jax.ops.segment_sum(
        lax.all_gather(back_flat, "dp", axis=0, tiled=True), target, num_segments=vocab_rows + 1
    )[:vocab_rows]
    first_dp = (dp_rank == 0).astype(jnp.float32)
    first_all = first_dp * (tp_rank == 0).astype(jnp.float32)
    grad_attn, grad_ffn, grad_positions, grad_bias_qv, grad_bias_up, grad_norms = lax.psum(
        (grad_attn, grad_ffn, grad_positions, grad_bias_qv, grad_bias_up, grad_norms), "dp"
    )
    big_squares = first_dp * (squares(grad_attn) + squares(grad_ffn))
    local_squares = (
        big_squares
        + squares(grad_embedding)
        + first_dp * (squares(grad_positions) + squares(grad_bias_qv) + squares(grad_bias_up))
        + first_all
        * (
            squares(grad_norms)
            + squares(grad_head_first)
            + squares(grad_head_second)
            + squares(grad_head_bias)
        )
    )
    total_squares = lax.psum(local_squares, ("dp", "tensor"))
    grad_norm = jnp.sqrt(total_squares)
    factor = jnp.minimum(1.0, CLIP_SCALE * math.sqrt(PARAMS) / (grad_norm + 1e-06))
    new_attn, next_attn = advance(attn_weights, mom_attn, grad_attn, factor)
    new_ffn, next_ffn = advance(ffn_weights, ffn_momentum, grad_ffn, factor)
    new_embedding, next_embedding = advance(embedding, mom_embedding, grad_embedding, factor)
    new_positions, next_positions = advance(positions, mom_positions, grad_positions, factor)
    new_bias_qv, next_bias_qv = advance(bias_qv, mom_bias_qv, grad_bias_qv, factor)
    new_bias_up, next_bias_up = advance(bias_up, mom_bias_up, grad_bias_up, factor)
    new_norms, next_norms = advance(norms, mom_norms, grad_norms, factor)
    new_head_first, next_head_first = advance(head_first, mom_head_first, grad_head_first, factor)
    new_head_second, next_head_second = advance(
        head_second, mom_head_second, grad_head_second, factor
    )
    new_head_bias, next_head_bias = advance(head_bias, mom_head_bias, grad_head_bias, factor)
    return (
        new_embedding,
        new_positions,
        new_attn,
        new_ffn,
        new_bias_qv,
        new_bias_up,
        new_norms,
        new_head_first,
        new_head_second,
        new_head_bias,
        next_embedding,
        next_positions,
        next_attn,
        next_ffn,
        next_bias_qv,
        next_bias_up,
        next_norms,
        next_head_first,
        next_head_second,
        next_head_bias,
        loss,
        grad_norm,
    )


MESH = pl.DeviceIdType.MESH
VMEM = pl.BlockSpec(memory_space=pltpu.VMEM)


def cube_partners(groups, shards):
    dp, tp = lax.axis_index("dp"), lax.axis_index("tensor")
    partners = []
    for size, at in ((shards, 1), (groups, 0)):
        bit = 1
        while bit < size:
            here = (dp, tp)[at]
            there = here + bit * (1 - 2 * ((here // bit) % 2))
            partners.append((dp, there) if at else (there, tp))
            bit *= 2
    return partners


def greet(partners):
    barrier = pltpu.get_barrier_semaphore()
    for partner in partners:
        pl.semaphore_signal(barrier, inc=1, device_id=partner, device_id_type=MESH)
    pl.semaphore_wait(barrier, len(partners))


def cube_stages(groups, shards):
    return (groups * shards).bit_length() - 1


def cube_gather_kernel(groups, shards, x_ref, o_ref, held, send_sem, recv_sem):
    partners = cube_partners(groups, shards)
    greet(partners)
    me = lax.axis_index("dp") * shards + lax.axis_index("tensor")
    held[pl.ds(me, 1)] = x_ref[...][None]
    for stage, partner in enumerate(partners):
        size = 1 << stage
        mine = pl.ds((me // size) * size, size)
        copy = pltpu.make_async_remote_copy(
            src_ref=held.at[mine],
            dst_ref=held.at[mine],
            send_sem=send_sem.at[stage],
            recv_sem=recv_sem.at[stage],
            device_id=partner,
            device_id_type=MESH,
        )
        copy.start()
        copy.wait()
    o_ref[...] = held[...]


def cube_gather(block, groups, shards, collective_id):
    stages = cube_stages(groups, shards)
    shape = (groups * shards, *block.shape)
    return pl.pallas_call(
        functools.partial(cube_gather_kernel, groups, shards),
        out_shape=jax.ShapeDtypeStruct(shape, block.dtype),
        in_specs=[VMEM],
        out_specs=VMEM,
        scratch_shapes=[
            pltpu.VMEM(shape, block.dtype),
            pltpu.SemaphoreType.DMA((stages,)),
            pltpu.SemaphoreType.DMA((stages,)),
        ],
        compiler_params=pltpu.CompilerParams(collective_id=collective_id, has_side_effects=True),
    )(block)


def fold_squares(block):
    block = block * block
    folded = jnp.sum(block.reshape(block.shape[0] // 8, 8, block.shape[1]), axis=0)
    total = folded[:, :128]
    for start in range(128, block.shape[1], 128):
        total = total + folded[:, start : start + 128]
    return total


def ring_kernel(groups, shards, parts, arrays, shared_rows, *refs):
    refs = list(refs)
    inputs = [refs.pop(0) for _ in range(arrays)]
    base = refs.pop(0)
    outputs = [refs.pop(0) for _ in range(arrays)]
    squares_ref = refs.pop(0)
    slots = [refs.pop(0) for _ in range(arrays)]
    send_sem, recv_sem, sent, landed, cube_send, cube_recv = refs
    depth = groups // 2
    dp, tp = lax.axis_index("dp"), lax.axis_index("tensor")
    side, level = dp % 2, dp // 2
    place = level * (1 - side) + (groups - 1 - level) * side

    def device_at(spot):
        spot = (spot + groups) % groups
        far = spot // depth
        return (2 * (spot * (1 - far) + (groups - 1 - spot) * far) + far, tp)

    partners = cube_partners(groups, shards) if shared_rows else []
    greet([device_at(place + 1), device_at(place - 1), *partners])
    streams = []
    for array in range(arrays):
        rows = inputs[array].shape[1] // (2 * parts)
        for part in range(2 * parts):
            streams.append((array, 1 - 2 * (part % 2), part * rows, rows))

    def chunk(step, way):
        return (place + groups * 2 - way * step) % groups

    copies = []

    def send(source, target, send_at, recv_at, device):
        copy = pltpu.make_async_remote_copy(
            src_ref=source,
            dst_ref=target,
            send_sem=send_at,
            recv_sem=recv_at,
            device_id=device,
            device_id_type=MESH,
        )
        copy.start()
        copies.append(copy)
        return copy

    def pass_on(index, step, source, target):
        device = device_at(place + streams[index][1])
        return send(source, target, send_sem.at[index, step], recv_sem.at[index, step], device)

    flying = [None] * len(streams)
    for step in range(groups - 1):
        for index, (array, way, start, size) in enumerate(streams):
            rows = pl.ds(start, size)
            if step == 0:
                source = inputs[array].at[chunk(0, way), rows]
            else:
                flying[index].wait_recv()
                source = slots[array].at[step - 1, rows]
                source[...] = source[...] + inputs[array][chunk(step, way), rows]
            flying[index] = pass_on(index, step, source, slots[array].at[step, rows])
    total = base[...]
    crossing = None
    for step in range(groups - 1):
        for index, (array, way, start, size) in enumerate(streams):
            rows = pl.ds(start, size)
            flying[index].wait_recv()
            now = chunk(groups - 1 + step, way)
            if step == 0:
                block = slots[array][groups - 2, rows] + inputs[array][now, rows]
                outputs[array][now, rows] = block
                if shared_rows:
                    depth_rows = inputs[array].shape[1]
                    limit = groups * depth_rows - shared_rows * (1 - (shards - tp) // shards)
                    at = now * depth_rows + start + lax.broadcasted_iota(jnp.int32, block.shape, 0)
                    block = jnp.where(at < limit, block, 0.0)
                total = total + fold_squares(block)
            out = outputs[array].at[now, rows]
            flying[index] = pass_on(index, groups - 1 + step, out, out)
        if step <= len(partners) and partners:
            if step == 0:
                sent[0] = total
            else:
                crossing.wait_recv()
                sent[step] = sent[step - 1] + landed[step - 1]
            if step < len(partners):
                crossing = send(
                    sent.at[step], landed.at[step], cube_send.at[step], cube_recv.at[step], partners[step]
                )
    squares_ref[...] = sent[len(partners)] if partners else total
    for copy in flying:
        copy.wait_recv()
    for copy in copies:
        copy.wait_send()


def ring_sum(arrays, base, groups, shards, parts, shared_rows, collective_id):
    blocks = [array.reshape(groups, array.shape[0] // groups, array.shape[1]) for array in arrays]
    streams = 2 * parts * len(blocks)
    steps = 2 * (groups - 1)
    stages = cube_stages(groups, shards)
    *sums, squared = pl.pallas_call(
        functools.partial(ring_kernel, groups, shards, parts, len(blocks), shared_rows),
        out_shape=[jax.ShapeDtypeStruct(block.shape, block.dtype) for block in [*blocks, base]],
        in_specs=[VMEM] * (len(blocks) + 1),
        out_specs=[VMEM] * (len(blocks) + 1),
        scratch_shapes=[
            *[pltpu.VMEM((groups - 1, *block.shape[1:]), block.dtype) for block in blocks],
            pltpu.SemaphoreType.DMA((streams, steps)),
            pltpu.SemaphoreType.DMA((streams, steps)),
            pltpu.VMEM((stages + 1, *base.shape), base.dtype),
            pltpu.VMEM((stages, *base.shape), base.dtype),
            pltpu.SemaphoreType.DMA((stages,)),
            pltpu.SemaphoreType.DMA((stages,)),
        ],
        compiler_params=pltpu.CompilerParams(
            collective_id=collective_id, has_side_effects=True, vmem_limit_bytes=48 << 20
        ),
        cost_estimate=pl.CostEstimate(flops=1, bytes_accessed=1024, transcendentals=0),
    )(*blocks, base)
    return [total.reshape(array.shape) for total, array in zip(sums, arrays)], squared


def spread_kernel(
    groups, w_ref, small_ref, o_ref, rows_ref, local_sem, pair_send, pair_recv, ring_send, ring_recv, core_send, core_recv
):
    depth = groups // 2
    dp, tp = lax.axis_index("dp"), lax.axis_index("tensor")
    far = tp + 2 - 4 * (tp // 2)
    core = (dp, tp + 1 - 2 * (tp % 2))
    side, level = dp % 2, dp // 2
    place = level * (1 - side) + (groups - 1 - level) * side

    def index_at(spot):
        spot = (spot + groups) % groups
        back = spot // depth
        return 2 * (spot * (1 - back) + (groups - 1 - spot) * back) + back

    def send(source, target, send_sem, recv_sem, device):
        copy = pltpu.make_async_remote_copy(
            src_ref=source,
            dst_ref=target,
            send_sem=send_sem,
            recv_sem=recv_sem,
            device_id=device,
            device_id_type=MESH,
        )
        copy.start()
        return copy

    greet([(index_at(place + 1), tp), (index_at(place - 1), tp), core, (dp, far)])
    cross = send(w_ref.at[dp], o_ref.at[tp, dp], pair_send.at[0], pair_recv.at[0], (dp, far))
    near = send(w_ref, o_ref.at[tp], pair_send.at[1], pair_recv.at[1], core)
    cross_rows = send(small_ref, rows_ref.at[tp], pair_send.at[2], pair_recv.at[2], (dp, far))
    near_rows = send(small_ref, rows_ref.at[tp], pair_send.at[3], pair_recv.at[3], core)
    local = pltpu.make_async_copy(w_ref, o_ref.at[tp], local_sem)
    local.start()
    rows_ref[tp] = small_ref[...]
    cross.wait_recv()
    lanes = ring_send.shape[0]
    size = w_ref.shape[1] // lanes
    flying = [None] * lanes
    started = [cross, cross_rows]
    handed = [near, near_rows]
    for step in range(groups):
        for lane in range(lanes):
            way = 1 - 2 * (lane % 2)
            block = o_ref.at[far, index_at(place + groups - way * step), pl.ds(lane * size, size)]
            if step > 0:
                flying[lane].wait_recv()
            if step < groups - 1:
                flying[lane] = send(
                    block, block, ring_send.at[lane, step], ring_recv.at[lane, step], (index_at(place + way), tp)
                )
                started.append(flying[lane])
            handed.append(send(block, block, core_send.at[lane, step], core_recv.at[lane, step], core))
    cross_rows.wait_recv()
    handed.append(send(rows_ref.at[far], rows_ref.at[far], pair_send.at[4], pair_recv.at[4], core))
    for copy in handed:
        copy.wait_recv()
        copy.wait_send()
    for copy in started:
        copy.wait_send()
    local.wait()


def spread(weight, small, groups, collective_id):
    rows = weight.shape[0] // groups
    lanes = 4
    gathered, gathered_rows = pl.pallas_call(
        functools.partial(spread_kernel, groups),
        out_shape=[
            jax.ShapeDtypeStruct((4, groups, rows, weight.shape[1]), weight.dtype),
            jax.ShapeDtypeStruct((4, *small.shape), small.dtype),
        ],
        in_specs=[pl.BlockSpec(memory_space=pl.ANY), VMEM],
        out_specs=[VMEM, VMEM],
        scratch_shapes=[
            pltpu.SemaphoreType.DMA,
            pltpu.SemaphoreType.DMA((5,)),
            pltpu.SemaphoreType.DMA((5,)),
            pltpu.SemaphoreType.DMA((lanes, groups - 1)),
            pltpu.SemaphoreType.DMA((lanes, groups - 1)),
            pltpu.SemaphoreType.DMA((lanes, groups)),
            pltpu.SemaphoreType.DMA((lanes, groups)),
        ],
        compiler_params=pltpu.CompilerParams(
            collective_id=collective_id, has_side_effects=True, vmem_limit_bytes=32 << 20
        ),
        cost_estimate=pl.CostEstimate(flops=1, bytes_accessed=1024, transcendentals=0),
    )(weight.reshape(groups, rows, weight.shape[1]), small)
    return gathered.reshape(4, *weight.shape), gathered_rows


def halves(array):
    high = array.astype(jnp.bfloat16)
    return high, (array - high.astype(jnp.float32)).astype(jnp.bfloat16)


def dot_rows(left, right):
    return lax.dot_general(left, right, (((1,), (1,)), ((), ())), preferred_element_type=jnp.float32)


def dot_plain(left, right):
    return lax.dot_general(left, right, (((1,), (0,)), ((), ())), preferred_element_type=jnp.float32)


def one_head(array, head):
    lane = lax.broadcasted_iota(jnp.int32, array.shape, 1)
    return jnp.where(lane // HEAD_DIM == head, array, 0.0)


def score_tile(twice_k, low_k, high_q, low_q, bias):
    wide = dot_rows(twice_k, jnp.concatenate([high_q, low_q], axis=1))
    return wide + dot_rows(low_k, high_q) + bias


def attend_kernel(slots, tile, q_ref, k_ref, v_ref, bias_ref, o_ref, lse_ref):
    scale = 1.0 / math.sqrt(HEAD_DIM)
    high_k, low_k = halves(k_ref[0])
    twice_k = jnp.concatenate([high_k, high_k], axis=1)
    high_v, low_v = halves(v_ref[0].T)
    for start in range(0, q_ref.shape[1], tile):
        rows = pl.ds(start, tile)
        first = 0 if start < slots else slots
        keys = slice(first, first + slots)
        found = []
        for head in range(2):
            high_q, low_q = halves(one_head(q_ref[0, rows] * scale, head))
            scores = score_tile(twice_k[keys], low_k[keys], high_q, low_q, bias_ref[pl.ds(first, slots)])
            peak = jnp.max(scores, axis=0, keepdims=True)
            probs = jnp.exp(scores - peak)
            total = jnp.sum(probs, axis=0, keepdims=True)
            lse_ref[0, pl.ds(head, 1), rows] = peak + jnp.log(total)
            high_p, low_p = halves(probs)
            lanes = slice(head * HEAD_DIM, (head + 1) * HEAD_DIM)
            both = jnp.concatenate([high_v[lanes, keys], low_v[lanes, keys]], axis=0)
            wide = dot_plain(both, high_p)
            mixed = wide[:HEAD_DIM] + wide[HEAD_DIM:] + dot_plain(high_v[lanes, keys], low_p)
            found.append(mixed / total)
        o_ref[0, rows] = jnp.concatenate(found, axis=0).T


def attend_back_kernel(slots, tile, q_ref, k_ref, v_ref, bias_ref, o_ref, lse_ref, d_ref, dq_ref, dk_ref, dv_ref):
    scale = 1.0 / math.sqrt(HEAD_DIM)
    high_k, low_k = halves(k_ref[0])
    twice_k = jnp.concatenate([high_k, high_k], axis=1)
    high_v, low_v = halves(v_ref[0])
    twice_v = jnp.concatenate([high_v, high_v], axis=1)
    high_kt, low_kt = halves(k_ref[0].T)
    ones = jnp.ones((8, 2 * HEAD_DIM), jnp.bfloat16)
    lanes = 2 * HEAD_DIM
    for first in (0, slots):
        keys = slice(first, first + slots)
        key_rows = pl.ds(first, slots)
        for start in range(first, min(first + slots, q_ref.shape[1]), tile):
            rows = pl.ds(start, tile)
            back_qt = []
            for head in range(2):
                high_q, low_q = halves(one_head(q_ref[0, rows] * scale, head))
                back = one_head(d_ref[0, rows], head)
                high_d, low_d = halves(back)
                scores = score_tile(twice_k[keys], low_k[keys], high_q, low_q, bias_ref[key_rows])
                probs = jnp.exp(scores - lse_ref[0, pl.ds(head, 1), rows])
                high_x, low_x = halves(back * o_ref[0, rows])
                inner = (dot_rows(ones, high_x) + dot_rows(ones, low_x))[:1]
                back_s = probs * (score_tile(twice_v[keys], low_v[keys], high_d, low_d, 0.0) - inner)
                high_p, low_p = halves(probs)
                high_s, low_s = halves(back_s)
                wide = dot_plain(high_p, jnp.concatenate([high_d, low_d], axis=1))
                back_v = wide[:, :lanes] + wide[:, lanes:] + dot_plain(low_p, high_d)
                wide = dot_plain(high_s, jnp.concatenate([high_q, low_q], axis=1))
                back_k = wide[:, :lanes] + wide[:, lanes:] + dot_plain(low_s, high_q)
                if start == first and head == 0:
                    dv_ref[0, key_rows] = back_v
                    dk_ref[0, key_rows] = back_k
                else:
                    dv_ref[0, key_rows] += back_v
                    dk_ref[0, key_rows] += back_k
                mine = slice(head * HEAD_DIM, (head + 1) * HEAD_DIM)
                both = jnp.concatenate([high_kt[mine, keys], low_kt[mine, keys]], axis=0)
                wide = dot_plain(both, high_s)
                back_qt.append(wide[:HEAD_DIM] + wide[HEAD_DIM:] + dot_plain(high_kt[mine, keys], low_s))
            dq_ref[0, rows] = jnp.concatenate(back_qt, axis=0).T * scale


def attend_call(kernel, slots, inputs, outputs):
    lanes = 2 * HEAD_DIM
    queries = inputs[0]
    per_shard = queries.shape[2] // lanes
    pairs = queries.shape[0] * per_shard

    def spec(shape):
        if shape[1] == 1:
            return pl.BlockSpec(shape, lambda i: (0, 0))
        if shape[1] == 2:
            return pl.BlockSpec((1, *shape[1:]), lambda i: (i, 0, 0))
        return pl.BlockSpec((1, shape[1], lanes), lambda i: (i // per_shard, 0, i % per_shard))

    work = 7 * 2 * pairs * 2 * queries.shape[1] * slots * HEAD_DIM * 3
    return pl.pallas_call(
        functools.partial(kernel, slots, slots // 2),
        grid=(pairs,),
        in_specs=[spec(x.shape) for x in inputs],
        out_specs=[spec(shape) for shape in outputs],
        out_shape=[jax.ShapeDtypeStruct(shape, jnp.float32) for shape in outputs],
        compiler_params=pltpu.CompilerParams(vmem_limit_bytes=48 << 20),
        cost_estimate=pl.CostEstimate(flops=4 * work, bytes_accessed=20 << 20, transcendentals=0),
    )(*inputs)


WIDE = 512


def dot_three(high_left, low_left, right, dot):
    high, low = halves(right)
    return dot(high_left, high) + dot(high_left, low) + dot(low_left, high)


def times_kernel(finish, extras, x_ref, w_ref, *refs):
    more, outs, (high, low) = refs[:extras], refs[extras:-2], refs[-2:]

    @pl.when((pl.program_id(0) == 0) & (pl.program_id(1) == 0))
    def _():
        high[...], low[...] = halves(x_ref[...])

    weight = w_ref[...].reshape(w_ref.shape[-2], w_ref.shape[-1])
    finish(dot_three(high[...], low[...], weight, dot_plain), more, outs)


def times(x, w, which, finish, extras, outs):
    shards, depth, columns = w.shape[0], w.shape[-2], w.shape[-1]
    rows, wide = x.shape[0], min(WIDE, columns)
    if w.ndim == 4:
        w_spec = pl.BlockSpec((1, 1, depth, wide), lambda j, c: (j, which, 0, c))
    else:
        w_spec = pl.BlockSpec((1, depth, wide), lambda j, c: (j, 0, c))

    def spec(shape):
        return pl.BlockSpec((1, shape[1], wide), lambda j, c: (j, 0, c))

    results = pl.pallas_call(
        functools.partial(times_kernel, finish, len(extras)),
        grid=(shards, columns // wide),
        in_specs=[pl.BlockSpec((rows, depth), lambda j, c: (0, 0)), w_spec, *[spec(e.shape) for e in extras]],
        out_specs=[spec(shape) for shape in outs],
        out_shape=[jax.ShapeDtypeStruct(shape, jnp.float32) for shape in outs],
        scratch_shapes=[pltpu.VMEM((rows, depth), jnp.bfloat16)] * 2,
        compiler_params=pltpu.CompilerParams(vmem_limit_bytes=48 << 20),
        cost_estimate=pl.CostEstimate(
            flops=6 * rows * depth * shards * columns, bytes_accessed=4 * w.size, transcendentals=0
        ),
    )(x, w, *extras)
    return results


def keep_tile(tile, more, outs):
    outs[0][0] = tile


def add_row(tile, more, outs):
    outs[0][0] = tile + more[0][0]


def gelu_tile(tile, more, outs):
    outs[0][0], outs[1][0] = gelu_both(tile + more[0][0])


def scale_tile(tile, more, outs):
    tile = tile * more[0][0]
    outs[0][0] = tile
    outs[1][0] = jnp.sum(tile, axis=0, keepdims=True)


def gather_back_kernel(count, base_ref, *refs):
    out = refs[-1]

    @pl.when((pl.program_id(0) == 0) & (pl.program_id(1) == 0))
    def _():
        out[...] = base_ref[...]

    for a_ref, w_ref in zip(refs[:count], refs[count : 2 * count]):
        high, low = halves(a_ref[0])
        weight = w_ref[...].reshape(w_ref.shape[-2], w_ref.shape[-1])
        rows = pl.ds(0, a_ref.shape[1])
        out[rows] += dot_three(high, low, weight, dot_rows)


def gather_back(base, terms):
    arrays = [array for array, _, _ in terms]
    shards, _, columns = arrays[0].shape
    wide = min(WIDE, columns)

    def w_spec(w, which):
        if w.ndim == 4:
            return pl.BlockSpec((1, 1, w.shape[-2], wide), lambda j, c: (j, which, 0, c))
        return pl.BlockSpec((1, w.shape[-2], wide), lambda j, c: (j, 0, c))

    work = sum(6 * array.size * w.shape[-2] for array, w, _ in terms)
    return pl.pallas_call(
        functools.partial(gather_back_kernel, len(terms)),
        grid=(shards, columns // wide),
        in_specs=[
            pl.BlockSpec(base.shape, lambda j, c: (0, 0)),
            *[pl.BlockSpec((1, a.shape[1], wide), lambda j, c: (j, 0, c)) for a in arrays],
            *[w_spec(w, which) for _, w, which in terms],
        ],
        out_specs=pl.BlockSpec(base.shape, lambda j, c: (0, 0)),
        out_shape=jax.ShapeDtypeStruct(base.shape, jnp.float32),
        compiler_params=pltpu.CompilerParams(vmem_limit_bytes=48 << 20),
        cost_estimate=pl.CostEstimate(flops=work, bytes_accessed=16 << 20, transcendentals=0),
    )(base, *arrays, *[w for _, w, _ in terms])


def outer_kernel(x_ref, d_ref, *refs):
    out, high, low = refs[-3:]

    @pl.when((pl.program_id(0) == 0) & (pl.program_id(1) == 0))
    def _():
        high[...], low[...] = halves(x_ref[...].T)

    out[0] = dot_three(high[...], low[...], d_ref[0], dot_plain)


def outer(x, d, rows, at, into=None):
    tokens, depth = x.shape
    shards, _, columns = d.shape
    wide = min(WIDE, columns)
    held = [] if into is None else [into]
    return pl.pallas_call(
        outer_kernel,
        grid=(shards, columns // wide),
        in_specs=[
            pl.BlockSpec((tokens, depth), lambda j, c: (0, 0)),
            pl.BlockSpec((1, tokens, wide), lambda j, c: (j, 0, c)),
            *[pl.BlockSpec(memory_space=pl.ANY) for _ in held],
        ],
        out_specs=pl.BlockSpec((1, depth, wide), lambda j, c: (j, at, c)),
        out_shape=jax.ShapeDtypeStruct((shards, rows, columns), jnp.float32),
        scratch_shapes=[pltpu.VMEM((depth, tokens), jnp.bfloat16)] * 2,
        input_output_aliases={2: 0} if held else {},
        compiler_params=pltpu.CompilerParams(vmem_limit_bytes=48 << 20),
        cost_estimate=pl.CostEstimate(
            flops=6 * tokens * depth * shards * columns, bytes_accessed=4 * shards * depth * columns, transcendentals=0
        ),
    )(x, d, *held)


def normalise(values):
    center = values - jnp.mean(values, axis=-1, keepdims=True)
    scale = lax.rsqrt(jnp.mean(center * center, axis=-1, keepdims=True) + EPS)
    return center * scale, scale


def normalise_back(back, gain, unit, scale):
    inner = back * gain
    grad = scale * (
        inner
        - jnp.mean(inner, axis=-1, keepdims=True)
        - unit * jnp.mean(inner * unit, axis=-1, keepdims=True)
    )
    return grad, jnp.sum(back * unit, axis=0), jnp.sum(back, axis=0)


def gelu_both(values):
    cdf = 0.5 * (1.0 + lax.erf(values * math.sqrt(0.5)))
    pdf = jnp.exp(-0.5 * values * values) * (1.0 / math.sqrt(2.0 * math.pi))
    return values * cdf, cdf + values * pdf


def product(subscripts, left, right):
    return jnp.einsum(subscripts, left, right, precision=PRODUCT)


def request_lists(ids, vocab_rows, owners):
    count = ids.shape[0]
    index = lax.broadcasted_iota(jnp.int32, (count,), 0)
    earlier = index[None, :] < index[:, None]
    same = (ids[None, :] == ids[:, None]) & earlier
    first = jnp.logical_not(jnp.any(same, axis=1))
    owner = ids // vocab_rows
    ahead = (owner[None, :] == owner[:, None]) & earlier & first[None, :]
    rank = jnp.sum(ahead.astype(jnp.int32), axis=1)
    return owner, jnp.where(first, rank, -1)


def round_list(ids, owner, rank, round_index, owners):
    place = rank - round_index * CAPACITY
    inside = (rank >= 0) & (place >= 0) & (place < CAPACITY)
    place = jnp.where(inside, owner * CAPACITY + place, -1)
    wanted = lax.broadcasted_iota(jnp.int32, (owners * CAPACITY, 1), 0)
    return jnp.sum(jnp.where(place[None, :] == wanted, ids[None, :] + 1, 0), axis=1) - 1


def trade(block):
    return lax.all_to_all(block, ("dp", "tensor"), 0, 0, tiled=True)


def fast_on_device(
    token_ids, lengths, partners, embedding, positions, attn_weights, ffn_weights, bias_qv, bias_up, norms,
    head_first, head_second, head_bias, mom_embedding, mom_positions, mom_attn, ffn_momentum, mom_bias_qv,
    mom_bias_up, mom_norms, mom_head_first, mom_head_second, mom_head_bias, *, groups, shards
):
    seqs, slots = token_ids.shape
    half = slots // 2
    vocab_rows, cols = embedding.shape
    width = cols * shards
    devices = groups * shards
    hidden = bias_up.shape[0]
    heads = width // HEAD_DIM
    dp_rank = lax.axis_index("dp")
    tp_rank = lax.axis_index("tensor")
    pair = tp_rank // 2
    side = tp_rank % 2
    base = dp_rank * vocab_rows

    whole_seq = 3 * pair + 2 * side
    split_seq = 3 * pair + 1
    whole_ids = lax.dynamic_index_in_dim(token_ids, whole_seq, 0, keepdims=False)
    split_ids = lax.dynamic_index_in_dim(token_ids, split_seq, 0, keepdims=False)
    ids = jnp.concatenate([whole_ids, lax.dynamic_slice_in_dim(split_ids, side * half, half)])
    count = ids.shape[0]
    whole_length = lax.dynamic_index_in_dim(lengths, whole_seq, 0, keepdims=False)
    split_length = lax.dynamic_index_in_dim(lengths, split_seq, 0, keepdims=False)

    all_attn = lax.all_gather(attn_weights, "tensor")
    parts_shape = (shards, count, hidden)
    all_ffn_down = lax.all_gather(ffn_weights[1], "tensor")
    small = jnp.concatenate([positions[2 : slots + 2], bias_qv, bias_up.reshape(-1, cols)], axis=0)
    small = jnp.pad(small, ((0, -small.shape[0] % 8), (0, 0)))
    swap = [(i, i ^ 1) for i in range(shards)]
    owner, rank = request_lists(ids, vocab_rows, groups)
    rounds_here = jnp.max(rank) // CAPACITY + 1

    def serve(round_index):
        wanted = round_list(ids, owner, rank, round_index, groups)
        lists = jnp.broadcast_to(wanted.reshape(groups, 1, CAPACITY), (groups, shards, CAPACITY))
        lists = lists.reshape(devices, CAPACITY)
        tail = jnp.broadcast_to(rounds_here, (devices, 1)).astype(jnp.int32)
        lists = jnp.concatenate([lists, tail, jnp.zeros((devices, 127 - CAPACITY), jnp.int32)], axis=1)
        asked = trade(lists)
        rows = asked[:, :CAPACITY].reshape(-1) - base
        rounds = jnp.max(asked[:, CAPACITY])
        return wanted, rows, rounds

    def find(rows):
        return jnp.take(embedding, rows, axis=0, mode="clip")

    def expand(wanted, landed):
        landed = landed.reshape(groups, shards, CAPACITY, cols)
        landed = landed.transpose(0, 2, 1, 3).reshape(groups * CAPACITY, width)
        chosen = (ids[:, None] == wanted[None, :]).astype(jnp.float32)
        return jnp.matmul(chosen, landed, precision=HIGH)

    wanted_first, rows_first, rounds = serve(0)
    found, up_weights = lax.optimization_barrier((find(rows_first), ffn_weights[0]))
    all_ffn_up, all_small = spread(up_weights, small, groups, 6)
    landed, all_small = lax.optimization_barrier((trade(found), all_small))
    all_positions = all_small[:, :slots].transpose(1, 0, 2).reshape(slots, width)
    all_bias_up = all_small[:, slots + 2 : slots + 2 + hidden // cols].reshape(-1)
    tokens = expand(wanted_first, landed)

    def more(state):
        return state[0] < rounds

    def fetch_more(state):
        round_index, total = state
        wanted, rows, _ = serve(round_index)
        return round_index + 1, total + expand(wanted, trade(find(rows)))

    _, tokens = lax.while_loop(more, fetch_more, (jnp.int32(1), tokens))
    own_positions = jnp.concatenate(
        [all_positions, lax.dynamic_slice_in_dim(all_positions, side * half, half)], axis=0
    )
    embedded = tokens + own_positions
    unit_zero, scale_zero = normalise(embedded)
    h_zero = unit_zero * norms[0] + norms[1]

    h_other = lax.ppermute(h_zero[slots:], "tensor", swap)
    h_keys = jnp.concatenate([h_zero, h_other], axis=0)
    bias_q, bias_v = all_small[:, slots], all_small[:, slots + 1]
    keys_shape = (shards, count + half, cols)
    (queries,) = times(h_zero, all_attn, 0, add_row, [bias_q[:, None, :]], [(shards, count, cols)])
    (keys_all,) = times(h_keys, all_attn, 1, keep_tile, [], [keys_shape])
    (values,) = times(h_keys, all_attn, 2, add_row, [bias_v[:, None, :]], [keys_shape])
    key_index = lax.broadcasted_iota(jnp.int32, (slots,), 0)
    own_first = jnp.where(
        key_index < half, side * half + key_index, (1 - side) * half + key_index - half
    )
    counted = jnp.concatenate([key_index < whole_length, own_first < split_length])
    key_bias = jnp.where(counted, 0.0, -1e30).astype(jnp.float32)[:, None]
    mixed, lse = attend_call(
        attend_kernel,
        slots,
        (queries, keys_all, values, key_bias),
        (queries.shape, (heads // 2, 2, count)),
    )
    x_one = gather_back(h_zero + norms[6], [(mixed, all_attn, 3)])
    unit_one, scale_one = normalise(x_one)
    h_one = unit_one * norms[2] + norms[3]

    bias_tiles = all_bias_up.reshape(shards, 1, hidden)
    act, act_slope = times(h_one, all_ffn_up, 0, gelu_tile, [bias_tiles], [parts_shape, parts_shape])
    x_two = gather_back(h_one + norms[7], [(act, all_ffn_down, 0)])
    unit_two, scale_two = normalise(x_two)
    h_two = unit_two * norms[4] + norms[5]

    slot = lax.broadcasted_iota(jnp.int32, (count,), 0)
    in_whole = slot < slots
    place = jnp.where(in_whole, slot, slot - slots + side * half)
    keep = place < jnp.where(in_whole, whole_length, split_length)
    weight_whole = jnp.where(keep & in_whole, 1.0 / whole_length.astype(jnp.float32), 0.0)
    weight_split = jnp.where(keep & ~in_whole, 1.0 / split_length.astype(jnp.float32), 0.0)
    sums = jnp.stack(
        [jnp.sum(h_two * weight_whole[:, None], axis=0), jnp.sum(h_two * weight_split[:, None], axis=0)]
    )
    all_sums = cube_gather(sums.reshape(-1, 128), groups, shards, 5).reshape(groups * shards // 2, 2, 2, width)
    all_pooled = jnp.stack(
        [all_sums[:, 0, 0], all_sums[:, 0, 1] + all_sums[:, 1, 1], all_sums[:, 1, 0]], axis=1
    ).reshape(groups * seqs, width)
    loss, head_pull = jax.vjp(
        lambda rows, first_w, second_w, bias_w: contrast(rows, first_w, second_w, bias_w, partners),
        all_pooled,
        head_first,
        head_second,
        head_bias,
    )
    back_pooled, grad_head_first, grad_head_second, grad_head_bias = head_pull(jnp.ones_like(loss))
    first_row = dp_rank * seqs
    back_whole = lax.dynamic_index_in_dim(back_pooled, first_row + whole_seq, 0, keepdims=False)
    back_split = lax.dynamic_index_in_dim(back_pooled, first_row + split_seq, 0, keepdims=False)
    back_h_two = weight_whole[:, None] * back_whole[None, :] + weight_split[:, None] * back_split[None, :]

    back_x_two, grad_gain_two, grad_shift_two = normalise_back(back_h_two, norms[4], unit_two, scale_two)
    grad_down = outer(back_x_two, act, width, 0)
    sum_down = lax.psum_scatter(grad_down, "tensor", scatter_dimension=0, tiled=False)
    back_up, grad_bias_up = times(
        back_x_two, all_ffn_down, 0, scale_tile, [act_slope], [parts_shape, bias_tiles.shape]
    )
    grad_up = outer(h_one, back_up, width, 0)
    back_up, grad_up = lax.optimization_barrier((back_up, grad_up))
    sum_up = lax.psum_scatter(grad_up, "tensor", scatter_dimension=0, tiled=False)
    back_h_one = gather_back(back_x_two, [(back_up, all_ffn_up, 0)])
    back_x_one, grad_gain_one, grad_shift_one = normalise_back(back_h_one, norms[2], unit_one, scale_one)

    (back_mixed,) = times(back_x_one, all_attn, 3, keep_tile, [], [mixed.shape])
    back_q, back_k, back_v = attend_call(
        attend_back_kernel,
        slots,
        (queries, keys_all, values, key_bias, mixed, lse, back_mixed),
        (queries.shape, keys_all.shape, values.shape),
    )
    base_keys = jnp.pad(back_x_one, ((0, half), (0, 0)))
    back_keys = gather_back(
        base_keys, [(back_q, all_attn, 0), (back_k, all_attn, 1), (back_v, all_attn, 2)]
    )
    back_other = lax.ppermute(back_keys[count:], "tensor", swap)
    back_h_zero = back_keys[:count]
    back_h_zero = back_h_zero + jnp.pad(back_other, ((slots, 0), (0, 0)))
    back_embedded, grad_gain_zero, grad_shift_zero = normalise_back(back_h_zero, norms[0], unit_zero, scale_zero)

    def send_back(wanted):
        chosen = (wanted[:, None] == ids[None, :]).astype(jnp.float32)
        summed = jnp.matmul(chosen, back_embedded, precision=HIGH)
        parts = summed.reshape(groups, CAPACITY, shards, cols).transpose(0, 2, 1, 3)
        return parts.reshape(devices * CAPACITY, cols)

    def add_rows(landed, rows, total):
        target = jnp.where(rows >= 0, rows, vocab_rows)
        return total.at[target].add(landed, mode="drop")

    leaving, back_q, back_k, back_v, back_x_one = lax.optimization_barrier(
        (send_back(wanted_first), back_q, back_k, back_v, back_x_one)
    )
    landed_first = trade(leaving)
    part_rows = 4 * width + slots + 256
    parts_attn = outer(h_zero, back_q, part_rows, 0)
    parts_attn = outer(h_keys, back_k, part_rows, 1, parts_attn)
    parts_attn = outer(h_keys, back_v, part_rows, 2, parts_attn)
    parts_attn = outer(back_x_one, mixed, part_rows, 3, parts_attn)
    grad_small = jnp.concatenate(
        [
            jnp.stack(
                [
                    grad_gain_zero,
                    grad_shift_zero,
                    grad_gain_one,
                    grad_shift_one,
                    grad_gain_two,
                    grad_shift_two,
                    jnp.sum(back_x_one, axis=0),
                    jnp.sum(back_x_two, axis=0),
                    jnp.sum(back_q, axis=1).reshape(-1),
                    jnp.sum(back_v, axis=1).reshape(-1),
                ]
            ),
            grad_bias_up.reshape(-1, width),
        ],
        axis=0,
    )
    half_rows = jnp.where(side == 0, 1.0, 0.0) * back_embedded[slots:]
    other_rows = back_embedded[slots:] - half_rows
    grad_pos_full = back_embedded[:slots] + jnp.concatenate([half_rows, other_rows], axis=0)
    grad_pos_parts = grad_pos_full.reshape(slots, shards, cols)
    grad_pos_parts = grad_pos_parts.transpose(1, 0, 2)
    small_size = grad_small.size
    small_rows = jnp.pad(grad_small.reshape(-1), (0, 256 * cols - small_size)).reshape(1, 256, cols)
    small_rows = jnp.broadcast_to(small_rows, (shards, 256, cols))
    parts_attn = lax.dynamic_update_slice(parts_attn, grad_pos_parts, (0, 4 * width, 0))
    parts_attn = lax.dynamic_update_slice(parts_attn, small_rows, (0, 4 * width + slots, 0))
    landed_first, parts_attn = lax.optimization_barrier((landed_first, parts_attn))
    sum_attn = lax.psum_scatter(parts_attn, "tensor", scatter_dimension=0, tiled=False)
    first_all = (dp_rank == 0).astype(jnp.float32) * (tp_rank == 0).astype(jnp.float32)
    head_squares = first_all * (squares(grad_head_first) + squares(grad_head_second) + squares(grad_head_bias))
    corner = (lax.broadcasted_iota(jnp.int32, (8, 128), 0) + lax.broadcasted_iota(jnp.int32, (8, 128), 1)) == 0
    tile = jnp.where(corner, head_squares, 0.0)
    (sum_down,), tile = ring_sum([sum_down], tile, groups, shards, 2, 0, 1)
    (sum_up,), squared = ring_sum([sum_up], tile, groups, shards, 2, 0, 3)
    landed_first, sum_up = lax.optimization_barrier((landed_first, sum_up))
    zero_table = jnp.zeros((vocab_rows, cols), jnp.float32)
    grad_embedding = add_rows(landed_first, rows_first, zero_table)

    def give_more(state):
        round_index, total = state
        wanted, rows, _ = serve(round_index)
        return round_index + 1, add_rows(trade(send_back(wanted)), rows, total)

    _, grad_embedding = lax.while_loop(more, give_more, (jnp.int32(1), grad_embedding))

    squared = squared + jnp.where(corner, squares(grad_embedding), 0.0)
    sum_attn, grad_embedding = lax.optimization_barrier((sum_attn, grad_embedding))
    (sum_attn,), squared = ring_sum([sum_attn], squared, groups, shards, 2, 256, 2)
    sum_small = sum_attn[-256:].reshape(-1)[:small_size].reshape(grad_small.shape)
    grad_norms = sum_small[:8]
    grad_bias_qv = lax.dynamic_slice_in_dim(sum_small[8:10], tp_rank * cols, cols, 1)
    grad_bias_up = lax.dynamic_slice_in_dim(sum_small[10:].reshape(-1), tp_rank * hidden, hidden)
    grad_attn = sum_attn[: 4 * width].reshape(4, width, cols)
    grad_ffn_up, grad_ffn_down = sum_up, sum_down
    grad_pos = sum_attn[4 * width : -256]

    grad_norm = jnp.sqrt(jnp.sum(squared))
    factor = jnp.minimum(1.0, CLIP_SCALE * math.sqrt(PARAMS) / (grad_norm + 1e-06))
    grad_positions = jnp.pad(grad_pos, ((2, positions.shape[0] - slots - 2), (0, 0)))
    grad_ffn = jnp.stack([grad_ffn_up, grad_ffn_down])
    new_embedding, next_embedding = advance(embedding, mom_embedding, grad_embedding, factor)
    new_positions, next_positions = advance(positions, mom_positions, grad_positions, factor)
    new_attn, next_attn = advance(attn_weights, mom_attn, grad_attn, factor)
    new_ffn, next_ffn = advance(ffn_weights, ffn_momentum, grad_ffn, factor)
    new_bias_qv, next_bias_qv = advance(bias_qv, mom_bias_qv, grad_bias_qv, factor)
    new_bias_up, next_bias_up = advance(bias_up, mom_bias_up, grad_bias_up, factor)
    new_norms, next_norms = advance(norms, mom_norms, grad_norms, factor)
    new_head_first, next_head_first = advance(head_first, mom_head_first, grad_head_first, factor)
    new_head_second, next_head_second = advance(head_second, mom_head_second, grad_head_second, factor)
    new_head_bias, next_head_bias = advance(head_bias, mom_head_bias, grad_head_bias, factor)
    return (
        new_embedding, new_positions, new_attn, new_ffn, new_bias_qv, new_bias_up, new_norms, new_head_first,
        new_head_second, new_head_bias, next_embedding, next_positions, next_attn, next_ffn, next_bias_qv,
        next_bias_up, next_norms, next_head_first, next_head_second, next_head_bias, loss, grad_norm,
    )


def solution(mesh):
    in_specs = (
        P("dp", None),
        P("dp"),
        P(),
        P("dp", "tensor"),
        P(None, "tensor"),
        P(None, None, "tensor"),
        P(None, None, "tensor"),
        P(None, "tensor"),
        P("tensor"),
        P(),
        P(),
        P(),
        P(),
        P("dp", "tensor"),
        P(None, "tensor"),
        P(None, None, "tensor"),
        P(None, None, "tensor"),
        P(None, "tensor"),
        P("tensor"),
        P(),
        P(),
        P(),
        P(),
    )
    out_specs = (
        P("dp", "tensor"),
        P(None, "tensor"),
        P(None, None, "tensor"),
        P(None, None, "tensor"),
        P(None, "tensor"),
        P("tensor"),
        P(),
        P(),
        P(),
        P(),
        P("dp", "tensor"),
        P(None, "tensor"),
        P(None, None, "tensor"),
        P(None, None, "tensor"),
        P(None, "tensor"),
        P("tensor"),
        P(),
        P(),
        P(),
        P(),
        P(),
        P(),
    )
    groups, shards = mesh.shape["dp"], mesh.shape["tensor"]

    def run(*arrays):
        body = on_device
        if 2 * (arrays[0].shape[0] // groups) == 3 * shards:
            body = functools.partial(fast_on_device, groups=groups, shards=shards)
        return jax.shard_map(
            body, mesh=mesh, in_specs=in_specs, out_specs=out_specs, check_vma=False
        )(*arrays)

    return run
```

```python
import functools
import math

import jax
import jax.numpy as jnp
from jax import lax
from jax.experimental import pallas as pl
from jax.experimental.pallas import tpu as pltpu
from jax.sharding import PartitionSpec as P

HEAD_DIM = 64
PARAMS = 65044736


EPS = 1e-05
SOFTMAX_TEMP = 0.1
DECAY = 0.9
RATE = 100000.0
CLIP_SCALE = 1e-06
HIGH = lax.Precision.HIGHEST
PRODUCT = lax.Precision.HIGH
CAPACITY = 88
SMALL_ROWS = 64


def precise_product(left, right):
    return jnp.matmul(left, right, precision=HIGH)


def norm_rows(values, gain, shift):
    center = values - jnp.mean(values, axis=-1, keepdims=True)
    spread = jnp.mean(center * center, axis=-1, keepdims=True)
    return center * lax.rsqrt(spread + EPS) * gain + shift


def attend(normed, lengths, attn, bias_qv):
    seqs, slots, width = normed.shape
    cols = attn.shape[2]
    heads = cols // HEAD_DIM
    queries = (precise_product(normed, attn[0]) + bias_qv[0]).reshape(seqs, slots, heads, HEAD_DIM)
    keys_all = precise_product(normed, attn[1]).reshape(seqs, slots, heads, HEAD_DIM)
    values = (precise_product(normed, attn[2]) + bias_qv[1]).reshape(seqs, slots, heads, HEAD_DIM)
    scores = jnp.einsum("sqhd,skhd->shqk", queries, keys_all, precision=HIGH) / math.sqrt(HEAD_DIM)
    valid = lax.broadcasted_iota(jnp.int32, (seqs, slots), 1) < lengths[:, None]
    scores = jnp.where(valid[:, None, None, :], scores, -1e30)
    probs = jax.nn.softmax(scores, axis=-1)
    mixed = jnp.einsum("shqk,skhd->sqhd", probs, values, precision=HIGH).reshape(seqs, slots, cols)
    return precise_product(mixed, attn[3].T)


def expand(normed, ffn, bias_up):
    hidden = jax.nn.gelu(precise_product(normed, ffn[0]) + bias_up, approximate=False)
    return precise_product(hidden, ffn[1].T)


def contrast(pooled, head_first, head_second, head_bias, partners):
    middle = jax.nn.gelu(precise_product(pooled, head_first) + head_bias, approximate=False)
    output = precise_product(middle, head_second)
    unit_vectors = output * lax.rsqrt(jnp.sum(output * output, axis=-1, keepdims=True) + 1e-06)
    similarity_scores = precise_product(unit_vectors, unit_vectors.T) / SOFTMAX_TEMP
    count = similarity_scores.shape[0]
    index = lax.broadcasted_iota(jnp.int32, (count,), 0)
    similarity_scores = jnp.where(index[:, None] == index[None, :], -1e30, similarity_scores)
    totals = jax.nn.logsumexp(similarity_scores, axis=-1)
    paired_rows = jnp.sum(
        jnp.where(index[None, :] == partners[:, None], similarity_scores, 0.0), axis=-1
    )
    return jnp.sum(totals - paired_rows)


def owner_rows(ids_part, base, vocab_rows):
    local_ids = ids_part - base
    inside = (local_ids >= 0) & (local_ids < vocab_rows)
    return jnp.where(inside, local_ids, vocab_rows)


def advance(weight, moment, grad, factor):
    clipped = factor * grad
    moment_new = DECAY * moment + (1.0 - DECAY) * clipped
    return (weight - RATE * (DECAY * moment_new + (1.0 - DECAY) * clipped), moment_new)


def squares(array):
    return jnp.sum(array * array)


def on_device(
    token_ids,
    lengths,
    partners,
    embedding,
    positions,
    attn_weights,
    ffn_weights,
    bias_qv,
    bias_up,
    norms,
    head_first,
    head_second,
    head_bias,
    mom_embedding,
    mom_positions,
    mom_attn,
    ffn_momentum,
    mom_bias_qv,
    mom_bias_up,
    mom_norms,
    mom_head_first,
    mom_head_second,
    mom_head_bias,
):
    seqs, slots = token_ids.shape
    vocab_rows, cols = embedding.shape
    dp_rank = lax.axis_index("dp")
    tp_rank = lax.axis_index("tensor")
    base = dp_rank * vocab_rows
    all_ids = lax.all_gather(token_ids, "dp", axis=0, tiled=True).reshape(-1)
    padded_table = jnp.concatenate([embedding, jnp.zeros((1, cols), jnp.float32)], axis=0)
    rows_ids = owner_rows(all_ids, base, vocab_rows)
    token_rows = lax.psum_scatter(
        jnp.take(padded_table, rows_ids, axis=0), "dp", scatter_dimension=0, tiled=True
    )
    token_cols = token_rows.reshape(seqs, slots, cols) + positions[2 : slots + 2][None]
    embedded = lax.all_gather(token_cols, "tensor", axis=2, tiled=True)
    h_zero, ln_zero_pull = jax.vjp(norm_rows, embedded, norms[0], norms[1])
    attn_part, attn_pull = jax.vjp(
        lambda normed, weights, biases: attend(normed, lengths, weights, biases),
        h_zero,
        attn_weights,
        bias_qv,
    )
    x_one = h_zero + lax.psum(attn_part, "tensor") + norms[6]
    h_one, ln_one_pull = jax.vjp(norm_rows, x_one, norms[2], norms[3])
    ffn_part, ffn_pull = jax.vjp(expand, h_one, ffn_weights, bias_up)
    x_two = h_one + lax.psum(ffn_part, "tensor") + norms[7]
    h_two, ln_two_pull = jax.vjp(norm_rows, x_two, norms[4], norms[5])
    valid = (lax.broadcasted_iota(jnp.int32, (seqs, slots), 1) < lengths[:, None]).astype(
        jnp.float32
    )
    len_float = lengths.astype(jnp.float32)
    pooled = jnp.sum(h_two * valid[:, :, None], axis=1) / len_float[:, None]
    all_pooled = lax.all_gather(pooled, "dp", axis=0, tiled=True)
    loss, head_pull = jax.vjp(
        lambda rows, first_w, second_w, bias_w: contrast(rows, first_w, second_w, bias_w, partners),
        all_pooled,
        head_first,
        head_second,
        head_bias,
    )
    back_pooled_all, grad_head_first, grad_head_second, grad_head_bias = head_pull(
        jnp.ones_like(loss)
    )
    back_pooled = lax.dynamic_slice_in_dim(back_pooled_all, dp_rank * seqs, seqs)
    back_h_two = valid[:, :, None] * (back_pooled / len_float[:, None])[:, None, :]
    back_x_two, grad_gain_two, grad_shift_two = ln_two_pull(back_h_two)
    back_h_one_part, grad_ffn, grad_bias_up = ffn_pull(back_x_two)
    back_h_one = back_x_two + lax.psum(back_h_one_part, "tensor")
    back_x_one, grad_gain_one, grad_shift_one = ln_one_pull(back_h_one)
    back_h_zero_part, grad_attn, grad_bias_qv = attn_pull(back_x_one)
    back_h_zero = back_x_one + lax.psum(back_h_zero_part, "tensor")
    back_embedded, grad_gain_zero, grad_shift_zero = ln_zero_pull(back_h_zero)
    back_cols = lax.dynamic_slice_in_dim(back_embedded, tp_rank * cols, cols, 2)
    grad_positions = jnp.pad(
        jnp.sum(back_cols, axis=0), ((2, positions.shape[0] - slots - 2), (0, 0))
    )
    grad_norms = jnp.stack(
        [
            grad_gain_zero,
            grad_shift_zero,
            grad_gain_one,
            grad_shift_one,
            grad_gain_two,
            grad_shift_two,
            jnp.sum(back_x_one, axis=(0, 1)),
            jnp.sum(back_x_two, axis=(0, 1)),
        ]
    )
    back_flat = back_cols.reshape(seqs * slots, cols)
    target = owner_rows(all_ids, base, vocab_rows)
    grad_embedding = jax.ops.segment_sum(
        lax.all_gather(back_flat, "dp", axis=0, tiled=True), target, num_segments=vocab_rows + 1
    )[:vocab_rows]
    first_dp = (dp_rank == 0).astype(jnp.float32)
    first_all = first_dp * (tp_rank == 0).astype(jnp.float32)
    grad_attn, grad_ffn, grad_positions, grad_bias_qv, grad_bias_up, grad_norms = lax.psum(
        (grad_attn, grad_ffn, grad_positions, grad_bias_qv, grad_bias_up, grad_norms), "dp"
    )
    big_squares = first_dp * (squares(grad_attn) + squares(grad_ffn))
    local_squares = (
        big_squares
        + squares(grad_embedding)
        + first_dp * (squares(grad_positions) + squares(grad_bias_qv) + squares(grad_bias_up))
        + first_all
        * (
            squares(grad_norms)
            + squares(grad_head_first)
            + squares(grad_head_second)
            + squares(grad_head_bias)
        )
    )
    total_squares = lax.psum(local_squares, ("dp", "tensor"))
    grad_norm = jnp.sqrt(total_squares)
    factor = jnp.minimum(1.0, CLIP_SCALE * math.sqrt(PARAMS) / (grad_norm + 1e-06))
    new_attn, next_attn = advance(attn_weights, mom_attn, grad_attn, factor)
    new_ffn, next_ffn = advance(ffn_weights, ffn_momentum, grad_ffn, factor)
    new_embedding, next_embedding = advance(embedding, mom_embedding, grad_embedding, factor)
    new_positions, next_positions = advance(positions, mom_positions, grad_positions, factor)
    new_bias_qv, next_bias_qv = advance(bias_qv, mom_bias_qv, grad_bias_qv, factor)
    new_bias_up, next_bias_up = advance(bias_up, mom_bias_up, grad_bias_up, factor)
    new_norms, next_norms = advance(norms, mom_norms, grad_norms, factor)
    new_head_first, next_head_first = advance(head_first, mom_head_first, grad_head_first, factor)
    new_head_second, next_head_second = advance(
        head_second, mom_head_second, grad_head_second, factor
    )
    new_head_bias, next_head_bias = advance(head_bias, mom_head_bias, grad_head_bias, factor)
    return (
        new_embedding,
        new_positions,
        new_attn,
        new_ffn,
        new_bias_qv,
        new_bias_up,
        new_norms,
        new_head_first,
        new_head_second,
        new_head_bias,
        next_embedding,
        next_positions,
        next_attn,
        next_ffn,
        next_bias_qv,
        next_bias_up,
        next_norms,
        next_head_first,
        next_head_second,
        next_head_bias,
        loss,
        grad_norm,
    )


MESH = pl.DeviceIdType.MESH
VMEM = pl.BlockSpec(memory_space=pltpu.VMEM)


def cube_partners(groups, shards):
    dp, tp = lax.axis_index("dp"), lax.axis_index("tensor")
    partners = []
    for size, at in ((shards, 1), (groups, 0)):
        bit = 1
        while bit < size:
            here = (dp, tp)[at]
            there = here + bit * (1 - 2 * ((here // bit) % 2))
            partners.append((dp, there) if at else (there, tp))
            bit *= 2
    return partners


def greet(partners):
    barrier = pltpu.get_barrier_semaphore()
    for partner in partners:
        pl.semaphore_signal(barrier, inc=1, device_id=partner, device_id_type=MESH)
    pl.semaphore_wait(barrier, len(partners))


def cube_stages(groups, shards):
    return (groups * shards).bit_length() - 1


def cube_gather_kernel(groups, shards, x_ref, o_ref, held, send_sem, recv_sem):
    partners = cube_partners(groups, shards)
    greet(partners)
    me = lax.axis_index("dp") * shards + lax.axis_index("tensor")
    held[pl.ds(me, 1)] = x_ref[...][None]
    for stage, partner in enumerate(partners):
        size = 1 << stage
        mine = pl.ds((me // size) * size, size)
        copy = pltpu.make_async_remote_copy(
            src_ref=held.at[mine],
            dst_ref=held.at[mine],
            send_sem=send_sem.at[stage],
            recv_sem=recv_sem.at[stage],
            device_id=partner,
            device_id_type=MESH,
        )
        copy.start()
        copy.wait()
    o_ref[...] = held[...]


def cube_gather(block, groups, shards, collective_id):
    stages = cube_stages(groups, shards)
    shape = (groups * shards, *block.shape)
    return pl.pallas_call(
        functools.partial(cube_gather_kernel, groups, shards),
        out_shape=jax.ShapeDtypeStruct(shape, block.dtype),
        in_specs=[VMEM],
        out_specs=VMEM,
        scratch_shapes=[
            pltpu.VMEM(shape, block.dtype),
            pltpu.SemaphoreType.DMA((stages,)),
            pltpu.SemaphoreType.DMA((stages,)),
        ],
        compiler_params=pltpu.CompilerParams(collective_id=collective_id, has_side_effects=True),
    )(block)


def fold_squares(block):
    block = block * block
    folded = jnp.sum(block.reshape(block.shape[0] // 8, 8, block.shape[1]), axis=0)
    total = folded[:, :128]
    for start in range(128, block.shape[1], 128):
        total = total + folded[:, start : start + 128]
    return total


def ring_kernel(groups, shards, parts, arrays, shared_rows, *refs):
    refs = list(refs)
    inputs = [refs.pop(0) for _ in range(arrays)]
    base = refs.pop(0)
    outputs = [refs.pop(0) for _ in range(arrays)]
    squares_ref = refs.pop(0)
    slots = [refs.pop(0) for _ in range(arrays)]
    send_sem, recv_sem, sent, landed, cube_send, cube_recv = refs
    depth = groups // 2
    dp, tp = lax.axis_index("dp"), lax.axis_index("tensor")
    side, level = dp % 2, dp // 2
    place = level * (1 - side) + (groups - 1 - level) * side

    def device_at(spot):
        spot = (spot + groups) % groups
        far = spot // depth
        return (2 * (spot * (1 - far) + (groups - 1 - spot) * far) + far, tp)

    partners = cube_partners(groups, shards) if shared_rows else []
    greet([device_at(place + 1), device_at(place - 1), *partners])
    streams = []
    for array in range(arrays):
        tiles = inputs[array].shape[1] // 8
        edges = [8 * (tiles * part // (2 * parts)) for part in range(2 * parts + 1)]
        for part in range(2 * parts):
            streams.append((array, 1 - 2 * (part % 2), edges[part], edges[part + 1] - edges[part]))

    def chunk(step, way):
        return (place + groups * 2 - way * step) % groups

    copies = []

    def send(source, target, send_at, recv_at, device):
        copy = pltpu.make_async_remote_copy(
            src_ref=source,
            dst_ref=target,
            send_sem=send_at,
            recv_sem=recv_at,
            device_id=device,
            device_id_type=MESH,
        )
        copy.start()
        copies.append(copy)
        return copy

    def pass_on(index, step, source, target):
        device = device_at(place + streams[index][1])
        return send(source, target, send_sem.at[index, step], recv_sem.at[index, step], device)

    flying = [None] * len(streams)
    for step in range(groups - 1):
        for index, (array, way, start, size) in enumerate(streams):
            rows = pl.ds(start, size)
            if step == 0:
                source = inputs[array].at[chunk(0, way), rows]
            else:
                flying[index].wait_recv()
                source = slots[array].at[step - 1, rows]
                source[...] = source[...] + inputs[array][chunk(step, way), rows]
            flying[index] = pass_on(index, step, source, slots[array].at[step, rows])
    total = base[...]
    crossing = None
    for step in range(groups - 1):
        for index, (array, way, start, size) in enumerate(streams):
            rows = pl.ds(start, size)
            flying[index].wait_recv()
            now = chunk(groups - 1 + step, way)
            if step == 0:
                block = slots[array][groups - 2, rows] + inputs[array][now, rows]
                outputs[array][now, rows] = block
                if shared_rows:
                    depth_rows = inputs[array].shape[1]
                    limit = groups * depth_rows - shared_rows * (1 - (shards - tp) // shards)
                    at = now * depth_rows + start + lax.broadcasted_iota(jnp.int32, block.shape, 0)
                    block = jnp.where(at < limit, block, 0.0)
                total = total + fold_squares(block)
            out = outputs[array].at[now, rows]
            flying[index] = pass_on(index, groups - 1 + step, out, out)
        if step <= len(partners) and partners:
            if step == 0:
                sent[0] = total
            else:
                crossing.wait_recv()
                sent[step] = sent[step - 1] + landed[step - 1]
            if step < len(partners):
                crossing = send(
                    sent.at[step], landed.at[step], cube_send.at[step], cube_recv.at[step], partners[step]
                )
    squares_ref[...] = sent[len(partners)] if partners else total
    for copy in flying:
        copy.wait_recv()
    for copy in copies:
        copy.wait_send()


def ring_sum(arrays, base, groups, shards, parts, shared_rows, collective_id):
    blocks = [array.reshape(groups, array.shape[0] // groups, array.shape[1]) for array in arrays]
    streams = 2 * parts * len(blocks)
    steps = 2 * (groups - 1)
    stages = cube_stages(groups, shards)
    *sums, squared = pl.pallas_call(
        functools.partial(ring_kernel, groups, shards, parts, len(blocks), shared_rows),
        out_shape=[jax.ShapeDtypeStruct(block.shape, block.dtype) for block in [*blocks, base]],
        in_specs=[VMEM] * (len(blocks) + 1),
        out_specs=[VMEM] * (len(blocks) + 1),
        scratch_shapes=[
            *[pltpu.VMEM((groups - 1, *block.shape[1:]), block.dtype) for block in blocks],
            pltpu.SemaphoreType.DMA((streams, steps)),
            pltpu.SemaphoreType.DMA((streams, steps)),
            pltpu.VMEM((stages + 1, *base.shape), base.dtype),
            pltpu.VMEM((stages, *base.shape), base.dtype),
            pltpu.SemaphoreType.DMA((stages,)),
            pltpu.SemaphoreType.DMA((stages,)),
        ],
        compiler_params=pltpu.CompilerParams(
            collective_id=collective_id, has_side_effects=True, vmem_limit_bytes=48 << 20
        ),
        cost_estimate=pl.CostEstimate(flops=1, bytes_accessed=1024, transcendentals=0),
    )(*blocks, base)
    return [total.reshape(array.shape) for total, array in zip(sums, arrays)], squared


def spread_kernel(
    groups, w_ref, small_ref, o_ref, rows_ref, local_sem, pair_send, pair_recv, ring_send, ring_recv, core_send, core_recv
):
    depth = groups // 2
    dp, tp = lax.axis_index("dp"), lax.axis_index("tensor")
    far = tp + 2 - 4 * (tp // 2)
    core = (dp, tp + 1 - 2 * (tp % 2))
    side, level = dp % 2, dp // 2
    place = level * (1 - side) + (groups - 1 - level) * side

    def index_at(spot):
        spot = (spot + groups) % groups
        back = spot // depth
        return 2 * (spot * (1 - back) + (groups - 1 - spot) * back) + back

    def send(source, target, send_sem, recv_sem, device):
        copy = pltpu.make_async_remote_copy(
            src_ref=source,
            dst_ref=target,
            send_sem=send_sem,
            recv_sem=recv_sem,
            device_id=device,
            device_id_type=MESH,
        )
        copy.start()
        return copy

    greet([(index_at(place + 1), tp), (index_at(place - 1), tp), core, (dp, far)])
    cross = send(w_ref.at[dp], o_ref.at[tp, dp], pair_send.at[0], pair_recv.at[0], (dp, far))
    near = send(w_ref, o_ref.at[tp], pair_send.at[1], pair_recv.at[1], core)
    cross_rows = send(small_ref, rows_ref.at[tp], pair_send.at[2], pair_recv.at[2], (dp, far))
    near_rows = send(small_ref, rows_ref.at[tp], pair_send.at[3], pair_recv.at[3], core)
    local = pltpu.make_async_copy(w_ref, o_ref.at[tp], local_sem)
    local.start()
    rows_ref[tp] = small_ref[...]
    cross.wait_recv()
    lanes = ring_send.shape[0]
    size = w_ref.shape[1] // lanes
    flying = [None] * lanes
    started = [cross, cross_rows]
    handed = [near, near_rows]
    for step in range(groups):
        for lane in range(lanes):
            way = 1 - 2 * (lane % 2)
            block = o_ref.at[far, index_at(place + groups - way * step), pl.ds(lane * size, size)]
            if step > 0:
                flying[lane].wait_recv()
            if step < groups - 1:
                flying[lane] = send(
                    block, block, ring_send.at[lane, step], ring_recv.at[lane, step], (index_at(place + way), tp)
                )
                started.append(flying[lane])
            handed.append(send(block, block, core_send.at[lane, step], core_recv.at[lane, step], core))
    cross_rows.wait_recv()
    handed.append(send(rows_ref.at[far], rows_ref.at[far], pair_send.at[4], pair_recv.at[4], core))
    for copy in handed:
        copy.wait_recv()
        copy.wait_send()
    for copy in started:
        copy.wait_send()
    local.wait()


def spread(weight, small, groups, collective_id):
    rows = weight.shape[0] // groups
    lanes = 4
    gathered, gathered_rows = pl.pallas_call(
        functools.partial(spread_kernel, groups),
        out_shape=[
            jax.ShapeDtypeStruct((4, groups, rows, weight.shape[1]), weight.dtype),
            jax.ShapeDtypeStruct((4, *small.shape), small.dtype),
        ],
        in_specs=[pl.BlockSpec(memory_space=pl.ANY), VMEM],
        out_specs=[VMEM, VMEM],
        scratch_shapes=[
            pltpu.SemaphoreType.DMA,
            pltpu.SemaphoreType.DMA((5,)),
            pltpu.SemaphoreType.DMA((5,)),
            pltpu.SemaphoreType.DMA((lanes, groups - 1)),
            pltpu.SemaphoreType.DMA((lanes, groups - 1)),
            pltpu.SemaphoreType.DMA((lanes, groups)),
            pltpu.SemaphoreType.DMA((lanes, groups)),
        ],
        compiler_params=pltpu.CompilerParams(
            collective_id=collective_id, has_side_effects=True, vmem_limit_bytes=32 << 20
        ),
        cost_estimate=pl.CostEstimate(flops=1, bytes_accessed=1024, transcendentals=0),
    )(weight.reshape(groups, rows, weight.shape[1]), small)
    return gathered.reshape(4, *weight.shape), gathered_rows


def halves(array):
    high = array.astype(jnp.bfloat16)
    return high, (array - high.astype(jnp.float32)).astype(jnp.bfloat16)


def dot_rows(left, right):
    return lax.dot_general(left, right, (((1,), (1,)), ((), ())), preferred_element_type=jnp.float32)


def dot_plain(left, right):
    return lax.dot_general(left, right, (((1,), (0,)), ((), ())), preferred_element_type=jnp.float32)


def one_head(array, head):
    lane = lax.broadcasted_iota(jnp.int32, array.shape, 1)
    return jnp.where(lane // HEAD_DIM == head, array, 0.0)


def score_tile(twice_k, low_k, high_q, low_q, bias):
    wide = dot_rows(twice_k, jnp.concatenate([high_q, low_q], axis=1))
    return wide + dot_rows(low_k, high_q) + bias


def attend_kernel(slots, tile, q_ref, k_ref, v_ref, bias_ref, o_ref, lse_ref):
    scale = 1.0 / math.sqrt(HEAD_DIM)
    high_k, low_k = halves(k_ref[0])
    twice_k = jnp.concatenate([high_k, high_k], axis=1)
    high_v, low_v = halves(v_ref[0].T)
    def scores_of(start):
        first = 0 if start < slots else slots
        keys = slice(first, first + slots)
        found = []
        for head in range(2):
            high_q, low_q = halves(one_head(q_ref[0, pl.ds(start, tile)] * scale, head))
            found.append(score_tile(twice_k[keys], low_k[keys], high_q, low_q, bias_ref[pl.ds(first, slots)]))
        return found

    starts = list(range(0, q_ref.shape[1], tile))
    ready = scores_of(starts[0])
    for index, start in enumerate(starts):
        rows = pl.ds(start, tile)
        first = 0 if start < slots else slots
        keys = slice(first, first + slots)
        score_pair = ready
        if index + 1 < len(starts):
            ready = scores_of(starts[index + 1])
        peaks = [jnp.max(jnp.max(s.reshape(8, -1, tile), axis=0), axis=0, keepdims=True) for s in score_pair]
        pairs = [jnp.exp(s - p) for s, p in zip(score_pair, peaks)]
        found = []
        for head in range(2):
            peak, probs = peaks[head], pairs[head]
            total = jnp.sum(jnp.sum(probs.reshape(8, -1, tile), axis=0), axis=0, keepdims=True)
            lse_ref[0, pl.ds(head, 1), rows] = peak + jnp.log(total)
            high_p, low_p = halves(probs)
            lanes = slice(head * HEAD_DIM, (head + 1) * HEAD_DIM)
            both = jnp.concatenate([high_v[lanes, keys], low_v[lanes, keys]], axis=0)
            wide = dot_plain(both, high_p)
            mixed = wide[:HEAD_DIM] + wide[HEAD_DIM:] + dot_plain(high_v[lanes, keys], low_p)
            found.append(mixed / total)
        o_ref[0, rows] = jnp.concatenate(found, axis=0).T


def attend_back_kernel(slots, tile, q_ref, k_ref, v_ref, bias_ref, o_ref, lse_ref, d_ref, dq_ref, dk_ref, dv_ref):
    scale = 1.0 / math.sqrt(HEAD_DIM)
    high_k, low_k = halves(k_ref[0])
    twice_k = jnp.concatenate([high_k, high_k], axis=1)
    high_v, low_v = halves(v_ref[0])
    twice_v = jnp.concatenate([high_v, high_v], axis=1)
    high_kt, low_kt = halves(k_ref[0].T)
    ones = jnp.ones((8, 2 * HEAD_DIM), jnp.bfloat16)
    lanes = 2 * HEAD_DIM
    for first in (0, slots):
        keys = slice(first, first + slots)
        key_rows = pl.ds(first, slots)
        for start in range(first, min(first + slots, q_ref.shape[1]), tile):
            rows = pl.ds(start, tile)
            back_qt = []
            for head in range(2):
                high_q, low_q = halves(one_head(q_ref[0, rows] * scale, head))
                back = one_head(d_ref[0, rows], head)
                high_d, low_d = halves(back)
                scores = score_tile(twice_k[keys], low_k[keys], high_q, low_q, bias_ref[key_rows])
                probs = jnp.exp(scores - lse_ref[0, pl.ds(head, 1), rows])
                high_x, low_x = halves(back * o_ref[0, rows])
                inner = (dot_rows(ones, high_x) + dot_rows(ones, low_x))[:1]
                back_s = probs * (score_tile(twice_v[keys], low_v[keys], high_d, low_d, 0.0) - inner)
                high_p, low_p = halves(probs)
                high_s, low_s = halves(back_s)
                wide = dot_plain(high_p, jnp.concatenate([high_d, low_d], axis=1))
                back_v = wide[:, :lanes] + wide[:, lanes:] + dot_plain(low_p, high_d)
                wide = dot_plain(high_s, jnp.concatenate([high_q, low_q], axis=1))
                back_k = wide[:, :lanes] + wide[:, lanes:] + dot_plain(low_s, high_q)
                if start == first and head == 0:
                    dv_ref[0, key_rows] = back_v
                    dk_ref[0, key_rows] = back_k
                else:
                    dv_ref[0, key_rows] += back_v
                    dk_ref[0, key_rows] += back_k
                mine = slice(head * HEAD_DIM, (head + 1) * HEAD_DIM)
                both = jnp.concatenate([high_kt[mine, keys], low_kt[mine, keys]], axis=0)
                wide = dot_plain(both, high_s)
                back_qt.append(wide[:HEAD_DIM] + wide[HEAD_DIM:] + dot_plain(high_kt[mine, keys], low_s))
            dq_ref[0, rows] = jnp.concatenate(back_qt, axis=0).T * scale


def attend_call(kernel, slots, inputs, outputs):
    lanes = 2 * HEAD_DIM
    queries = inputs[0]
    per_shard = queries.shape[2] // lanes
    pairs = queries.shape[0] * per_shard

    def spec(shape):
        if shape[1] == 1:
            return pl.BlockSpec(shape, lambda i: (0, 0))
        if shape[1] == 2:
            return pl.BlockSpec((1, *shape[1:]), lambda i: (i, 0, 0))
        return pl.BlockSpec((1, shape[1], lanes), lambda i: (i // per_shard, 0, i % per_shard))

    work = 7 * 2 * pairs * 2 * queries.shape[1] * slots * HEAD_DIM * 3
    return pl.pallas_call(
        functools.partial(kernel, slots, slots // 2),
        grid=(pairs,),
        in_specs=[spec(x.shape) for x in inputs],
        out_specs=[spec(shape) for shape in outputs],
        out_shape=[jax.ShapeDtypeStruct(shape, jnp.float32) for shape in outputs],
        compiler_params=pltpu.CompilerParams(vmem_limit_bytes=48 << 20),
        cost_estimate=pl.CostEstimate(flops=4 * work, bytes_accessed=20 << 20, transcendentals=0),
    )(*inputs)


WIDE = 512


def dot_three(high_left, low_left, right, dot):
    high, low = halves(right)
    return dot(high_left, high) + dot(high_left, low) + dot(low_left, high)


def times_kernel(finish, extras, x_ref, w_ref, *refs):
    more, outs, (high, low) = refs[:extras], refs[extras:-2], refs[-2:]

    @pl.when((pl.program_id(0) == 0) & (pl.program_id(1) == 0))
    def _():
        high[...], low[...] = halves(x_ref[...])

    weight = w_ref[...].reshape(w_ref.shape[-2], w_ref.shape[-1])
    finish(dot_three(high[...], low[...], weight, dot_plain), more, outs)


def times(x, w, which, finish, extras, outs):
    shards, depth, columns = w.shape[0], w.shape[-2], w.shape[-1]
    rows, wide = x.shape[0], min(WIDE, columns)
    if w.ndim == 4:
        w_spec = pl.BlockSpec((1, 1, depth, wide), lambda j, c: (j, which, 0, c))
    else:
        w_spec = pl.BlockSpec((1, depth, wide), lambda j, c: (j, 0, c))

    def spec(shape):
        return pl.BlockSpec((1, shape[1], wide), lambda j, c: (j, 0, c))

    results = pl.pallas_call(
        functools.partial(times_kernel, finish, len(extras)),
        grid=(shards, columns // wide),
        in_specs=[pl.BlockSpec((rows, depth), lambda j, c: (0, 0)), w_spec, *[spec(e.shape) for e in extras]],
        out_specs=[spec(shape) for shape in outs],
        out_shape=[jax.ShapeDtypeStruct(shape, jnp.float32) for shape in outs],
        scratch_shapes=[pltpu.VMEM((rows, depth), jnp.bfloat16)] * 2,
        compiler_params=pltpu.CompilerParams(vmem_limit_bytes=48 << 20),
        cost_estimate=pl.CostEstimate(
            flops=6 * rows * depth * shards * columns, bytes_accessed=4 * w.size, transcendentals=0
        ),
    )(x, w, *extras)
    return results


def keep_tile(tile, more, outs):
    outs[0][0] = tile


def add_row(tile, more, outs):
    outs[0][0] = tile + more[0][0]


def gelu_tile(tile, more, outs):
    outs[0][0], outs[1][0] = gelu_both(tile + more[0][0])


def scale_tile(tile, more, outs):
    tile = tile * more[0][0]
    outs[0][0] = tile
    outs[1][0] = jnp.sum(tile, axis=0, keepdims=True)


def project_kernel(count, x_ref, y_ref, wq_ref, wk_ref, wv_ref, bq_ref, bv_ref, q_ref, k_ref, v_ref, high, low):
    @pl.when(pl.program_id(0) == 0)
    def _():
        high[:count], low[:count] = halves(x_ref[...])
        high[count:], low[count:] = halves(y_ref[...])

    q_ref[0] = dot_three(high[:count], low[:count], wq_ref[0, 0], dot_plain) + bq_ref[0]
    k_ref[0] = dot_three(high[...], low[...], wk_ref[0, 0], dot_plain)
    v_ref[0] = dot_three(high[...], low[...], wv_ref[0, 0], dot_plain) + bv_ref[0]


def project(x, y, w, bias_q, bias_v):
    count, depth = x.shape
    rows = count + y.shape[0]
    shards, _, _, columns = w.shape

    def weight(which):
        return pl.BlockSpec((1, 1, depth, columns), lambda j: (j, which, 0, 0))

    def tile(height):
        return pl.BlockSpec((1, height, columns), lambda j: (j, 0, 0))

    return pl.pallas_call(
        functools.partial(project_kernel, count),
        grid=(shards,),
        in_specs=[
            pl.BlockSpec(x.shape, lambda j: (0, 0)),
            pl.BlockSpec(y.shape, lambda j: (0, 0)),
            *[weight(which) for which in range(3)],
            tile(1),
            tile(1),
        ],
        out_specs=[tile(count), tile(rows), tile(rows)],
        out_shape=[jax.ShapeDtypeStruct((shards, n, columns), jnp.float32) for n in (count, rows, rows)],
        scratch_shapes=[pltpu.VMEM((rows, depth), jnp.bfloat16)] * 2,
        compiler_params=pltpu.CompilerParams(vmem_limit_bytes=48 << 20),
        cost_estimate=pl.CostEstimate(
            flops=6 * (count + 2 * rows) * depth * shards * columns, bytes_accessed=24 << 20, transcendentals=0
        ),
    )(x, y, w, w, w, bias_q, bias_v)


def gather_back_kernel(count, base_ref, *refs):
    out = refs[-1]

    @pl.when((pl.program_id(0) == 0) & (pl.program_id(1) == 0))
    def _():
        filled = base_ref.shape[0]
        out[:filled] = base_ref[...]
        if filled < out.shape[0]:
            out[filled:] = jnp.zeros((out.shape[0] - filled, out.shape[1]), jnp.float32)

    for a_ref, w_ref in zip(refs[:count], refs[count : 2 * count]):
        high, low = halves(a_ref[0])
        weight = w_ref[...].reshape(w_ref.shape[-2], w_ref.shape[-1])
        rows = pl.ds(0, a_ref.shape[1])
        out[rows] += dot_three(high, low, weight, dot_rows)


def gather_back(base, terms):
    arrays = [array for array, _, _ in terms]
    shards, _, columns = arrays[0].shape
    wide = min(WIDE, columns)
    total = (max(array.shape[1] for array in arrays), base.shape[1])

    def w_spec(w, which):
        if w.ndim == 4:
            return pl.BlockSpec((1, 1, w.shape[-2], wide), lambda j, c: (j, which, 0, c))
        return pl.BlockSpec((1, w.shape[-2], wide), lambda j, c: (j, 0, c))

    work = sum(6 * array.size * w.shape[-2] for array, w, _ in terms)
    return pl.pallas_call(
        functools.partial(gather_back_kernel, len(terms)),
        grid=(shards, columns // wide),
        in_specs=[
            pl.BlockSpec(base.shape, lambda j, c: (0, 0)),
            *[pl.BlockSpec((1, a.shape[1], wide), lambda j, c: (j, 0, c)) for a in arrays],
            *[w_spec(w, which) for _, w, which in terms],
        ],
        out_specs=pl.BlockSpec(total, lambda j, c: (0, 0)),
        out_shape=jax.ShapeDtypeStruct(total, jnp.float32),
        compiler_params=pltpu.CompilerParams(vmem_limit_bytes=48 << 20),
        cost_estimate=pl.CostEstimate(flops=work, bytes_accessed=16 << 20, transcendentals=0),
    )(base, *arrays, *[w for _, w, _ in terms])


def outer_kernel(x_ref, d_ref, *refs):
    out, high, low = refs[-3:]

    @pl.when((pl.program_id(0) == 0) & (pl.program_id(1) == 0))
    def _():
        high[...], low[...] = halves(x_ref[...].T)

    out[0] = dot_three(high[...], low[...], d_ref[0], dot_plain)


def outer(x, d, rows, at, into=None):
    tokens, depth = x.shape
    shards, _, columns = d.shape
    wide = min(WIDE, columns)
    held = [] if into is None else [into]
    return pl.pallas_call(
        outer_kernel,
        grid=(shards, columns // wide),
        in_specs=[
            pl.BlockSpec((tokens, depth), lambda j, c: (0, 0)),
            pl.BlockSpec((1, tokens, wide), lambda j, c: (j, 0, c)),
            *[pl.BlockSpec(memory_space=pl.ANY) for _ in held],
        ],
        out_specs=pl.BlockSpec((1, depth, wide), lambda j, c: (j, at, c)),
        out_shape=jax.ShapeDtypeStruct((shards, rows, columns), jnp.float32),
        scratch_shapes=[pltpu.VMEM((depth, tokens), jnp.bfloat16)] * 2,
        input_output_aliases={2: 0} if held else {},
        compiler_params=pltpu.CompilerParams(vmem_limit_bytes=48 << 20),
        cost_estimate=pl.CostEstimate(
            flops=6 * tokens * depth * shards * columns, bytes_accessed=4 * shards * depth * columns, transcendentals=0
        ),
    )(x, d, *held)


def outer_three_kernel(count, x_ref, y_ref, q_ref, k_ref, v_ref, out, high, low):
    @pl.when(pl.program_id(0) == 0)
    def _():
        high[:, :count], low[:, :count] = halves(x_ref[...].T)
        high[:, count:], low[:, count:] = halves(y_ref[...].T)

    depth = high.shape[0]
    out[0, pl.ds(0, depth)] = dot_three(high[:, :count], low[:, :count], q_ref[0], dot_plain)
    out[0, pl.ds(depth, depth)] = dot_three(high[...], low[...], k_ref[0], dot_plain)
    out[0, pl.ds(2 * depth, depth)] = dot_three(high[...], low[...], v_ref[0], dot_plain)


def outer_three(x, y, back_q, back_k, back_v, rows):
    shards, tokens, columns = back_k.shape
    count, depth = x.shape

    def tile(height):
        return pl.BlockSpec((1, height, columns), lambda j: (j, 0, 0))

    return pl.pallas_call(
        functools.partial(outer_three_kernel, count),
        grid=(shards,),
        in_specs=[
            pl.BlockSpec(x.shape, lambda j: (0, 0)),
            pl.BlockSpec(y.shape, lambda j: (0, 0)),
            tile(count),
            tile(tokens),
            tile(tokens),
        ],
        out_specs=tile(3 * depth),
        out_shape=jax.ShapeDtypeStruct((shards, rows, columns), jnp.float32),
        scratch_shapes=[pltpu.VMEM((depth, tokens), jnp.bfloat16)] * 2,
        compiler_params=pltpu.CompilerParams(vmem_limit_bytes=48 << 20),
        cost_estimate=pl.CostEstimate(
            flops=6 * (count + 2 * tokens) * depth * shards * columns, bytes_accessed=24 << 20, transcendentals=0
        ),
    )(x, y, back_q, back_k, back_v)


def thirds(array):
    high, rest = array.astype(jnp.bfloat16), None
    rest = array - high.astype(jnp.float32)
    middle = rest.astype(jnp.bfloat16)
    return high, middle, (rest - middle.astype(jnp.float32)).astype(jnp.bfloat16)


def select_rows(column, row, block):
    chosen = jnp.where(column == row, 1.0, 0.0).astype(jnp.bfloat16)
    high, middle, low = thirds(block)
    return dot_plain(chosen, high) + dot_plain(chosen, middle) + dot_plain(chosen, low)


def pack_kernel(wanted_ref, ids_ref, x_ref, o_ref):
    o_ref[...] = select_rows(wanted_ref[...], ids_ref[...], x_ref[...]).reshape(o_ref.shape)


def pack(wanted, ids, rows, groups, shards):
    cols = rows.shape[1] // shards
    return pl.pallas_call(
        pack_kernel,
        grid=(shards,),
        in_specs=[
            pl.BlockSpec((wanted.shape[0], 1), lambda j: (0, 0)),
            pl.BlockSpec((1, ids.shape[0]), lambda j: (0, 0)),
            pl.BlockSpec((ids.shape[0], cols), lambda j: (0, j)),
        ],
        out_specs=pl.BlockSpec((groups, 1, CAPACITY, cols), lambda j: (0, j, 0, 0)),
        out_shape=jax.ShapeDtypeStruct((groups, shards, CAPACITY, cols), jnp.float32),
        compiler_params=pltpu.CompilerParams(vmem_limit_bytes=32 << 20),
    )(wanted[:, None], ids[None, :], rows)


def expand_kernel(ids_ref, wanted_ref, x_ref, o_ref):
    block = x_ref[...].reshape(wanted_ref.shape[1], x_ref.shape[-1])
    o_ref[...] = select_rows(ids_ref[...], wanted_ref[...], block)


def expand_rows(ids, wanted, landed):
    groups, shards, _, cols = landed.shape
    return pl.pallas_call(
        expand_kernel,
        grid=(shards,),
        in_specs=[
            pl.BlockSpec((ids.shape[0], 1), lambda j: (0, 0)),
            pl.BlockSpec((1, wanted.shape[0]), lambda j: (0, 0)),
            pl.BlockSpec((groups, 1, CAPACITY, cols), lambda j: (0, j, 0, 0)),
        ],
        out_specs=pl.BlockSpec((ids.shape[0], cols), lambda j: (0, j)),
        out_shape=jax.ShapeDtypeStruct((ids.shape[0], shards * cols), jnp.float32),
        compiler_params=pltpu.CompilerParams(vmem_limit_bytes=32 << 20),
    )(ids[:, None], wanted[None, :], landed)


def normalise(values):
    center = values - jnp.mean(values, axis=-1, keepdims=True)
    scale = lax.rsqrt(jnp.mean(center * center, axis=-1, keepdims=True) + EPS)
    return center * scale, scale


def normalise_back(back, gain, unit, scale):
    inner = back * gain
    grad = scale * (
        inner
        - jnp.mean(inner, axis=-1, keepdims=True)
        - unit * jnp.mean(inner * unit, axis=-1, keepdims=True)
    )
    return grad, jnp.sum(back * unit, axis=0), jnp.sum(back, axis=0)


def gelu_both(values):
    cdf = 0.5 * (1.0 + lax.erf(values * math.sqrt(0.5)))
    pdf = jnp.exp(-0.5 * values * values) * (1.0 / math.sqrt(2.0 * math.pi))
    return values * cdf, cdf + values * pdf


def product(subscripts, left, right):
    return jnp.einsum(subscripts, left, right, precision=PRODUCT)


def request_lists(ids, vocab_rows, owners):
    count = ids.shape[0]
    index = lax.broadcasted_iota(jnp.int32, (count,), 0)
    earlier = index[None, :] < index[:, None]
    same = (ids[None, :] == ids[:, None]) & earlier
    first = jnp.logical_not(jnp.any(same, axis=1))
    owner = ids // vocab_rows
    ahead = (owner[None, :] == owner[:, None]) & earlier & first[None, :]
    rank = jnp.sum(ahead.astype(jnp.int32), axis=1)
    return owner, jnp.where(first, rank, -1)


def round_list(ids, owner, rank, round_index, owners):
    place = rank - round_index * CAPACITY
    inside = (rank >= 0) & (place >= 0) & (place < CAPACITY)
    place = jnp.where(inside, owner * CAPACITY + place, -1)
    wanted = lax.broadcasted_iota(jnp.int32, (owners * CAPACITY, 1), 0)
    return jnp.sum(jnp.where(place[None, :] == wanted, ids[None, :] + 1, 0), axis=1) - 1


def trade(block):
    return lax.all_to_all(block, ("dp", "tensor"), 0, 0, tiled=True)


def fast_on_device(
    token_ids, lengths, partners, embedding, positions, attn_weights, ffn_weights, bias_qv, bias_up, norms,
    head_first, head_second, head_bias, mom_embedding, mom_positions, mom_attn, ffn_momentum, mom_bias_qv,
    mom_bias_up, mom_norms, mom_head_first, mom_head_second, mom_head_bias, *, groups, shards
):
    seqs, slots = token_ids.shape
    half = slots // 2
    vocab_rows, cols = embedding.shape
    width = cols * shards
    devices = groups * shards
    hidden = bias_up.shape[0]
    heads = width // HEAD_DIM
    dp_rank = lax.axis_index("dp")
    tp_rank = lax.axis_index("tensor")
    pair = tp_rank // 2
    side = tp_rank % 2
    base = dp_rank * vocab_rows

    whole_seq = 3 * pair + 2 * side
    split_seq = 3 * pair + 1
    whole_ids = lax.dynamic_index_in_dim(token_ids, whole_seq, 0, keepdims=False)
    split_ids = lax.dynamic_index_in_dim(token_ids, split_seq, 0, keepdims=False)
    ids = jnp.concatenate([whole_ids, lax.dynamic_slice_in_dim(split_ids, side * half, half)])
    count = ids.shape[0]
    whole_length = lax.dynamic_index_in_dim(lengths, whole_seq, 0, keepdims=False)
    split_length = lax.dynamic_index_in_dim(lengths, split_seq, 0, keepdims=False)

    all_attn = lax.all_gather(attn_weights, "tensor")
    parts_shape = (shards, count, hidden)
    all_ffn_down = lax.all_gather(ffn_weights[1], "tensor")
    small = jnp.concatenate([positions[2 : slots + 2], bias_qv, bias_up.reshape(-1, cols)], axis=0)
    small = jnp.pad(small, ((0, -small.shape[0] % 8), (0, 0)))
    swap = [(i, i ^ 1) for i in range(shards)]
    owner, rank = request_lists(ids, vocab_rows, groups)
    rounds_here = jnp.max(rank) // CAPACITY + 1

    def serve(round_index):
        wanted = round_list(ids, owner, rank, round_index, groups)
        lists = jnp.broadcast_to(wanted.reshape(groups, 1, CAPACITY), (groups, shards, CAPACITY))
        lists = lists.reshape(devices, CAPACITY)
        tail = jnp.broadcast_to(rounds_here, (devices, 1)).astype(jnp.int32)
        lists = jnp.concatenate([lists, tail, jnp.zeros((devices, 127 - CAPACITY), jnp.int32)], axis=1)
        asked = trade(lists)
        rows = asked[:, :CAPACITY].reshape(-1) - base
        rounds = jnp.max(asked[:, CAPACITY])
        return wanted, rows, rounds

    def find(rows):
        return jnp.take(embedding, rows, axis=0, mode="clip")

    def expand(wanted, landed):
        return expand_rows(ids, wanted, landed.reshape(groups, shards, CAPACITY, cols))

    wanted_first, rows_first, rounds = serve(0)
    found, up_weights = lax.optimization_barrier((find(rows_first), ffn_weights[0]))
    all_ffn_up, all_small = spread(up_weights, small, groups, 6)
    landed, all_small = lax.optimization_barrier((trade(found), all_small))
    all_positions = all_small[:, :slots].transpose(1, 0, 2).reshape(slots, width)
    all_bias_up = all_small[:, slots + 2 : slots + 2 + hidden // cols].reshape(-1)
    tokens = expand(wanted_first, landed)

    def more(state):
        return state[0] < rounds

    def fetch_more(state):
        round_index, total = state
        wanted, rows, _ = serve(round_index)
        return round_index + 1, total + expand(wanted, trade(find(rows)))

    _, tokens = lax.while_loop(more, fetch_more, (jnp.int32(1), tokens))
    own_positions = jnp.concatenate(
        [all_positions, lax.dynamic_slice_in_dim(all_positions, side * half, half)], axis=0
    )
    embedded = tokens + own_positions
    unit_zero, scale_zero = normalise(embedded)
    h_zero = unit_zero * norms[0] + norms[1]

    h_other = lax.ppermute(h_zero[slots:], "tensor", swap)
    bias_q, bias_v = all_small[:, slots], all_small[:, slots + 1]
    queries, keys_all, values = project(h_zero, h_other, all_attn, bias_q[:, None, :], bias_v[:, None, :])
    key_index = lax.broadcasted_iota(jnp.int32, (slots,), 0)
    own_first = jnp.where(
        key_index < half, side * half + key_index, (1 - side) * half + key_index - half
    )
    counted = jnp.concatenate([key_index < whole_length, own_first < split_length])
    key_bias = jnp.where(counted, 0.0, -1e30).astype(jnp.float32)[:, None]
    mixed, lse = attend_call(
        attend_kernel,
        slots,
        (queries, keys_all, values, key_bias),
        (queries.shape, (heads // 2, 2, count)),
    )
    x_one = gather_back(h_zero + norms[6], [(mixed, all_attn, 3)])
    unit_one, scale_one = normalise(x_one)
    h_one = unit_one * norms[2] + norms[3]

    bias_tiles = all_bias_up.reshape(shards, 1, hidden)
    act, act_slope = times(h_one, all_ffn_up, 0, gelu_tile, [bias_tiles], [parts_shape, parts_shape])
    x_two = gather_back(h_one + norms[7], [(act, all_ffn_down, 0)])
    unit_two, scale_two = normalise(x_two)
    h_two = unit_two * norms[4] + norms[5]

    slot = lax.broadcasted_iota(jnp.int32, (count,), 0)
    in_whole = slot < slots
    place = jnp.where(in_whole, slot, slot - slots + side * half)
    keep = place < jnp.where(in_whole, whole_length, split_length)
    weight_whole = jnp.where(keep & in_whole, 1.0 / whole_length.astype(jnp.float32), 0.0)
    weight_split = jnp.where(keep & ~in_whole, 1.0 / split_length.astype(jnp.float32), 0.0)
    sums = jnp.stack(
        [jnp.sum(h_two * weight_whole[:, None], axis=0), jnp.sum(h_two * weight_split[:, None], axis=0)]
    )
    all_sums = cube_gather(sums.reshape(-1, 128), groups, shards, 5).reshape(groups * shards // 2, 2, 2, width)
    all_pooled = jnp.stack(
        [all_sums[:, 0, 0], all_sums[:, 0, 1] + all_sums[:, 1, 1], all_sums[:, 1, 0]], axis=1
    ).reshape(groups * seqs, width)
    loss, head_pull = jax.vjp(
        lambda rows, first_w, second_w, bias_w: contrast(rows, first_w, second_w, bias_w, partners),
        all_pooled,
        head_first,
        head_second,
        head_bias,
    )
    back_pooled, grad_head_first, grad_head_second, grad_head_bias = head_pull(jnp.ones_like(loss))
    first_row = dp_rank * seqs
    back_whole = lax.dynamic_index_in_dim(back_pooled, first_row + whole_seq, 0, keepdims=False)
    back_split = lax.dynamic_index_in_dim(back_pooled, first_row + split_seq, 0, keepdims=False)
    back_h_two = weight_whole[:, None] * back_whole[None, :] + weight_split[:, None] * back_split[None, :]

    back_x_two, grad_gain_two, grad_shift_two = normalise_back(back_h_two, norms[4], unit_two, scale_two)
    grad_down = outer(back_x_two, act, width, 0)
    sum_down = lax.psum_scatter(grad_down, "tensor", scatter_dimension=0, tiled=False)
    back_up, grad_bias_up = times(
        back_x_two, all_ffn_down, 0, scale_tile, [act_slope], [parts_shape, bias_tiles.shape]
    )
    grad_up = outer(h_one, back_up, width, 0)
    back_up, grad_up = lax.optimization_barrier((back_up, grad_up))
    sum_up = lax.psum_scatter(grad_up, "tensor", scatter_dimension=0, tiled=False)
    back_h_one = gather_back(back_x_two, [(back_up, all_ffn_up, 0)])
    back_x_one, grad_gain_one, grad_shift_one = normalise_back(back_h_one, norms[2], unit_one, scale_one)

    (back_mixed,) = times(back_x_one, all_attn, 3, keep_tile, [], [mixed.shape])
    back_q, back_k, back_v = attend_call(
        attend_back_kernel,
        slots,
        (queries, keys_all, values, key_bias, mixed, lse, back_mixed),
        (queries.shape, keys_all.shape, values.shape),
    )
    back_keys = gather_back(
        back_x_one, [(back_q, all_attn, 0), (back_k, all_attn, 1), (back_v, all_attn, 2)]
    )
    back_other = lax.ppermute(back_keys[count:], "tensor", swap)
    back_h_zero = back_keys[:count]
    back_h_zero = back_h_zero + jnp.pad(back_other, ((slots, 0), (0, 0)))
    back_embedded, grad_gain_zero, grad_shift_zero = normalise_back(back_h_zero, norms[0], unit_zero, scale_zero)

    def send_back(wanted):
        return pack(wanted, ids, back_embedded, groups, shards).reshape(devices * CAPACITY, cols)

    def add_rows(landed, rows, total):
        target = jnp.where(rows >= 0, rows, vocab_rows)
        return total.at[target].add(landed, mode="drop")

    leaving, back_q, back_k, back_v, back_x_one = lax.optimization_barrier(
        (send_back(wanted_first), back_q, back_k, back_v, back_x_one)
    )
    landed_first = trade(leaving)
    part_rows = 4 * width + slots + SMALL_ROWS
    parts_attn = outer_three(h_zero, h_other, back_q, back_k, back_v, part_rows)
    parts_attn = outer(back_x_one, mixed, part_rows, 3, parts_attn)
    grad_small = jnp.concatenate(
        [
            jnp.stack(
                [
                    grad_gain_zero,
                    grad_shift_zero,
                    grad_gain_one,
                    grad_shift_one,
                    grad_gain_two,
                    grad_shift_two,
                    jnp.sum(back_x_one, axis=0),
                    jnp.sum(back_x_two, axis=0),
                    jnp.sum(back_q, axis=1).reshape(-1),
                    jnp.sum(back_v, axis=1).reshape(-1),
                ]
            ),
            grad_bias_up.reshape(-1, width),
        ],
        axis=0,
    )
    half_rows = jnp.where(side == 0, 1.0, 0.0) * back_embedded[slots:]
    other_rows = back_embedded[slots:] - half_rows
    grad_pos_full = back_embedded[:slots] + jnp.concatenate([half_rows, other_rows], axis=0)
    grad_pos_parts = grad_pos_full.reshape(slots, shards, cols)
    grad_pos_parts = grad_pos_parts.transpose(1, 0, 2)
    small_size = grad_small.size
    small_rows = jnp.pad(grad_small.reshape(-1), (0, SMALL_ROWS * cols - small_size)).reshape(1, SMALL_ROWS, cols)
    small_rows = jnp.broadcast_to(small_rows, (shards, SMALL_ROWS, cols))
    parts_attn = lax.dynamic_update_slice(parts_attn, grad_pos_parts, (0, 4 * width, 0))
    parts_attn = lax.dynamic_update_slice(parts_attn, small_rows, (0, 4 * width + slots, 0))
    landed_first, parts_attn = lax.optimization_barrier((landed_first, parts_attn))
    sum_attn = lax.psum_scatter(parts_attn, "tensor", scatter_dimension=0, tiled=False)
    first_all = (dp_rank == 0).astype(jnp.float32) * (tp_rank == 0).astype(jnp.float32)
    head_squares = first_all * (squares(grad_head_first) + squares(grad_head_second) + squares(grad_head_bias))
    corner = (lax.broadcasted_iota(jnp.int32, (8, 128), 0) + lax.broadcasted_iota(jnp.int32, (8, 128), 1)) == 0
    tile = jnp.where(corner, head_squares, 0.0)
    (sum_down,), tile = ring_sum([sum_down], tile, groups, shards, 2, 0, 1)
    (sum_up,), squared = ring_sum([sum_up], tile, groups, shards, 2, 0, 3)
    landed_first, sum_up = lax.optimization_barrier((landed_first, sum_up))
    zero_table = jnp.zeros((vocab_rows, cols), jnp.float32)
    grad_embedding = add_rows(landed_first, rows_first, zero_table)

    def give_more(state):
        round_index, total = state
        wanted, rows, _ = serve(round_index)
        return round_index + 1, add_rows(trade(send_back(wanted)), rows, total)

    _, grad_embedding = lax.while_loop(more, give_more, (jnp.int32(1), grad_embedding))

    squared = squared + jnp.where(corner, squares(grad_embedding), 0.0)
    sum_attn, grad_embedding = lax.optimization_barrier((sum_attn, grad_embedding))
    (sum_attn,), squared = ring_sum([sum_attn], squared, groups, shards, 2, SMALL_ROWS, 2)
    sum_small = sum_attn[-SMALL_ROWS:].reshape(-1)[:small_size].reshape(grad_small.shape)
    grad_norms = sum_small[:8]
    grad_bias_qv = lax.dynamic_slice_in_dim(sum_small[8:10], tp_rank * cols, cols, 1)
    grad_bias_up = lax.dynamic_slice_in_dim(sum_small[10:].reshape(-1), tp_rank * hidden, hidden)
    grad_attn = sum_attn[: 4 * width]
    grad_ffn_up, grad_ffn_down = sum_up, sum_down
    grad_pos = sum_attn[4 * width : -SMALL_ROWS]

    grad_norm = jnp.sqrt(jnp.sum(squared))
    factor = jnp.minimum(1.0, CLIP_SCALE * math.sqrt(PARAMS) / (grad_norm + 1e-06))
    grad_positions = jnp.pad(grad_pos, ((2, positions.shape[0] - slots - 2), (0, 0)))
    grad_ffn = jnp.stack([grad_ffn_up, grad_ffn_down])
    new_embedding, next_embedding = advance(embedding, mom_embedding, grad_embedding, factor)
    new_positions, next_positions = advance(positions, mom_positions, grad_positions, factor)
    flat_attn, flat_mom = attn_weights.reshape(-1, cols), mom_attn.reshape(-1, cols)
    new_attn, next_attn = (x.reshape(attn_weights.shape) for x in advance(flat_attn, flat_mom, grad_attn, factor))
    new_ffn, next_ffn = advance(ffn_weights, ffn_momentum, grad_ffn, factor)
    new_bias_qv, next_bias_qv = advance(bias_qv, mom_bias_qv, grad_bias_qv, factor)
    new_bias_up, next_bias_up = advance(bias_up, mom_bias_up, grad_bias_up, factor)
    new_norms, next_norms = advance(norms, mom_norms, grad_norms, factor)
    new_head_first, next_head_first = advance(head_first, mom_head_first, grad_head_first, factor)
    new_head_second, next_head_second = advance(head_second, mom_head_second, grad_head_second, factor)
    new_head_bias, next_head_bias = advance(head_bias, mom_head_bias, grad_head_bias, factor)
    return (
        new_embedding, new_positions, new_attn, new_ffn, new_bias_qv, new_bias_up, new_norms, new_head_first,
        new_head_second, new_head_bias, next_embedding, next_positions, next_attn, next_ffn, next_bias_qv,
        next_bias_up, next_norms, next_head_first, next_head_second, next_head_bias, loss, grad_norm,
    )


def solution(mesh):
    in_specs = (
        P("dp", None),
        P("dp"),
        P(),
        P("dp", "tensor"),
        P(None, "tensor"),
        P(None, None, "tensor"),
        P(None, None, "tensor"),
        P(None, "tensor"),
        P("tensor"),
        P(),
        P(),
        P(),
        P(),
        P("dp", "tensor"),
        P(None, "tensor"),
        P(None, None, "tensor"),
        P(None, None, "tensor"),
        P(None, "tensor"),
        P("tensor"),
        P(),
        P(),
        P(),
        P(),
    )
    out_specs = (
        P("dp", "tensor"),
        P(None, "tensor"),
        P(None, None, "tensor"),
        P(None, None, "tensor"),
        P(None, "tensor"),
        P("tensor"),
        P(),
        P(),
        P(),
        P(),
        P("dp", "tensor"),
        P(None, "tensor"),
        P(None, None, "tensor"),
        P(None, None, "tensor"),
        P(None, "tensor"),
        P("tensor"),
        P(),
        P(),
        P(),
        P(),
        P(),
        P(),
    )
    groups, shards = mesh.shape["dp"], mesh.shape["tensor"]

    def run(*arrays):
        body = on_device
        if 2 * (arrays[0].shape[0] // groups) == 3 * shards:
            body = functools.partial(fast_on_device, groups=groups, shards=shards)
        return jax.shard_map(
            body, mesh=mesh, in_specs=in_specs, out_specs=out_specs, check_vma=False
        )(*arrays)

    return run
```

```python
import functools
import math

import jax
import jax.numpy as jnp
from jax import lax
from jax.experimental import pallas as pl
from jax.experimental.pallas import tpu as pltpu
from jax.sharding import PartitionSpec as P

HEAD_DIM = 64
PARAMS = 65044736


EPS = 1e-05
SOFTMAX_TEMP = 0.1
DECAY = 0.9
RATE = 100000.0
CLIP_SCALE = 1e-06
HIGH = lax.Precision.HIGHEST
PRODUCT = lax.Precision.HIGH
CAPACITY = 88
SMALL_ROWS = 64


def precise_product(left, right):
    return jnp.matmul(left, right, precision=HIGH)


def norm_rows(values, gain, shift):
    center = values - jnp.mean(values, axis=-1, keepdims=True)
    spread = jnp.mean(center * center, axis=-1, keepdims=True)
    return center * lax.rsqrt(spread + EPS) * gain + shift


def attend(normed, lengths, attn, bias_qv):
    seqs, slots, width = normed.shape
    cols = attn.shape[2]
    heads = cols // HEAD_DIM
    queries = (precise_product(normed, attn[0]) + bias_qv[0]).reshape(seqs, slots, heads, HEAD_DIM)
    keys_all = precise_product(normed, attn[1]).reshape(seqs, slots, heads, HEAD_DIM)
    values = (precise_product(normed, attn[2]) + bias_qv[1]).reshape(seqs, slots, heads, HEAD_DIM)
    scores = jnp.einsum("sqhd,skhd->shqk", queries, keys_all, precision=HIGH) / math.sqrt(HEAD_DIM)
    valid = lax.broadcasted_iota(jnp.int32, (seqs, slots), 1) < lengths[:, None]
    scores = jnp.where(valid[:, None, None, :], scores, -1e30)
    probs = jax.nn.softmax(scores, axis=-1)
    mixed = jnp.einsum("shqk,skhd->sqhd", probs, values, precision=HIGH).reshape(seqs, slots, cols)
    return precise_product(mixed, attn[3].T)


def expand(normed, ffn, bias_up):
    hidden = jax.nn.gelu(precise_product(normed, ffn[0]) + bias_up, approximate=False)
    return precise_product(hidden, ffn[1].T)


def contrast(pooled, head_first, head_second, head_bias, partners):
    middle = jax.nn.gelu(precise_product(pooled, head_first) + head_bias, approximate=False)
    output = precise_product(middle, head_second)
    unit_vectors = output * lax.rsqrt(jnp.sum(output * output, axis=-1, keepdims=True) + 1e-06)
    similarity_scores = precise_product(unit_vectors, unit_vectors.T) / SOFTMAX_TEMP
    count = similarity_scores.shape[0]
    index = lax.broadcasted_iota(jnp.int32, (count,), 0)
    similarity_scores = jnp.where(index[:, None] == index[None, :], -1e30, similarity_scores)
    totals = jax.nn.logsumexp(similarity_scores, axis=-1)
    paired_rows = jnp.sum(
        jnp.where(index[None, :] == partners[:, None], similarity_scores, 0.0), axis=-1
    )
    return jnp.sum(totals - paired_rows)


def owner_rows(ids_part, base, vocab_rows):
    local_ids = ids_part - base
    inside = (local_ids >= 0) & (local_ids < vocab_rows)
    return jnp.where(inside, local_ids, vocab_rows)


def advance(weight, moment, grad, factor):
    clipped = factor * grad
    moment_new = DECAY * moment + (1.0 - DECAY) * clipped
    return (weight - RATE * (DECAY * moment_new + (1.0 - DECAY) * clipped), moment_new)


def squares(array):
    return jnp.sum(array * array)


def on_device(
    token_ids,
    lengths,
    partners,
    embedding,
    positions,
    attn_weights,
    ffn_weights,
    bias_qv,
    bias_up,
    norms,
    head_first,
    head_second,
    head_bias,
    mom_embedding,
    mom_positions,
    mom_attn,
    ffn_momentum,
    mom_bias_qv,
    mom_bias_up,
    mom_norms,
    mom_head_first,
    mom_head_second,
    mom_head_bias,
):
    seqs, slots = token_ids.shape
    vocab_rows, cols = embedding.shape
    dp_rank = lax.axis_index("dp")
    tp_rank = lax.axis_index("tensor")
    base = dp_rank * vocab_rows
    all_ids = lax.all_gather(token_ids, "dp", axis=0, tiled=True).reshape(-1)
    padded_table = jnp.concatenate([embedding, jnp.zeros((1, cols), jnp.float32)], axis=0)
    rows_ids = owner_rows(all_ids, base, vocab_rows)
    token_rows = lax.psum_scatter(
        jnp.take(padded_table, rows_ids, axis=0), "dp", scatter_dimension=0, tiled=True
    )
    token_cols = token_rows.reshape(seqs, slots, cols) + positions[2 : slots + 2][None]
    embedded = lax.all_gather(token_cols, "tensor", axis=2, tiled=True)
    h_zero, ln_zero_pull = jax.vjp(norm_rows, embedded, norms[0], norms[1])
    attn_part, attn_pull = jax.vjp(
        lambda normed, weights, biases: attend(normed, lengths, weights, biases),
        h_zero,
        attn_weights,
        bias_qv,
    )
    x_one = h_zero + lax.psum(attn_part, "tensor") + norms[6]
    h_one, ln_one_pull = jax.vjp(norm_rows, x_one, norms[2], norms[3])
    ffn_part, ffn_pull = jax.vjp(expand, h_one, ffn_weights, bias_up)
    x_two = h_one + lax.psum(ffn_part, "tensor") + norms[7]
    h_two, ln_two_pull = jax.vjp(norm_rows, x_two, norms[4], norms[5])
    valid = (lax.broadcasted_iota(jnp.int32, (seqs, slots), 1) < lengths[:, None]).astype(
        jnp.float32
    )
    len_float = lengths.astype(jnp.float32)
    pooled = jnp.sum(h_two * valid[:, :, None], axis=1) / len_float[:, None]
    all_pooled = lax.all_gather(pooled, "dp", axis=0, tiled=True)
    loss, head_pull = jax.vjp(
        lambda rows, first_w, second_w, bias_w: contrast(rows, first_w, second_w, bias_w, partners),
        all_pooled,
        head_first,
        head_second,
        head_bias,
    )
    back_pooled_all, grad_head_first, grad_head_second, grad_head_bias = head_pull(
        jnp.ones_like(loss)
    )
    back_pooled = lax.dynamic_slice_in_dim(back_pooled_all, dp_rank * seqs, seqs)
    back_h_two = valid[:, :, None] * (back_pooled / len_float[:, None])[:, None, :]
    back_x_two, grad_gain_two, grad_shift_two = ln_two_pull(back_h_two)
    back_h_one_part, grad_ffn, grad_bias_up = ffn_pull(back_x_two)
    back_h_one = back_x_two + lax.psum(back_h_one_part, "tensor")
    back_x_one, grad_gain_one, grad_shift_one = ln_one_pull(back_h_one)
    back_h_zero_part, grad_attn, grad_bias_qv = attn_pull(back_x_one)
    back_h_zero = back_x_one + lax.psum(back_h_zero_part, "tensor")
    back_embedded, grad_gain_zero, grad_shift_zero = ln_zero_pull(back_h_zero)
    back_cols = lax.dynamic_slice_in_dim(back_embedded, tp_rank * cols, cols, 2)
    grad_positions = jnp.pad(
        jnp.sum(back_cols, axis=0), ((2, positions.shape[0] - slots - 2), (0, 0))
    )
    grad_norms = jnp.stack(
        [
            grad_gain_zero,
            grad_shift_zero,
            grad_gain_one,
            grad_shift_one,
            grad_gain_two,
            grad_shift_two,
            jnp.sum(back_x_one, axis=(0, 1)),
            jnp.sum(back_x_two, axis=(0, 1)),
        ]
    )
    back_flat = back_cols.reshape(seqs * slots, cols)
    target = owner_rows(all_ids, base, vocab_rows)
    grad_embedding = jax.ops.segment_sum(
        lax.all_gather(back_flat, "dp", axis=0, tiled=True), target, num_segments=vocab_rows + 1
    )[:vocab_rows]
    first_dp = (dp_rank == 0).astype(jnp.float32)
    first_all = first_dp * (tp_rank == 0).astype(jnp.float32)
    grad_attn, grad_ffn, grad_positions, grad_bias_qv, grad_bias_up, grad_norms = lax.psum(
        (grad_attn, grad_ffn, grad_positions, grad_bias_qv, grad_bias_up, grad_norms), "dp"
    )
    big_squares = first_dp * (squares(grad_attn) + squares(grad_ffn))
    local_squares = (
        big_squares
        + squares(grad_embedding)
        + first_dp * (squares(grad_positions) + squares(grad_bias_qv) + squares(grad_bias_up))
        + first_all
        * (
            squares(grad_norms)
            + squares(grad_head_first)
            + squares(grad_head_second)
            + squares(grad_head_bias)
        )
    )
    total_squares = lax.psum(local_squares, ("dp", "tensor"))
    grad_norm = jnp.sqrt(total_squares)
    factor = jnp.minimum(1.0, CLIP_SCALE * math.sqrt(PARAMS) / (grad_norm + 1e-06))
    new_attn, next_attn = advance(attn_weights, mom_attn, grad_attn, factor)
    new_ffn, next_ffn = advance(ffn_weights, ffn_momentum, grad_ffn, factor)
    new_embedding, next_embedding = advance(embedding, mom_embedding, grad_embedding, factor)
    new_positions, next_positions = advance(positions, mom_positions, grad_positions, factor)
    new_bias_qv, next_bias_qv = advance(bias_qv, mom_bias_qv, grad_bias_qv, factor)
    new_bias_up, next_bias_up = advance(bias_up, mom_bias_up, grad_bias_up, factor)
    new_norms, next_norms = advance(norms, mom_norms, grad_norms, factor)
    new_head_first, next_head_first = advance(head_first, mom_head_first, grad_head_first, factor)
    new_head_second, next_head_second = advance(
        head_second, mom_head_second, grad_head_second, factor
    )
    new_head_bias, next_head_bias = advance(head_bias, mom_head_bias, grad_head_bias, factor)
    return (
        new_embedding,
        new_positions,
        new_attn,
        new_ffn,
        new_bias_qv,
        new_bias_up,
        new_norms,
        new_head_first,
        new_head_second,
        new_head_bias,
        next_embedding,
        next_positions,
        next_attn,
        next_ffn,
        next_bias_qv,
        next_bias_up,
        next_norms,
        next_head_first,
        next_head_second,
        next_head_bias,
        loss,
        grad_norm,
    )


MESH = pl.DeviceIdType.MESH
VMEM = pl.BlockSpec(memory_space=pltpu.VMEM)


def cube_partners(groups, shards):
    dp, tp = lax.axis_index("dp"), lax.axis_index("tensor")
    partners = []
    for size, at in ((shards, 1), (groups, 0)):
        bit = 1
        while bit < size:
            here = (dp, tp)[at]
            there = here + bit * (1 - 2 * ((here // bit) % 2))
            partners.append((dp, there) if at else (there, tp))
            bit *= 2
    return partners


def greet(partners):
    barrier = pltpu.get_barrier_semaphore()
    for partner in partners:
        pl.semaphore_signal(barrier, inc=1, device_id=partner, device_id_type=MESH)
    pl.semaphore_wait(barrier, len(partners))


def cube_stages(groups, shards):
    return (groups * shards).bit_length() - 1


def meet_kernel(groups, shards, x_ref, o_ref, held, send_sem, recv_sem):
    dp, tp = lax.axis_index("dp"), lax.axis_index("tensor")
    near = [(dp, (tp + k) % shards) for k in range(1, shards)]
    far = [((dp + k) % groups, tp) for k in range(1, groups)]
    greet([*near, *far])
    me = dp * shards + tp
    held[pl.ds(me, 1)] = x_ref[...][None]
    at = 0
    for partners, mine in ((near, pl.ds(me, 1)), (far, pl.ds(dp * shards, shards))):
        copies = []
        for partner in partners:
            copy = pltpu.make_async_remote_copy(
                src_ref=held.at[mine],
                dst_ref=held.at[mine],
                send_sem=send_sem.at[at],
                recv_sem=recv_sem.at[at],
                device_id=partner,
                device_id_type=MESH,
            )
            copy.start()
            copies.append(copy)
            at += 1
        for copy in copies:
            copy.wait()
    o_ref[...] = held[...]


def meet(block, groups, shards, collective_id):
    shape = (groups * shards, *block.shape)
    return pl.pallas_call(
        functools.partial(meet_kernel, groups, shards),
        out_shape=jax.ShapeDtypeStruct(shape, block.dtype),
        in_specs=[VMEM],
        out_specs=VMEM,
        scratch_shapes=[
            pltpu.VMEM(shape, block.dtype),
            pltpu.SemaphoreType.DMA((groups + shards - 2,)),
            pltpu.SemaphoreType.DMA((groups + shards - 2,)),
        ],
        compiler_params=pltpu.CompilerParams(collective_id=collective_id, has_side_effects=True),
    )(block)


def fold_squares(block):
    block = block * block
    folded = jnp.sum(block.reshape(block.shape[0] // 8, 8, block.shape[1]), axis=0)
    total = folded[:, :128]
    for start in range(128, block.shape[1], 128):
        total = total + folded[:, start : start + 128]
    return total


def ring_kernel(groups, shards, parts, arrays, shared_rows, *refs):
    refs = list(refs)
    inputs = [refs.pop(0) for _ in range(arrays)]
    base = refs.pop(0)
    outputs = [refs.pop(0) for _ in range(arrays)]
    squares_ref = refs.pop(0)
    slots = [refs.pop(0) for _ in range(arrays)]
    send_sem, recv_sem, sent, landed, cube_send, cube_recv = refs
    depth = groups // 2
    dp, tp = lax.axis_index("dp"), lax.axis_index("tensor")
    side, level = dp % 2, dp // 2
    place = level * (1 - side) + (groups - 1 - level) * side

    def device_at(spot):
        spot = (spot + groups) % groups
        far = spot // depth
        return (2 * (spot * (1 - far) + (groups - 1 - spot) * far) + far, tp)

    partners = cube_partners(groups, shards) if shared_rows else []
    greet([device_at(place + 1), device_at(place - 1), *partners])
    streams = []
    for array in range(arrays):
        tiles = inputs[array].shape[1] // 8
        edges = [8 * (tiles * part // (2 * parts)) for part in range(2 * parts + 1)]
        for part in range(2 * parts):
            streams.append((array, 1 - 2 * (part % 2), edges[part], edges[part + 1] - edges[part]))

    def chunk(step, way):
        return (place + groups * 2 - way * step) % groups

    copies = []

    def send(source, target, send_at, recv_at, device):
        copy = pltpu.make_async_remote_copy(
            src_ref=source,
            dst_ref=target,
            send_sem=send_at,
            recv_sem=recv_at,
            device_id=device,
            device_id_type=MESH,
        )
        copy.start()
        copies.append(copy)
        return copy

    def pass_on(index, step, source, target):
        device = device_at(place + streams[index][1])
        return send(source, target, send_sem.at[index, step], recv_sem.at[index, step], device)

    flying = [None] * len(streams)
    for step in range(groups - 1):
        for index, (array, way, start, size) in enumerate(streams):
            rows = pl.ds(start, size)
            if step == 0:
                source = inputs[array].at[chunk(0, way), rows]
            else:
                flying[index].wait_recv()
                source = slots[array].at[step - 1, rows]
                source[...] = source[...] + inputs[array][chunk(step, way), rows]
            flying[index] = pass_on(index, step, source, slots[array].at[step, rows])
    total = base[...]
    crossing = None
    for step in range(groups - 1):
        for index, (array, way, start, size) in enumerate(streams):
            rows = pl.ds(start, size)
            flying[index].wait_recv()
            now = chunk(groups - 1 + step, way)
            if step == 0:
                block = slots[array][groups - 2, rows] + inputs[array][now, rows]
                outputs[array][now, rows] = block
                if shared_rows:
                    depth_rows = inputs[array].shape[1]
                    limit = groups * depth_rows - shared_rows * (1 - (shards - tp) // shards)
                    at = now * depth_rows + start + lax.broadcasted_iota(jnp.int32, block.shape, 0)
                    block = jnp.where(at < limit, block, 0.0)
                total = total + fold_squares(block)
            out = outputs[array].at[now, rows]
            flying[index] = pass_on(index, groups - 1 + step, out, out)
        if step <= len(partners) and partners:
            if step == 0:
                sent[0] = total
            else:
                crossing.wait_recv()
                sent[step] = sent[step - 1] + landed[step - 1]
            if step < len(partners):
                crossing = send(
                    sent.at[step], landed.at[step], cube_send.at[step], cube_recv.at[step], partners[step]
                )
    squares_ref[...] = sent[len(partners)] if partners else total
    for copy in flying:
        copy.wait_recv()
    for copy in copies:
        copy.wait_send()


def ring_sum(arrays, base, groups, shards, parts, shared_rows, collective_id):
    blocks = [array.reshape(groups, array.shape[0] // groups, array.shape[1]) for array in arrays]
    streams = 2 * parts * len(blocks)
    steps = 2 * (groups - 1)
    stages = cube_stages(groups, shards)
    *sums, squared = pl.pallas_call(
        functools.partial(ring_kernel, groups, shards, parts, len(blocks), shared_rows),
        out_shape=[jax.ShapeDtypeStruct(block.shape, block.dtype) for block in [*blocks, base]],
        in_specs=[VMEM] * (len(blocks) + 1),
        out_specs=[VMEM] * (len(blocks) + 1),
        scratch_shapes=[
            *[pltpu.VMEM((groups - 1, *block.shape[1:]), block.dtype) for block in blocks],
            pltpu.SemaphoreType.DMA((streams, steps)),
            pltpu.SemaphoreType.DMA((streams, steps)),
            pltpu.VMEM((stages + 1, *base.shape), base.dtype),
            pltpu.VMEM((stages, *base.shape), base.dtype),
            pltpu.SemaphoreType.DMA((stages,)),
            pltpu.SemaphoreType.DMA((stages,)),
        ],
        compiler_params=pltpu.CompilerParams(
            collective_id=collective_id, has_side_effects=True, vmem_limit_bytes=48 << 20
        ),
        cost_estimate=pl.CostEstimate(flops=1, bytes_accessed=1024, transcendentals=0),
    )(*blocks, base)
    return [total.reshape(array.shape) for total, array in zip(sums, arrays)], squared


def spread_kernel(
    groups, w_ref, small_ref, o_ref, rows_ref, local_sem, pair_send, pair_recv, ring_send, ring_recv, core_send, core_recv
):
    depth = groups // 2
    dp, tp = lax.axis_index("dp"), lax.axis_index("tensor")
    far = tp + 2 - 4 * (tp // 2)
    core = (dp, tp + 1 - 2 * (tp % 2))
    side, level = dp % 2, dp // 2
    place = level * (1 - side) + (groups - 1 - level) * side

    def index_at(spot):
        spot = (spot + groups) % groups
        back = spot // depth
        return 2 * (spot * (1 - back) + (groups - 1 - spot) * back) + back

    def send(source, target, send_sem, recv_sem, device):
        copy = pltpu.make_async_remote_copy(
            src_ref=source,
            dst_ref=target,
            send_sem=send_sem,
            recv_sem=recv_sem,
            device_id=device,
            device_id_type=MESH,
        )
        copy.start()
        return copy

    greet([(index_at(place + 1), tp), (index_at(place - 1), tp), core, (dp, far)])
    cross = send(w_ref.at[dp], o_ref.at[tp, dp], pair_send.at[0], pair_recv.at[0], (dp, far))
    near = send(w_ref, o_ref.at[tp], pair_send.at[1], pair_recv.at[1], core)
    cross_rows = send(small_ref, rows_ref.at[tp], pair_send.at[2], pair_recv.at[2], (dp, far))
    near_rows = send(small_ref, rows_ref.at[tp], pair_send.at[3], pair_recv.at[3], core)
    local = pltpu.make_async_copy(w_ref, o_ref.at[tp], local_sem)
    local.start()
    rows_ref[tp] = small_ref[...]
    cross.wait_recv()
    lanes = ring_send.shape[0]
    size = w_ref.shape[1] // lanes
    flying = [None] * lanes
    started = [cross, cross_rows]
    handed = [near, near_rows]
    for step in range(groups):
        for lane in range(lanes):
            way = 1 - 2 * (lane % 2)
            block = o_ref.at[far, index_at(place + groups - way * step), pl.ds(lane * size, size)]
            if step > 0:
                flying[lane].wait_recv()
            if step < groups - 1:
                flying[lane] = send(
                    block, block, ring_send.at[lane, step], ring_recv.at[lane, step], (index_at(place + way), tp)
                )
                started.append(flying[lane])
            handed.append(send(block, block, core_send.at[lane, step], core_recv.at[lane, step], core))
    cross_rows.wait_recv()
    handed.append(send(rows_ref.at[far], rows_ref.at[far], pair_send.at[4], pair_recv.at[4], core))
    for copy in handed:
        copy.wait_recv()
        copy.wait_send()
    for copy in started:
        copy.wait_send()
    local.wait()


def spread(weight, small, groups, collective_id):
    rows = weight.shape[0] // groups
    lanes = 4
    gathered, gathered_rows = pl.pallas_call(
        functools.partial(spread_kernel, groups),
        out_shape=[
            jax.ShapeDtypeStruct((4, groups, rows, weight.shape[1]), weight.dtype),
            jax.ShapeDtypeStruct((4, *small.shape), small.dtype),
        ],
        in_specs=[pl.BlockSpec(memory_space=pl.ANY), VMEM],
        out_specs=[VMEM, VMEM],
        scratch_shapes=[
            pltpu.SemaphoreType.DMA,
            pltpu.SemaphoreType.DMA((5,)),
            pltpu.SemaphoreType.DMA((5,)),
            pltpu.SemaphoreType.DMA((lanes, groups - 1)),
            pltpu.SemaphoreType.DMA((lanes, groups - 1)),
            pltpu.SemaphoreType.DMA((lanes, groups)),
            pltpu.SemaphoreType.DMA((lanes, groups)),
        ],
        compiler_params=pltpu.CompilerParams(
            collective_id=collective_id, has_side_effects=True, vmem_limit_bytes=32 << 20
        ),
        cost_estimate=pl.CostEstimate(flops=1, bytes_accessed=1024, transcendentals=0),
    )(weight.reshape(groups, rows, weight.shape[1]), small)
    return gathered.reshape(4, *weight.shape), gathered_rows


def halves(array):
    high = array.astype(jnp.bfloat16)
    return high, (array - high.astype(jnp.float32)).astype(jnp.bfloat16)


def dot_rows(left, right):
    return lax.dot_general(left, right, (((1,), (1,)), ((), ())), preferred_element_type=jnp.float32)


def dot_plain(left, right):
    return lax.dot_general(left, right, (((1,), (0,)), ((), ())), preferred_element_type=jnp.float32)


def one_head(array, head):
    lane = lax.broadcasted_iota(jnp.int32, array.shape, 1)
    return jnp.where(lane // HEAD_DIM == head, array, 0.0)


def score_tile(twice_k, low_k, high_q, low_q, bias):
    wide = dot_rows(twice_k, jnp.concatenate([high_q, low_q], axis=1))
    return wide + dot_rows(low_k, high_q) + bias


def attend_kernel(slots, tile, q_ref, k_ref, v_ref, bias_ref, o_ref, lse_ref):
    scale = 1.0 / math.sqrt(HEAD_DIM)
    high_k, low_k = halves(k_ref[0])
    twice_k = jnp.concatenate([high_k, high_k], axis=1)
    high_v, low_v = halves(v_ref[0].T)
    def scores_of(start):
        first = 0 if start < slots else slots
        keys = slice(first, first + slots)
        found = []
        for head in range(2):
            high_q, low_q = halves(one_head(q_ref[0, pl.ds(start, tile)] * scale, head))
            found.append(score_tile(twice_k[keys], low_k[keys], high_q, low_q, bias_ref[pl.ds(first, slots)]))
        return found

    starts = list(range(0, q_ref.shape[1], tile))
    ready = scores_of(starts[0])
    for index, start in enumerate(starts):
        rows = pl.ds(start, tile)
        first = 0 if start < slots else slots
        keys = slice(first, first + slots)
        score_pair = ready
        if index + 1 < len(starts):
            ready = scores_of(starts[index + 1])
        peaks = [jnp.max(jnp.max(s.reshape(8, -1, tile), axis=0), axis=0, keepdims=True) for s in score_pair]
        pairs = [jnp.exp(s - p) for s, p in zip(score_pair, peaks)]
        found = []
        for head in range(2):
            peak, probs = peaks[head], pairs[head]
            total = jnp.sum(jnp.sum(probs.reshape(8, -1, tile), axis=0), axis=0, keepdims=True)
            lse_ref[0, pl.ds(head, 1), rows] = peak + jnp.log(total)
            high_p, low_p = halves(probs)
            lanes = slice(head * HEAD_DIM, (head + 1) * HEAD_DIM)
            both = jnp.concatenate([high_v[lanes, keys], low_v[lanes, keys]], axis=0)
            wide = dot_plain(both, high_p)
            mixed = wide[:HEAD_DIM] + wide[HEAD_DIM:] + dot_plain(high_v[lanes, keys], low_p)
            found.append(mixed / total)
        o_ref[0, rows] = jnp.concatenate(found, axis=0).T


def attend_back_kernel(slots, tile, q_ref, k_ref, v_ref, bias_ref, o_ref, lse_ref, d_ref, dq_ref, dk_ref, dv_ref):
    scale = 1.0 / math.sqrt(HEAD_DIM)
    high_k, low_k = halves(k_ref[0])
    twice_k = jnp.concatenate([high_k, high_k], axis=1)
    high_v, low_v = halves(v_ref[0])
    twice_v = jnp.concatenate([high_v, high_v], axis=1)
    high_kt, low_kt = halves(k_ref[0].T)
    ones = jnp.ones((8, 2 * HEAD_DIM), jnp.bfloat16)
    lanes = 2 * HEAD_DIM
    for first in (0, slots):
        keys = slice(first, first + slots)
        key_rows = pl.ds(first, slots)
        for start in range(first, min(first + slots, q_ref.shape[1]), tile):
            rows = pl.ds(start, tile)
            back_qt = []
            for head in range(2):
                high_q, low_q = halves(one_head(q_ref[0, rows] * scale, head))
                back = one_head(d_ref[0, rows], head)
                high_d, low_d = halves(back)
                scores = score_tile(twice_k[keys], low_k[keys], high_q, low_q, bias_ref[key_rows])
                probs = jnp.exp(scores - lse_ref[0, pl.ds(head, 1), rows])
                high_x, low_x = halves(back * o_ref[0, rows])
                inner = (dot_rows(ones, high_x) + dot_rows(ones, low_x))[:1]
                back_s = probs * (score_tile(twice_v[keys], low_v[keys], high_d, low_d, 0.0) - inner)
                high_p, low_p = halves(probs)
                high_s, low_s = halves(back_s)
                wide = dot_plain(high_p, jnp.concatenate([high_d, low_d], axis=1))
                back_v = wide[:, :lanes] + wide[:, lanes:] + dot_plain(low_p, high_d)
                wide = dot_plain(high_s, jnp.concatenate([high_q, low_q], axis=1))
                back_k = wide[:, :lanes] + wide[:, lanes:] + dot_plain(low_s, high_q)
                if start == first and head == 0:
                    dv_ref[0, key_rows] = back_v
                    dk_ref[0, key_rows] = back_k
                else:
                    dv_ref[0, key_rows] += back_v
                    dk_ref[0, key_rows] += back_k
                mine = slice(head * HEAD_DIM, (head + 1) * HEAD_DIM)
                both = jnp.concatenate([high_kt[mine, keys], low_kt[mine, keys]], axis=0)
                wide = dot_plain(both, high_s)
                back_qt.append(wide[:HEAD_DIM] + wide[HEAD_DIM:] + dot_plain(high_kt[mine, keys], low_s))
            dq_ref[0, rows] = jnp.concatenate(back_qt, axis=0).T * scale


def attend_call(kernel, slots, inputs, outputs):
    lanes = 2 * HEAD_DIM
    queries = inputs[0]
    per_shard = queries.shape[2] // lanes
    pairs = queries.shape[0] * per_shard

    def spec(shape):
        if shape[1] == 1:
            return pl.BlockSpec(shape, lambda i: (0, 0))
        if shape[1] == 2:
            return pl.BlockSpec((1, *shape[1:]), lambda i: (i, 0, 0))
        return pl.BlockSpec((1, shape[1], lanes), lambda i: (i // per_shard, 0, i % per_shard))

    work = 7 * 2 * pairs * 2 * queries.shape[1] * slots * HEAD_DIM * 3
    return pl.pallas_call(
        functools.partial(kernel, slots, slots // 2),
        grid=(pairs,),
        in_specs=[spec(x.shape) for x in inputs],
        out_specs=[spec(shape) for shape in outputs],
        out_shape=[jax.ShapeDtypeStruct(shape, jnp.float32) for shape in outputs],
        compiler_params=pltpu.CompilerParams(vmem_limit_bytes=48 << 20),
        cost_estimate=pl.CostEstimate(flops=4 * work, bytes_accessed=20 << 20, transcendentals=0),
    )(*inputs)


WIDE = 512


def dot_three(high_left, low_left, right, dot):
    high, low = halves(right)
    return dot(high_left, high) + dot(high_left, low) + dot(low_left, high)


def times_kernel(finish, extras, x_ref, w_ref, *refs):
    more, outs, (high, low) = refs[:extras], refs[extras:-2], refs[-2:]

    @pl.when((pl.program_id(0) == 0) & (pl.program_id(1) == 0))
    def _():
        high[...], low[...] = halves(x_ref[...])

    weight = w_ref[...].reshape(w_ref.shape[-2], w_ref.shape[-1])
    finish(dot_three(high[...], low[...], weight, dot_plain), more, outs)


def times(x, w, which, finish, extras, outs):
    shards, depth, columns = w.shape[0], w.shape[-2], w.shape[-1]
    rows, wide = x.shape[0], min(WIDE, columns)
    if w.ndim == 4:
        w_spec = pl.BlockSpec((1, 1, depth, wide), lambda j, c: (j, which, 0, c))
    else:
        w_spec = pl.BlockSpec((1, depth, wide), lambda j, c: (j, 0, c))

    def spec(shape):
        return pl.BlockSpec((1, shape[1], wide), lambda j, c: (j, 0, c))

    results = pl.pallas_call(
        functools.partial(times_kernel, finish, len(extras)),
        grid=(shards, columns // wide),
        in_specs=[pl.BlockSpec((rows, depth), lambda j, c: (0, 0)), w_spec, *[spec(e.shape) for e in extras]],
        out_specs=[spec(shape) for shape in outs],
        out_shape=[jax.ShapeDtypeStruct(shape, jnp.float32) for shape in outs],
        scratch_shapes=[pltpu.VMEM((rows, depth), jnp.bfloat16)] * 2,
        compiler_params=pltpu.CompilerParams(vmem_limit_bytes=48 << 20),
        cost_estimate=pl.CostEstimate(
            flops=6 * rows * depth * shards * columns, bytes_accessed=4 * w.size, transcendentals=0
        ),
    )(x, w, *extras)
    return results


def keep_tile(tile, more, outs):
    outs[0][0] = tile


def add_row(tile, more, outs):
    outs[0][0] = tile + more[0][0]


def gelu_tile(tile, more, outs):
    outs[0][0], outs[1][0] = gelu_both(tile + more[0][0])


def scale_tile(tile, more, outs):
    tile = tile * more[0][0]
    outs[0][0] = tile
    outs[1][0] = jnp.sum(tile, axis=0, keepdims=True)


def project_kernel(count, x_ref, y_ref, wq_ref, wk_ref, wv_ref, bq_ref, bv_ref, q_ref, k_ref, v_ref, high, low):
    @pl.when(pl.program_id(0) == 0)
    def _():
        high[:count], low[:count] = halves(x_ref[...])
        high[count:], low[count:] = halves(y_ref[...])

    q_ref[0] = dot_three(high[:count], low[:count], wq_ref[0, 0], dot_plain) + bq_ref[0]
    k_ref[0] = dot_three(high[...], low[...], wk_ref[0, 0], dot_plain)
    v_ref[0] = dot_three(high[...], low[...], wv_ref[0, 0], dot_plain) + bv_ref[0]


def project(x, y, w, bias_q, bias_v):
    count, depth = x.shape
    rows = count + y.shape[0]
    shards, _, _, columns = w.shape

    def weight(which):
        return pl.BlockSpec((1, 1, depth, columns), lambda j: (j, which, 0, 0))

    def tile(height):
        return pl.BlockSpec((1, height, columns), lambda j: (j, 0, 0))

    return pl.pallas_call(
        functools.partial(project_kernel, count),
        grid=(shards,),
        in_specs=[
            pl.BlockSpec(x.shape, lambda j: (0, 0)),
            pl.BlockSpec(y.shape, lambda j: (0, 0)),
            *[weight(which) for which in range(3)],
            tile(1),
            tile(1),
        ],
        out_specs=[tile(count), tile(rows), tile(rows)],
        out_shape=[jax.ShapeDtypeStruct((shards, n, columns), jnp.float32) for n in (count, rows, rows)],
        scratch_shapes=[pltpu.VMEM((rows, depth), jnp.bfloat16)] * 2,
        compiler_params=pltpu.CompilerParams(vmem_limit_bytes=48 << 20),
        cost_estimate=pl.CostEstimate(
            flops=6 * (count + 2 * rows) * depth * shards * columns, bytes_accessed=24 << 20, transcendentals=0
        ),
    )(x, y, w, w, w, bias_q, bias_v)


def gather_back_kernel(count, base_ref, *refs):
    out = refs[-1]

    @pl.when((pl.program_id(0) == 0) & (pl.program_id(1) == 0))
    def _():
        filled = base_ref.shape[0]
        out[:filled] = base_ref[...]
        if filled < out.shape[0]:
            out[filled:] = jnp.zeros((out.shape[0] - filled, out.shape[1]), jnp.float32)

    for a_ref, w_ref in zip(refs[:count], refs[count : 2 * count]):
        high, low = halves(a_ref[0])
        weight = w_ref[...].reshape(w_ref.shape[-2], w_ref.shape[-1])
        rows = pl.ds(0, a_ref.shape[1])
        out[rows] += dot_three(high, low, weight, dot_rows)


def gather_back(base, terms):
    arrays = [array for array, _, _ in terms]
    shards, _, columns = arrays[0].shape
    wide = min(WIDE, columns)
    total = (max(array.shape[1] for array in arrays), base.shape[1])

    def w_spec(w, which):
        if w.ndim == 4:
            return pl.BlockSpec((1, 1, w.shape[-2], wide), lambda j, c: (j, which, 0, c))
        return pl.BlockSpec((1, w.shape[-2], wide), lambda j, c: (j, 0, c))

    work = sum(6 * array.size * w.shape[-2] for array, w, _ in terms)
    return pl.pallas_call(
        functools.partial(gather_back_kernel, len(terms)),
        grid=(shards, columns // wide),
        in_specs=[
            pl.BlockSpec(base.shape, lambda j, c: (0, 0)),
            *[pl.BlockSpec((1, a.shape[1], wide), lambda j, c: (j, 0, c)) for a in arrays],
            *[w_spec(w, which) for _, w, which in terms],
        ],
        out_specs=pl.BlockSpec(total, lambda j, c: (0, 0)),
        out_shape=jax.ShapeDtypeStruct(total, jnp.float32),
        compiler_params=pltpu.CompilerParams(vmem_limit_bytes=48 << 20),
        cost_estimate=pl.CostEstimate(flops=work, bytes_accessed=16 << 20, transcendentals=0),
    )(base, *arrays, *[w for _, w, _ in terms])


def outer_kernel(x_ref, d_ref, *refs):
    out, high, low = refs[-3:]

    @pl.when((pl.program_id(0) == 0) & (pl.program_id(1) == 0))
    def _():
        high[...], low[...] = halves(x_ref[...].T)

    out[0] = dot_three(high[...], low[...], d_ref[0], dot_plain)


def outer(x, d, rows, at, into=None):
    tokens, depth = x.shape
    shards, _, columns = d.shape
    wide = min(WIDE, columns)
    held = [] if into is None else [into]
    return pl.pallas_call(
        outer_kernel,
        grid=(shards, columns // wide),
        in_specs=[
            pl.BlockSpec((tokens, depth), lambda j, c: (0, 0)),
            pl.BlockSpec((1, tokens, wide), lambda j, c: (j, 0, c)),
            *[pl.BlockSpec(memory_space=pl.ANY) for _ in held],
        ],
        out_specs=pl.BlockSpec((1, depth, wide), lambda j, c: (j, at, c)),
        out_shape=jax.ShapeDtypeStruct((shards, rows, columns), jnp.float32),
        scratch_shapes=[pltpu.VMEM((depth, tokens), jnp.bfloat16)] * 2,
        input_output_aliases={2: 0} if held else {},
        compiler_params=pltpu.CompilerParams(vmem_limit_bytes=48 << 20),
        cost_estimate=pl.CostEstimate(
            flops=6 * tokens * depth * shards * columns, bytes_accessed=4 * shards * depth * columns, transcendentals=0
        ),
    )(x, d, *held)


def outer_three_kernel(count, x_ref, y_ref, q_ref, k_ref, v_ref, out, high, low):
    @pl.when(pl.program_id(0) == 0)
    def _():
        high[:, :count], low[:, :count] = halves(x_ref[...].T)
        high[:, count:], low[:, count:] = halves(y_ref[...].T)

    depth = high.shape[0]
    out[0, pl.ds(0, depth)] = dot_three(high[:, :count], low[:, :count], q_ref[0], dot_plain)
    out[0, pl.ds(depth, depth)] = dot_three(high[...], low[...], k_ref[0], dot_plain)
    out[0, pl.ds(2 * depth, depth)] = dot_three(high[...], low[...], v_ref[0], dot_plain)


def outer_three(x, y, back_q, back_k, back_v, rows):
    shards, tokens, columns = back_k.shape
    count, depth = x.shape

    def tile(height):
        return pl.BlockSpec((1, height, columns), lambda j: (j, 0, 0))

    return pl.pallas_call(
        functools.partial(outer_three_kernel, count),
        grid=(shards,),
        in_specs=[
            pl.BlockSpec(x.shape, lambda j: (0, 0)),
            pl.BlockSpec(y.shape, lambda j: (0, 0)),
            tile(count),
            tile(tokens),
            tile(tokens),
        ],
        out_specs=tile(3 * depth),
        out_shape=jax.ShapeDtypeStruct((shards, rows, columns), jnp.float32),
        scratch_shapes=[pltpu.VMEM((depth, tokens), jnp.bfloat16)] * 2,
        compiler_params=pltpu.CompilerParams(vmem_limit_bytes=48 << 20),
        cost_estimate=pl.CostEstimate(
            flops=6 * (count + 2 * tokens) * depth * shards * columns, bytes_accessed=24 << 20, transcendentals=0
        ),
    )(x, y, back_q, back_k, back_v)


def thirds(array):
    high, rest = array.astype(jnp.bfloat16), None
    rest = array - high.astype(jnp.float32)
    middle = rest.astype(jnp.bfloat16)
    return high, middle, (rest - middle.astype(jnp.float32)).astype(jnp.bfloat16)


def select_rows(column, row, block):
    chosen = jnp.where(column == row, 1.0, 0.0).astype(jnp.bfloat16)
    high, middle, low = thirds(block)
    return dot_plain(chosen, high) + dot_plain(chosen, middle) + dot_plain(chosen, low)


def pack_kernel(wanted_ref, ids_ref, x_ref, o_ref):
    o_ref[...] = select_rows(wanted_ref[...], ids_ref[...], x_ref[...]).reshape(o_ref.shape)


def pack(wanted, ids, rows, groups, shards):
    cols = rows.shape[1] // shards
    return pl.pallas_call(
        pack_kernel,
        grid=(shards,),
        in_specs=[
            pl.BlockSpec((wanted.shape[0], 1), lambda j: (0, 0)),
            pl.BlockSpec((1, ids.shape[0]), lambda j: (0, 0)),
            pl.BlockSpec((ids.shape[0], cols), lambda j: (0, j)),
        ],
        out_specs=pl.BlockSpec((groups, 1, CAPACITY, cols), lambda j: (0, j, 0, 0)),
        out_shape=jax.ShapeDtypeStruct((groups, shards, CAPACITY, cols), jnp.float32),
        compiler_params=pltpu.CompilerParams(vmem_limit_bytes=32 << 20),
    )(wanted[:, None], ids[None, :], rows)


def expand_kernel(ids_ref, wanted_ref, x_ref, o_ref):
    block = x_ref[...].reshape(wanted_ref.shape[1], x_ref.shape[-1])
    o_ref[...] = select_rows(ids_ref[...], wanted_ref[...], block)


def expand_rows(ids, wanted, landed):
    groups, shards, _, cols = landed.shape
    return pl.pallas_call(
        expand_kernel,
        grid=(shards,),
        in_specs=[
            pl.BlockSpec((ids.shape[0], 1), lambda j: (0, 0)),
            pl.BlockSpec((1, wanted.shape[0]), lambda j: (0, 0)),
            pl.BlockSpec((groups, 1, CAPACITY, cols), lambda j: (0, j, 0, 0)),
        ],
        out_specs=pl.BlockSpec((ids.shape[0], cols), lambda j: (0, j)),
        out_shape=jax.ShapeDtypeStruct((ids.shape[0], shards * cols), jnp.float32),
        compiler_params=pltpu.CompilerParams(vmem_limit_bytes=32 << 20),
    )(ids[:, None], wanted[None, :], landed)


def normalise(values):
    center = values - jnp.mean(values, axis=-1, keepdims=True)
    scale = lax.rsqrt(jnp.mean(center * center, axis=-1, keepdims=True) + EPS)
    return center * scale, scale


def normalise_back(back, gain, unit, scale):
    inner = back * gain
    grad = scale * (
        inner
        - jnp.mean(inner, axis=-1, keepdims=True)
        - unit * jnp.mean(inner * unit, axis=-1, keepdims=True)
    )
    return grad, jnp.sum(back * unit, axis=0), jnp.sum(back, axis=0)


def gelu_both(values):
    cdf = 0.5 * (1.0 + lax.erf(values * math.sqrt(0.5)))
    pdf = jnp.exp(-0.5 * values * values) * (1.0 / math.sqrt(2.0 * math.pi))
    return values * cdf, cdf + values * pdf


def product(subscripts, left, right):
    return jnp.einsum(subscripts, left, right, precision=PRODUCT)


def request_lists(ids, vocab_rows, owners):
    count = ids.shape[0]
    index = lax.broadcasted_iota(jnp.int32, (count,), 0)
    earlier = index[None, :] < index[:, None]
    same = (ids[None, :] == ids[:, None]) & earlier
    first = jnp.logical_not(jnp.any(same, axis=1))
    owner = ids // vocab_rows
    ahead = (owner[None, :] == owner[:, None]) & earlier & first[None, :]
    rank = jnp.sum(ahead.astype(jnp.int32), axis=1)
    return owner, jnp.where(first, rank, -1)


def round_list(ids, owner, rank, round_index, owners):
    place = rank - round_index * CAPACITY
    inside = (rank >= 0) & (place >= 0) & (place < CAPACITY)
    place = jnp.where(inside, owner * CAPACITY + place, -1)
    wanted = lax.broadcasted_iota(jnp.int32, (owners * CAPACITY, 1), 0)
    return jnp.sum(jnp.where(place[None, :] == wanted, ids[None, :] + 1, 0), axis=1) - 1


def trade(block):
    return lax.all_to_all(block, ("dp", "tensor"), 0, 0, tiled=True)


def fast_on_device(
    token_ids, lengths, partners, embedding, positions, attn_weights, ffn_weights, bias_qv, bias_up, norms,
    head_first, head_second, head_bias, mom_embedding, mom_positions, mom_attn, ffn_momentum, mom_bias_qv,
    mom_bias_up, mom_norms, mom_head_first, mom_head_second, mom_head_bias, *, groups, shards
):
    seqs, slots = token_ids.shape
    half = slots // 2
    vocab_rows, cols = embedding.shape
    width = cols * shards
    devices = groups * shards
    hidden = bias_up.shape[0]
    heads = width // HEAD_DIM
    dp_rank = lax.axis_index("dp")
    tp_rank = lax.axis_index("tensor")
    pair = tp_rank // 2
    side = tp_rank % 2
    base = dp_rank * vocab_rows

    whole_seq = 3 * pair + 2 * side
    split_seq = 3 * pair + 1
    whole_ids = lax.dynamic_index_in_dim(token_ids, whole_seq, 0, keepdims=False)
    split_ids = lax.dynamic_index_in_dim(token_ids, split_seq, 0, keepdims=False)
    ids = jnp.concatenate([whole_ids, lax.dynamic_slice_in_dim(split_ids, side * half, half)])
    count = ids.shape[0]
    whole_length = lax.dynamic_index_in_dim(lengths, whole_seq, 0, keepdims=False)
    split_length = lax.dynamic_index_in_dim(lengths, split_seq, 0, keepdims=False)

    all_attn = lax.all_gather(attn_weights, "tensor")
    parts_shape = (shards, count, hidden)
    all_ffn_down = lax.all_gather(ffn_weights[1], "tensor")
    small = jnp.concatenate([positions[2 : slots + 2], bias_qv, bias_up.reshape(-1, cols)], axis=0)
    small = jnp.pad(small, ((0, -small.shape[0] % 8), (0, 0)))
    swap = [(i, i ^ 1) for i in range(shards)]
    owner, rank = request_lists(ids, vocab_rows, groups)
    rounds_here = jnp.max(rank) // CAPACITY + 1

    def serve(round_index):
        wanted = round_list(ids, owner, rank, round_index, groups)
        lists = jnp.broadcast_to(wanted.reshape(groups, 1, CAPACITY), (groups, shards, CAPACITY))
        lists = lists.reshape(devices, CAPACITY)
        tail = jnp.broadcast_to(rounds_here, (devices, 1)).astype(jnp.int32)
        lists = jnp.concatenate([lists, tail, jnp.zeros((devices, 127 - CAPACITY), jnp.int32)], axis=1)
        asked = trade(lists)
        rows = asked[:, :CAPACITY].reshape(-1) - base
        rounds = jnp.max(asked[:, CAPACITY])
        return wanted, rows, rounds

    def find(rows):
        return jnp.take(embedding, rows, axis=0, mode="clip")

    def expand(wanted, landed):
        return expand_rows(ids, wanted, landed.reshape(groups, shards, CAPACITY, cols))

    wanted_first, rows_first, rounds = serve(0)
    found, up_weights = lax.optimization_barrier((find(rows_first), ffn_weights[0]))
    all_ffn_up, all_small = spread(up_weights, small, groups, 6)
    landed, all_small = lax.optimization_barrier((trade(found), all_small))
    all_positions = all_small[:, :slots].transpose(1, 0, 2).reshape(slots, width)
    all_bias_up = all_small[:, slots + 2 : slots + 2 + hidden // cols].reshape(-1)
    tokens = expand(wanted_first, landed)

    def more(state):
        return state[0] < rounds

    def fetch_more(state):
        round_index, total = state
        wanted, rows, _ = serve(round_index)
        return round_index + 1, total + expand(wanted, trade(find(rows)))

    _, tokens = lax.while_loop(more, fetch_more, (jnp.int32(1), tokens))
    own_positions = jnp.concatenate(
        [all_positions, lax.dynamic_slice_in_dim(all_positions, side * half, half)], axis=0
    )
    embedded = tokens + own_positions
    unit_zero, scale_zero = normalise(embedded)
    h_zero = unit_zero * norms[0] + norms[1]

    h_other = lax.ppermute(h_zero[slots:], "tensor", swap)
    bias_q, bias_v = all_small[:, slots], all_small[:, slots + 1]
    queries, keys_all, values = project(h_zero, h_other, all_attn, bias_q[:, None, :], bias_v[:, None, :])
    key_index = lax.broadcasted_iota(jnp.int32, (slots,), 0)
    own_first = jnp.where(
        key_index < half, side * half + key_index, (1 - side) * half + key_index - half
    )
    counted = jnp.concatenate([key_index < whole_length, own_first < split_length])
    key_bias = jnp.where(counted, 0.0, -1e30).astype(jnp.float32)[:, None]
    mixed, lse = attend_call(
        attend_kernel,
        slots,
        (queries, keys_all, values, key_bias),
        (queries.shape, (heads // 2, 2, count)),
    )
    x_one = gather_back(h_zero + norms[6], [(mixed, all_attn, 3)])
    unit_one, scale_one = normalise(x_one)
    h_one = unit_one * norms[2] + norms[3]

    bias_tiles = all_bias_up.reshape(shards, 1, hidden)
    act, act_slope = times(h_one, all_ffn_up, 0, gelu_tile, [bias_tiles], [parts_shape, parts_shape])
    x_two = gather_back(h_one + norms[7], [(act, all_ffn_down, 0)])
    unit_two, scale_two = normalise(x_two)
    h_two = unit_two * norms[4] + norms[5]

    slot = lax.broadcasted_iota(jnp.int32, (count,), 0)
    in_whole = slot < slots
    place = jnp.where(in_whole, slot, slot - slots + side * half)
    keep = place < jnp.where(in_whole, whole_length, split_length)
    weight_whole = jnp.where(keep & in_whole, 1.0 / whole_length.astype(jnp.float32), 0.0)
    weight_split = jnp.where(keep & ~in_whole, 1.0 / split_length.astype(jnp.float32), 0.0)
    sums = jnp.stack(
        [jnp.sum(h_two * weight_whole[:, None], axis=0), jnp.sum(h_two * weight_split[:, None], axis=0)]
    )
    all_sums = meet(sums.reshape(-1, 128), groups, shards, 5).reshape(groups * shards // 2, 2, 2, width)
    all_pooled = jnp.stack(
        [all_sums[:, 0, 0], all_sums[:, 0, 1] + all_sums[:, 1, 1], all_sums[:, 1, 0]], axis=1
    ).reshape(groups * seqs, width)
    loss, head_pull = jax.vjp(
        lambda rows, first_w, second_w, bias_w: contrast(rows, first_w, second_w, bias_w, partners),
        all_pooled,
        head_first,
        head_second,
        head_bias,
    )
    back_pooled, grad_head_first, grad_head_second, grad_head_bias = head_pull(jnp.ones_like(loss))
    first_row = dp_rank * seqs
    back_whole = lax.dynamic_index_in_dim(back_pooled, first_row + whole_seq, 0, keepdims=False)
    back_split = lax.dynamic_index_in_dim(back_pooled, first_row + split_seq, 0, keepdims=False)
    back_h_two = weight_whole[:, None] * back_whole[None, :] + weight_split[:, None] * back_split[None, :]

    back_x_two, grad_gain_two, grad_shift_two = normalise_back(back_h_two, norms[4], unit_two, scale_two)
    grad_down = outer(back_x_two, act, width, 0)
    sum_down = lax.psum_scatter(grad_down, "tensor", scatter_dimension=0, tiled=False)
    back_up, grad_bias_up = times(
        back_x_two, all_ffn_down, 0, scale_tile, [act_slope], [parts_shape, bias_tiles.shape]
    )
    grad_up = outer(h_one, back_up, width, 0)
    back_up, grad_up = lax.optimization_barrier((back_up, grad_up))
    sum_up = lax.psum_scatter(grad_up, "tensor", scatter_dimension=0, tiled=False)
    back_h_one = gather_back(back_x_two, [(back_up, all_ffn_up, 0)])
    back_x_one, grad_gain_one, grad_shift_one = normalise_back(back_h_one, norms[2], unit_one, scale_one)

    (back_mixed,) = times(back_x_one, all_attn, 3, keep_tile, [], [mixed.shape])
    back_q, back_k, back_v = attend_call(
        attend_back_kernel,
        slots,
        (queries, keys_all, values, key_bias, mixed, lse, back_mixed),
        (queries.shape, keys_all.shape, values.shape),
    )
    back_keys = gather_back(
        back_x_one, [(back_q, all_attn, 0), (back_k, all_attn, 1), (back_v, all_attn, 2)]
    )
    back_other = lax.ppermute(back_keys[count:], "tensor", swap)
    back_h_zero = back_keys[:count]
    back_h_zero = back_h_zero + jnp.pad(back_other, ((slots, 0), (0, 0)))
    back_embedded, grad_gain_zero, grad_shift_zero = normalise_back(back_h_zero, norms[0], unit_zero, scale_zero)

    def send_back(wanted):
        return pack(wanted, ids, back_embedded, groups, shards).reshape(devices * CAPACITY, cols)

    def add_rows(landed, rows, total):
        target = jnp.where(rows >= 0, rows, vocab_rows)
        return total.at[target].add(landed, mode="drop")

    leaving, back_q, back_k, back_v, back_x_one = lax.optimization_barrier(
        (send_back(wanted_first), back_q, back_k, back_v, back_x_one)
    )
    landed_first = trade(leaving)
    part_rows = 4 * width + slots + SMALL_ROWS
    parts_attn = outer_three(h_zero, h_other, back_q, back_k, back_v, part_rows)
    parts_attn = outer(back_x_one, mixed, part_rows, 3, parts_attn)
    grad_small = jnp.concatenate(
        [
            jnp.stack(
                [
                    grad_gain_zero,
                    grad_shift_zero,
                    grad_gain_one,
                    grad_shift_one,
                    grad_gain_two,
                    grad_shift_two,
                    jnp.sum(back_x_one, axis=0),
                    jnp.sum(back_x_two, axis=0),
                    jnp.sum(back_q, axis=1).reshape(-1),
                    jnp.sum(back_v, axis=1).reshape(-1),
                ]
            ),
            grad_bias_up.reshape(-1, width),
        ],
        axis=0,
    )
    half_rows = jnp.where(side == 0, 1.0, 0.0) * back_embedded[slots:]
    other_rows = back_embedded[slots:] - half_rows
    grad_pos_full = back_embedded[:slots] + jnp.concatenate([half_rows, other_rows], axis=0)
    grad_pos_parts = grad_pos_full.reshape(slots, shards, cols)
    grad_pos_parts = grad_pos_parts.transpose(1, 0, 2)
    small_size = grad_small.size
    small_rows = jnp.pad(grad_small.reshape(-1), (0, SMALL_ROWS * cols - small_size)).reshape(1, SMALL_ROWS, cols)
    small_rows = jnp.broadcast_to(small_rows, (shards, SMALL_ROWS, cols))
    parts_attn = lax.dynamic_update_slice(parts_attn, grad_pos_parts, (0, 4 * width, 0))
    parts_attn = lax.dynamic_update_slice(parts_attn, small_rows, (0, 4 * width + slots, 0))
    first_all = (dp_rank == 0).astype(jnp.float32) * (tp_rank == 0).astype(jnp.float32)
    head_squares = first_all * (squares(grad_head_first) + squares(grad_head_second) + squares(grad_head_bias))
    landed_first, parts_attn, head_squares = lax.optimization_barrier((landed_first, parts_attn, head_squares))
    sum_attn = lax.psum_scatter(parts_attn, "tensor", scatter_dimension=0, tiled=False)
    corner = (lax.broadcasted_iota(jnp.int32, (8, 128), 0) + lax.broadcasted_iota(jnp.int32, (8, 128), 1)) == 0
    tile = jnp.where(corner, head_squares, 0.0)
    (sum_down,), tile = ring_sum([sum_down], tile, groups, shards, 2, 0, 1)
    (sum_up,), squared = ring_sum([sum_up], tile, groups, shards, 2, 0, 3)
    landed_first, sum_up = lax.optimization_barrier((landed_first, sum_up))
    zero_table = jnp.zeros((vocab_rows, cols), jnp.float32)
    grad_embedding = add_rows(landed_first, rows_first, zero_table)

    def give_more(state):
        round_index, total = state
        wanted, rows, _ = serve(round_index)
        return round_index + 1, add_rows(trade(send_back(wanted)), rows, total)

    _, grad_embedding = lax.while_loop(more, give_more, (jnp.int32(1), grad_embedding))

    squared = squared + jnp.where(corner, squares(grad_embedding), 0.0)
    sum_attn, grad_embedding = lax.optimization_barrier((sum_attn, grad_embedding))
    (sum_attn,), squared = ring_sum([sum_attn], squared, groups, shards, 2, SMALL_ROWS, 2)
    sum_small = sum_attn[-SMALL_ROWS:].reshape(-1)[:small_size].reshape(grad_small.shape)
    grad_norms = sum_small[:8]
    grad_bias_qv = lax.dynamic_slice_in_dim(sum_small[8:10], tp_rank * cols, cols, 1)
    grad_bias_up = lax.dynamic_slice_in_dim(sum_small[10:].reshape(-1), tp_rank * hidden, hidden)
    grad_attn = sum_attn[: 4 * width].reshape(4, width, cols)
    grad_ffn_up, grad_ffn_down = sum_up, sum_down
    grad_pos = sum_attn[4 * width : -SMALL_ROWS]

    grad_norm = jnp.sqrt(jnp.sum(squared))
    factor = jnp.minimum(1.0, CLIP_SCALE * math.sqrt(PARAMS) / (grad_norm + 1e-06))
    grad_positions = jnp.pad(grad_pos, ((2, positions.shape[0] - slots - 2), (0, 0)))
    grad_ffn = jnp.stack([grad_ffn_up, grad_ffn_down])
    new_embedding, next_embedding = advance(embedding, mom_embedding, grad_embedding, factor)
    new_positions, next_positions = advance(positions, mom_positions, grad_positions, factor)
    new_attn, next_attn = advance(attn_weights, mom_attn, grad_attn, factor)
    new_ffn, next_ffn = advance(ffn_weights, ffn_momentum, grad_ffn, factor)
    new_bias_qv, next_bias_qv = advance(bias_qv, mom_bias_qv, grad_bias_qv, factor)
    new_bias_up, next_bias_up = advance(bias_up, mom_bias_up, grad_bias_up, factor)
    new_norms, next_norms = advance(norms, mom_norms, grad_norms, factor)
    new_head_first, next_head_first = advance(head_first, mom_head_first, grad_head_first, factor)
    new_head_second, next_head_second = advance(head_second, mom_head_second, grad_head_second, factor)
    new_head_bias, next_head_bias = advance(head_bias, mom_head_bias, grad_head_bias, factor)
    return (
        new_embedding, new_positions, new_attn, new_ffn, new_bias_qv, new_bias_up, new_norms, new_head_first,
        new_head_second, new_head_bias, next_embedding, next_positions, next_attn, next_ffn, next_bias_qv,
        next_bias_up, next_norms, next_head_first, next_head_second, next_head_bias, loss, grad_norm,
    )


def solution(mesh):
    in_specs = (
        P("dp", None),
        P("dp"),
        P(),
        P("dp", "tensor"),
        P(None, "tensor"),
        P(None, None, "tensor"),
        P(None, None, "tensor"),
        P(None, "tensor"),
        P("tensor"),
        P(),
        P(),
        P(),
        P(),
        P("dp", "tensor"),
        P(None, "tensor"),
        P(None, None, "tensor"),
        P(None, None, "tensor"),
        P(None, "tensor"),
        P("tensor"),
        P(),
        P(),
        P(),
        P(),
    )
    out_specs = (
        P("dp", "tensor"),
        P(None, "tensor"),
        P(None, None, "tensor"),
        P(None, None, "tensor"),
        P(None, "tensor"),
        P("tensor"),
        P(),
        P(),
        P(),
        P(),
        P("dp", "tensor"),
        P(None, "tensor"),
        P(None, None, "tensor"),
        P(None, None, "tensor"),
        P(None, "tensor"),
        P("tensor"),
        P(),
        P(),
        P(),
        P(),
        P(),
        P(),
    )
    groups, shards = mesh.shape["dp"], mesh.shape["tensor"]

    def run(*arrays):
        body = on_device
        if 2 * (arrays[0].shape[0] // groups) == 3 * shards:
            body = functools.partial(fast_on_device, groups=groups, shards=shards)
        return jax.shard_map(
            body, mesh=mesh, in_specs=in_specs, out_specs=out_specs, check_vma=False
        )(*arrays)

    return run
```

```python
import functools
import math

import jax
import jax.numpy as jnp
from jax import lax
from jax.experimental import pallas as pl
from jax.experimental.pallas import tpu as pltpu
from jax.sharding import PartitionSpec as P

HEAD_DIM = 64
PARAMS = 65044736


EPS = 1e-05
SOFTMAX_TEMP = 0.1
DECAY = 0.9
RATE = 100000.0
CLIP_SCALE = 1e-06
HIGH = lax.Precision.HIGHEST
PRODUCT = lax.Precision.HIGH
CAPACITY = 88
SMALL_ROWS = 64


def precise_product(left, right):
    return jnp.matmul(left, right, precision=HIGH)


def norm_rows(values, gain, shift):
    center = values - jnp.mean(values, axis=-1, keepdims=True)
    spread = jnp.mean(center * center, axis=-1, keepdims=True)
    return center * lax.rsqrt(spread + EPS) * gain + shift


def attend(normed, lengths, attn, bias_qv):
    seqs, slots, width = normed.shape
    cols = attn.shape[2]
    heads = cols // HEAD_DIM
    queries = (precise_product(normed, attn[0]) + bias_qv[0]).reshape(seqs, slots, heads, HEAD_DIM)
    keys_all = precise_product(normed, attn[1]).reshape(seqs, slots, heads, HEAD_DIM)
    values = (precise_product(normed, attn[2]) + bias_qv[1]).reshape(seqs, slots, heads, HEAD_DIM)
    scores = jnp.einsum("sqhd,skhd->shqk", queries, keys_all, precision=HIGH) / math.sqrt(HEAD_DIM)
    valid = lax.broadcasted_iota(jnp.int32, (seqs, slots), 1) < lengths[:, None]
    scores = jnp.where(valid[:, None, None, :], scores, -1e30)
    probs = jax.nn.softmax(scores, axis=-1)
    mixed = jnp.einsum("shqk,skhd->sqhd", probs, values, precision=HIGH).reshape(seqs, slots, cols)
    return precise_product(mixed, attn[3].T)


def expand(normed, ffn, bias_up):
    hidden = jax.nn.gelu(precise_product(normed, ffn[0]) + bias_up, approximate=False)
    return precise_product(hidden, ffn[1].T)


def contrast(pooled, head_first, head_second, head_bias, partners):
    middle = jax.nn.gelu(precise_product(pooled, head_first) + head_bias, approximate=False)
    output = precise_product(middle, head_second)
    unit_vectors = output * lax.rsqrt(jnp.sum(output * output, axis=-1, keepdims=True) + 1e-06)
    similarity_scores = precise_product(unit_vectors, unit_vectors.T) / SOFTMAX_TEMP
    count = similarity_scores.shape[0]
    index = lax.broadcasted_iota(jnp.int32, (count,), 0)
    similarity_scores = jnp.where(index[:, None] == index[None, :], -1e30, similarity_scores)
    totals = jax.nn.logsumexp(similarity_scores, axis=-1)
    paired_rows = jnp.sum(
        jnp.where(index[None, :] == partners[:, None], similarity_scores, 0.0), axis=-1
    )
    return jnp.sum(totals - paired_rows)


def owner_rows(ids_part, base, vocab_rows):
    local_ids = ids_part - base
    inside = (local_ids >= 0) & (local_ids < vocab_rows)
    return jnp.where(inside, local_ids, vocab_rows)


def advance(weight, moment, grad, factor):
    clipped = factor * grad
    moment_new = DECAY * moment + (1.0 - DECAY) * clipped
    return (weight - RATE * (DECAY * moment_new + (1.0 - DECAY) * clipped), moment_new)


def squares(array):
    return jnp.sum(array * array)


def on_device(
    token_ids,
    lengths,
    partners,
    embedding,
    positions,
    attn_weights,
    ffn_weights,
    bias_qv,
    bias_up,
    norms,
    head_first,
    head_second,
    head_bias,
    mom_embedding,
    mom_positions,
    mom_attn,
    ffn_momentum,
    mom_bias_qv,
    mom_bias_up,
    mom_norms,
    mom_head_first,
    mom_head_second,
    mom_head_bias,
):
    seqs, slots = token_ids.shape
    vocab_rows, cols = embedding.shape
    dp_rank = lax.axis_index("dp")
    tp_rank = lax.axis_index("tensor")
    base = dp_rank * vocab_rows
    all_ids = lax.all_gather(token_ids, "dp", axis=0, tiled=True).reshape(-1)
    padded_table = jnp.concatenate([embedding, jnp.zeros((1, cols), jnp.float32)], axis=0)
    rows_ids = owner_rows(all_ids, base, vocab_rows)
    token_rows = lax.psum_scatter(
        jnp.take(padded_table, rows_ids, axis=0), "dp", scatter_dimension=0, tiled=True
    )
    token_cols = token_rows.reshape(seqs, slots, cols) + positions[2 : slots + 2][None]
    embedded = lax.all_gather(token_cols, "tensor", axis=2, tiled=True)
    h_zero, ln_zero_pull = jax.vjp(norm_rows, embedded, norms[0], norms[1])
    attn_part, attn_pull = jax.vjp(
        lambda normed, weights, biases: attend(normed, lengths, weights, biases),
        h_zero,
        attn_weights,
        bias_qv,
    )
    x_one = h_zero + lax.psum(attn_part, "tensor") + norms[6]
    h_one, ln_one_pull = jax.vjp(norm_rows, x_one, norms[2], norms[3])
    ffn_part, ffn_pull = jax.vjp(expand, h_one, ffn_weights, bias_up)
    x_two = h_one + lax.psum(ffn_part, "tensor") + norms[7]
    h_two, ln_two_pull = jax.vjp(norm_rows, x_two, norms[4], norms[5])
    valid = (lax.broadcasted_iota(jnp.int32, (seqs, slots), 1) < lengths[:, None]).astype(
        jnp.float32
    )
    len_float = lengths.astype(jnp.float32)
    pooled = jnp.sum(h_two * valid[:, :, None], axis=1) / len_float[:, None]
    all_pooled = lax.all_gather(pooled, "dp", axis=0, tiled=True)
    loss, head_pull = jax.vjp(
        lambda rows, first_w, second_w, bias_w: contrast(rows, first_w, second_w, bias_w, partners),
        all_pooled,
        head_first,
        head_second,
        head_bias,
    )
    back_pooled_all, grad_head_first, grad_head_second, grad_head_bias = head_pull(
        jnp.ones_like(loss)
    )
    back_pooled = lax.dynamic_slice_in_dim(back_pooled_all, dp_rank * seqs, seqs)
    back_h_two = valid[:, :, None] * (back_pooled / len_float[:, None])[:, None, :]
    back_x_two, grad_gain_two, grad_shift_two = ln_two_pull(back_h_two)
    back_h_one_part, grad_ffn, grad_bias_up = ffn_pull(back_x_two)
    back_h_one = back_x_two + lax.psum(back_h_one_part, "tensor")
    back_x_one, grad_gain_one, grad_shift_one = ln_one_pull(back_h_one)
    back_h_zero_part, grad_attn, grad_bias_qv = attn_pull(back_x_one)
    back_h_zero = back_x_one + lax.psum(back_h_zero_part, "tensor")
    back_embedded, grad_gain_zero, grad_shift_zero = ln_zero_pull(back_h_zero)
    back_cols = lax.dynamic_slice_in_dim(back_embedded, tp_rank * cols, cols, 2)
    grad_positions = jnp.pad(
        jnp.sum(back_cols, axis=0), ((2, positions.shape[0] - slots - 2), (0, 0))
    )
    grad_norms = jnp.stack(
        [
            grad_gain_zero,
            grad_shift_zero,
            grad_gain_one,
            grad_shift_one,
            grad_gain_two,
            grad_shift_two,
            jnp.sum(back_x_one, axis=(0, 1)),
            jnp.sum(back_x_two, axis=(0, 1)),
        ]
    )
    back_flat = back_cols.reshape(seqs * slots, cols)
    target = owner_rows(all_ids, base, vocab_rows)
    grad_embedding = jax.ops.segment_sum(
        lax.all_gather(back_flat, "dp", axis=0, tiled=True), target, num_segments=vocab_rows + 1
    )[:vocab_rows]
    first_dp = (dp_rank == 0).astype(jnp.float32)
    first_all = first_dp * (tp_rank == 0).astype(jnp.float32)
    grad_attn, grad_ffn, grad_positions, grad_bias_qv, grad_bias_up, grad_norms = lax.psum(
        (grad_attn, grad_ffn, grad_positions, grad_bias_qv, grad_bias_up, grad_norms), "dp"
    )
    big_squares = first_dp * (squares(grad_attn) + squares(grad_ffn))
    local_squares = (
        big_squares
        + squares(grad_embedding)
        + first_dp * (squares(grad_positions) + squares(grad_bias_qv) + squares(grad_bias_up))
        + first_all
        * (
            squares(grad_norms)
            + squares(grad_head_first)
            + squares(grad_head_second)
            + squares(grad_head_bias)
        )
    )
    total_squares = lax.psum(local_squares, ("dp", "tensor"))
    grad_norm = jnp.sqrt(total_squares)
    factor = jnp.minimum(1.0, CLIP_SCALE * math.sqrt(PARAMS) / (grad_norm + 1e-06))
    new_attn, next_attn = advance(attn_weights, mom_attn, grad_attn, factor)
    new_ffn, next_ffn = advance(ffn_weights, ffn_momentum, grad_ffn, factor)
    new_embedding, next_embedding = advance(embedding, mom_embedding, grad_embedding, factor)
    new_positions, next_positions = advance(positions, mom_positions, grad_positions, factor)
    new_bias_qv, next_bias_qv = advance(bias_qv, mom_bias_qv, grad_bias_qv, factor)
    new_bias_up, next_bias_up = advance(bias_up, mom_bias_up, grad_bias_up, factor)
    new_norms, next_norms = advance(norms, mom_norms, grad_norms, factor)
    new_head_first, next_head_first = advance(head_first, mom_head_first, grad_head_first, factor)
    new_head_second, next_head_second = advance(
        head_second, mom_head_second, grad_head_second, factor
    )
    new_head_bias, next_head_bias = advance(head_bias, mom_head_bias, grad_head_bias, factor)
    return (
        new_embedding,
        new_positions,
        new_attn,
        new_ffn,
        new_bias_qv,
        new_bias_up,
        new_norms,
        new_head_first,
        new_head_second,
        new_head_bias,
        next_embedding,
        next_positions,
        next_attn,
        next_ffn,
        next_bias_qv,
        next_bias_up,
        next_norms,
        next_head_first,
        next_head_second,
        next_head_bias,
        loss,
        grad_norm,
    )


MESH = pl.DeviceIdType.MESH
VMEM = pl.BlockSpec(memory_space=pltpu.VMEM)


def cube_partners(groups, shards):
    dp, tp = lax.axis_index("dp"), lax.axis_index("tensor")
    partners = []
    for size, at in ((shards, 1), (groups, 0)):
        bit = 1
        while bit < size:
            here = (dp, tp)[at]
            there = here + bit * (1 - 2 * ((here // bit) % 2))
            partners.append((dp, there) if at else (there, tp))
            bit *= 2
    return partners


def greet(partners):
    barrier = pltpu.get_barrier_semaphore()
    for partner in partners:
        pl.semaphore_signal(barrier, inc=1, device_id=partner, device_id_type=MESH)
    pl.semaphore_wait(barrier, len(partners))


def cube_stages(groups, shards):
    return (groups * shards).bit_length() - 1


def meet_kernel(groups, shards, x_ref, o_ref, held, send_sem, recv_sem):
    dp, tp = lax.axis_index("dp"), lax.axis_index("tensor")
    near = [(dp, (tp + k) % shards) for k in range(1, shards)]
    far = [((dp + k) % groups, tp) for k in range(1, groups)]
    greet([*near, *far])
    me = dp * shards + tp
    held[pl.ds(me, 1)] = x_ref[...][None]
    at = 0
    for partners, mine in ((near, pl.ds(me, 1)), (far, pl.ds(dp * shards, shards))):
        copies = []
        for partner in partners:
            copy = pltpu.make_async_remote_copy(
                src_ref=held.at[mine],
                dst_ref=held.at[mine],
                send_sem=send_sem.at[at],
                recv_sem=recv_sem.at[at],
                device_id=partner,
                device_id_type=MESH,
            )
            copy.start()
            copies.append(copy)
            at += 1
        for copy in copies:
            copy.wait()
    o_ref[...] = held[...]


def meet(block, groups, shards, collective_id):
    shape = (groups * shards, *block.shape)
    return pl.pallas_call(
        functools.partial(meet_kernel, groups, shards),
        out_shape=jax.ShapeDtypeStruct(shape, block.dtype),
        in_specs=[VMEM],
        out_specs=VMEM,
        scratch_shapes=[
            pltpu.VMEM(shape, block.dtype),
            pltpu.SemaphoreType.DMA((groups + shards - 2,)),
            pltpu.SemaphoreType.DMA((groups + shards - 2,)),
        ],
        compiler_params=pltpu.CompilerParams(collective_id=collective_id, has_side_effects=True),
    )(block)


def fold_squares(block):
    block = block * block
    folded = jnp.sum(block.reshape(block.shape[0] // 8, 8, block.shape[1]), axis=0)
    total = folded[:, :128]
    for start in range(128, block.shape[1], 128):
        total = total + folded[:, start : start + 128]
    return total


def ring_kernel(groups, shards, parts, arrays, shared_rows, *refs):
    refs = list(refs)
    inputs = [refs.pop(0) for _ in range(arrays)]
    base = refs.pop(0)
    outputs = [refs.pop(0) for _ in range(arrays)]
    squares_ref = refs.pop(0)
    slots = [refs.pop(0) for _ in range(arrays)]
    send_sem, recv_sem, sent, landed, cube_send, cube_recv = refs
    depth = groups // 2
    dp, tp = lax.axis_index("dp"), lax.axis_index("tensor")
    side, level = dp % 2, dp // 2
    place = level * (1 - side) + (groups - 1 - level) * side

    def device_at(spot):
        spot = (spot + groups) % groups
        far = spot // depth
        return (2 * (spot * (1 - far) + (groups - 1 - spot) * far) + far, tp)

    partners = cube_partners(groups, shards) if shared_rows else []
    greet([device_at(place + 1), device_at(place - 1), *partners])
    streams = []
    for array in range(arrays):
        tiles = inputs[array].shape[1] // 8
        edges = [8 * (tiles * part // (2 * parts)) for part in range(2 * parts + 1)]
        for part in range(2 * parts):
            streams.append((array, 1 - 2 * (part % 2), edges[part], edges[part + 1] - edges[part]))

    def chunk(step, way):
        return (place + groups * 2 - way * step) % groups

    copies = []

    def send(source, target, send_at, recv_at, device):
        copy = pltpu.make_async_remote_copy(
            src_ref=source,
            dst_ref=target,
            send_sem=send_at,
            recv_sem=recv_at,
            device_id=device,
            device_id_type=MESH,
        )
        copy.start()
        copies.append(copy)
        return copy

    def pass_on(index, step, source, target):
        device = device_at(place + streams[index][1])
        return send(source, target, send_sem.at[index, step], recv_sem.at[index, step], device)

    flying = [None] * len(streams)
    for step in range(groups - 1):
        for index, (array, way, start, size) in enumerate(streams):
            rows = pl.ds(start, size)
            if step == 0:
                source = inputs[array].at[chunk(0, way), rows]
            else:
                flying[index].wait_recv()
                source = slots[array].at[step - 1, rows]
                source[...] = source[...] + inputs[array][chunk(step, way), rows]
            flying[index] = pass_on(index, step, source, slots[array].at[step, rows])
    total = base[...]
    crossing = None
    for step in range(groups - 1):
        for index, (array, way, start, size) in enumerate(streams):
            rows = pl.ds(start, size)
            flying[index].wait_recv()
            now = chunk(groups - 1 + step, way)
            if step == 0:
                block = slots[array][groups - 2, rows] + inputs[array][now, rows]
                outputs[array][now, rows] = block
                if shared_rows:
                    depth_rows = inputs[array].shape[1]
                    limit = groups * depth_rows - shared_rows * (1 - (shards - tp) // shards)
                    at = now * depth_rows + start + lax.broadcasted_iota(jnp.int32, block.shape, 0)
                    block = jnp.where(at < limit, block, 0.0)
                total = total + fold_squares(block)
            out = outputs[array].at[now, rows]
            flying[index] = pass_on(index, groups - 1 + step, out, out)
        if step <= len(partners) and partners:
            if step == 0:
                sent[0] = total
            else:
                crossing.wait_recv()
                sent[step] = sent[step - 1] + landed[step - 1]
            if step < len(partners):
                crossing = send(
                    sent.at[step], landed.at[step], cube_send.at[step], cube_recv.at[step], partners[step]
                )
    squares_ref[...] = sent[len(partners)] if partners else total
    for copy in flying:
        copy.wait_recv()
    for copy in copies:
        copy.wait_send()


def ring_sum(arrays, base, groups, shards, parts, shared_rows, collective_id):
    blocks = [array.reshape(groups, array.shape[0] // groups, array.shape[1]) for array in arrays]
    streams = 2 * parts * len(blocks)
    steps = 2 * (groups - 1)
    stages = cube_stages(groups, shards)
    *sums, squared = pl.pallas_call(
        functools.partial(ring_kernel, groups, shards, parts, len(blocks), shared_rows),
        out_shape=[jax.ShapeDtypeStruct(block.shape, block.dtype) for block in [*blocks, base]],
        in_specs=[VMEM] * (len(blocks) + 1),
        out_specs=[VMEM] * (len(blocks) + 1),
        scratch_shapes=[
            *[pltpu.VMEM((groups - 1, *block.shape[1:]), block.dtype) for block in blocks],
            pltpu.SemaphoreType.DMA((streams, steps)),
            pltpu.SemaphoreType.DMA((streams, steps)),
            pltpu.VMEM((stages + 1, *base.shape), base.dtype),
            pltpu.VMEM((stages, *base.shape), base.dtype),
            pltpu.SemaphoreType.DMA((stages,)),
            pltpu.SemaphoreType.DMA((stages,)),
        ],
        compiler_params=pltpu.CompilerParams(
            collective_id=collective_id, has_side_effects=True, vmem_limit_bytes=48 << 20
        ),
        cost_estimate=pl.CostEstimate(flops=1, bytes_accessed=1024, transcendentals=0),
    )(*blocks, base)
    return [total.reshape(array.shape) for total, array in zip(sums, arrays)], squared


def spread_kernel(
    groups, w_ref, small_ref, o_ref, rows_ref, local_sem, pair_send, pair_recv, ring_send, ring_recv, core_send, core_recv
):
    depth = groups // 2
    dp, tp = lax.axis_index("dp"), lax.axis_index("tensor")
    far = tp + 2 - 4 * (tp // 2)
    core = (dp, tp + 1 - 2 * (tp % 2))
    side, level = dp % 2, dp // 2
    place = level * (1 - side) + (groups - 1 - level) * side

    def index_at(spot):
        spot = (spot + groups) % groups
        back = spot // depth
        return 2 * (spot * (1 - back) + (groups - 1 - spot) * back) + back

    def send(source, target, send_sem, recv_sem, device):
        copy = pltpu.make_async_remote_copy(
            src_ref=source,
            dst_ref=target,
            send_sem=send_sem,
            recv_sem=recv_sem,
            device_id=device,
            device_id_type=MESH,
        )
        copy.start()
        return copy

    greet([(index_at(place + 1), tp), (index_at(place - 1), tp), core, (dp, far)])
    cross = send(w_ref.at[dp], o_ref.at[tp, dp], pair_send.at[0], pair_recv.at[0], (dp, far))
    near = send(w_ref, o_ref.at[tp], pair_send.at[1], pair_recv.at[1], core)
    cross_rows = send(small_ref, rows_ref.at[tp], pair_send.at[2], pair_recv.at[2], (dp, far))
    near_rows = send(small_ref, rows_ref.at[tp], pair_send.at[3], pair_recv.at[3], core)
    local = pltpu.make_async_copy(w_ref, o_ref.at[tp], local_sem)
    local.start()
    rows_ref[tp] = small_ref[...]
    cross.wait_recv()
    lanes = ring_send.shape[0]
    size = w_ref.shape[1] // lanes
    flying = [None] * lanes
    started = [cross, cross_rows]
    handed = [near, near_rows]
    for step in range(groups):
        for lane in range(lanes):
            way = 1 - 2 * (lane % 2)
            block = o_ref.at[far, index_at(place + groups - way * step), pl.ds(lane * size, size)]
            if step > 0:
                flying[lane].wait_recv()
            if step < groups - 1:
                flying[lane] = send(
                    block, block, ring_send.at[lane, step], ring_recv.at[lane, step], (index_at(place + way), tp)
                )
                started.append(flying[lane])
            handed.append(send(block, block, core_send.at[lane, step], core_recv.at[lane, step], core))
    cross_rows.wait_recv()
    handed.append(send(rows_ref.at[far], rows_ref.at[far], pair_send.at[4], pair_recv.at[4], core))
    for copy in handed:
        copy.wait_recv()
        copy.wait_send()
    for copy in started:
        copy.wait_send()
    local.wait()


def spread(weight, small, groups, collective_id):
    rows = weight.shape[0] // groups
    lanes = 4
    gathered, gathered_rows = pl.pallas_call(
        functools.partial(spread_kernel, groups),
        out_shape=[
            jax.ShapeDtypeStruct((4, groups, rows, weight.shape[1]), weight.dtype),
            jax.ShapeDtypeStruct((4, *small.shape), small.dtype),
        ],
        in_specs=[pl.BlockSpec(memory_space=pl.ANY), VMEM],
        out_specs=[VMEM, VMEM],
        scratch_shapes=[
            pltpu.SemaphoreType.DMA,
            pltpu.SemaphoreType.DMA((5,)),
            pltpu.SemaphoreType.DMA((5,)),
            pltpu.SemaphoreType.DMA((lanes, groups - 1)),
            pltpu.SemaphoreType.DMA((lanes, groups - 1)),
            pltpu.SemaphoreType.DMA((lanes, groups)),
            pltpu.SemaphoreType.DMA((lanes, groups)),
        ],
        compiler_params=pltpu.CompilerParams(
            collective_id=collective_id, has_side_effects=True, vmem_limit_bytes=32 << 20
        ),
        cost_estimate=pl.CostEstimate(flops=1, bytes_accessed=1024, transcendentals=0),
    )(weight.reshape(groups, rows, weight.shape[1]), small)
    return gathered.reshape(4, *weight.shape), gathered_rows


def halves(array):
    high = array.astype(jnp.bfloat16)
    return high, (array - high.astype(jnp.float32)).astype(jnp.bfloat16)


def dot_rows(left, right):
    return lax.dot_general(left, right, (((1,), (1,)), ((), ())), preferred_element_type=jnp.float32)


def dot_plain(left, right):
    return lax.dot_general(left, right, (((1,), (0,)), ((), ())), preferred_element_type=jnp.float32)


def one_head(array, head):
    lane = lax.broadcasted_iota(jnp.int32, array.shape, 1)
    return jnp.where(lane // HEAD_DIM == head, array, 0.0)


def score_tile(twice_k, low_k, high_q, low_q, bias):
    wide = dot_rows(twice_k, jnp.concatenate([high_q, low_q], axis=1))
    return wide + dot_rows(low_k, high_q) + bias


def attend_kernel(slots, tile, q_ref, k_ref, v_ref, bias_ref, o_ref, lse_ref):
    scale = 1.0 / math.sqrt(HEAD_DIM)
    high_k, low_k = halves(k_ref[0])
    twice_k = jnp.concatenate([high_k, high_k], axis=1)
    high_v, low_v = halves(v_ref[0].T)
    def scores_of(start):
        first = 0 if start < slots else slots
        keys = slice(first, first + slots)
        found = []
        for head in range(2):
            high_q, low_q = halves(one_head(q_ref[0, pl.ds(start, tile)] * scale, head))
            found.append(score_tile(twice_k[keys], low_k[keys], high_q, low_q, bias_ref[pl.ds(first, slots)]))
        return found

    starts = list(range(0, q_ref.shape[1], tile))
    ready = scores_of(starts[0])
    for index, start in enumerate(starts):
        rows = pl.ds(start, tile)
        first = 0 if start < slots else slots
        keys = slice(first, first + slots)
        score_pair = ready
        if index + 1 < len(starts):
            ready = scores_of(starts[index + 1])
        peaks = [jnp.max(jnp.max(s.reshape(8, -1, tile), axis=0), axis=0, keepdims=True) for s in score_pair]
        pairs = [jnp.exp(s - p) for s, p in zip(score_pair, peaks)]
        found = []
        for head in range(2):
            peak, probs = peaks[head], pairs[head]
            total = jnp.sum(jnp.sum(probs.reshape(8, -1, tile), axis=0), axis=0, keepdims=True)
            lse_ref[0, pl.ds(head, 1), rows] = peak + jnp.log(total)
            high_p, low_p = halves(probs)
            lanes = slice(head * HEAD_DIM, (head + 1) * HEAD_DIM)
            both = jnp.concatenate([high_v[lanes, keys], low_v[lanes, keys]], axis=0)
            wide = dot_plain(both, high_p)
            mixed = wide[:HEAD_DIM] + wide[HEAD_DIM:] + dot_plain(high_v[lanes, keys], low_p)
            found.append(mixed / total)
        o_ref[0, rows] = jnp.concatenate(found, axis=0).T


def attend_back_kernel(slots, tile, q_ref, k_ref, v_ref, bias_ref, o_ref, lse_ref, d_ref, dq_ref, dk_ref, dv_ref):
    scale = 1.0 / math.sqrt(HEAD_DIM)
    high_k, low_k = halves(k_ref[0])
    twice_k = jnp.concatenate([high_k, high_k], axis=1)
    high_v, low_v = halves(v_ref[0])
    twice_v = jnp.concatenate([high_v, high_v], axis=1)
    high_kt, low_kt = halves(k_ref[0].T)
    ones = jnp.ones((8, 2 * HEAD_DIM), jnp.bfloat16)
    lanes = 2 * HEAD_DIM
    for first in (0, slots):
        keys = slice(first, first + slots)
        key_rows = pl.ds(first, slots)
        for start in range(first, min(first + slots, q_ref.shape[1]), tile):
            rows = pl.ds(start, tile)
            back_qt = []
            for head in range(2):
                high_q, low_q = halves(one_head(q_ref[0, rows] * scale, head))
                back = one_head(d_ref[0, rows], head)
                high_d, low_d = halves(back)
                scores = score_tile(twice_k[keys], low_k[keys], high_q, low_q, bias_ref[key_rows])
                probs = jnp.exp(scores - lse_ref[0, pl.ds(head, 1), rows])
                high_x, low_x = halves(back * o_ref[0, rows])
                inner = (dot_rows(ones, high_x) + dot_rows(ones, low_x))[:1]
                back_s = probs * (score_tile(twice_v[keys], low_v[keys], high_d, low_d, 0.0) - inner)
                high_p, low_p = halves(probs)
                high_s, low_s = halves(back_s)
                wide = dot_plain(high_p, jnp.concatenate([high_d, low_d], axis=1))
                back_v = wide[:, :lanes] + wide[:, lanes:] + dot_plain(low_p, high_d)
                wide = dot_plain(high_s, jnp.concatenate([high_q, low_q], axis=1))
                back_k = wide[:, :lanes] + wide[:, lanes:] + dot_plain(low_s, high_q)
                if start == first and head == 0:
                    dv_ref[0, key_rows] = back_v
                    dk_ref[0, key_rows] = back_k
                else:
                    dv_ref[0, key_rows] += back_v
                    dk_ref[0, key_rows] += back_k
                mine = slice(head * HEAD_DIM, (head + 1) * HEAD_DIM)
                both = jnp.concatenate([high_kt[mine, keys], low_kt[mine, keys]], axis=0)
                wide = dot_plain(both, high_s)
                back_qt.append(wide[:HEAD_DIM] + wide[HEAD_DIM:] + dot_plain(high_kt[mine, keys], low_s))
            dq_ref[0, rows] = jnp.concatenate(back_qt, axis=0).T * scale


def attend_call(kernel, slots, inputs, outputs):
    lanes = 2 * HEAD_DIM
    queries = inputs[0]
    per_shard = queries.shape[2] // lanes
    pairs = queries.shape[0] * per_shard

    def spec(shape):
        if shape[1] == 1:
            return pl.BlockSpec(shape, lambda i: (0, 0))
        if shape[1] == 2:
            return pl.BlockSpec((1, *shape[1:]), lambda i: (i, 0, 0))
        return pl.BlockSpec((1, shape[1], lanes), lambda i: (i // per_shard, 0, i % per_shard))

    return pl.pallas_call(
        functools.partial(kernel, slots, slots // 2),
        grid=(pairs,),
        in_specs=[spec(x.shape) for x in inputs],
        out_specs=[spec(shape) for shape in outputs],
        out_shape=[jax.ShapeDtypeStruct(shape, jnp.float32) for shape in outputs],
        compiler_params=pltpu.CompilerParams(vmem_limit_bytes=48 << 20),
        cost_estimate=pl.CostEstimate(flops=1, bytes_accessed=1024, transcendentals=0),
    )(*inputs)


WIDE = 512


def dot_three(high_left, low_left, right, dot):
    high, low = halves(right)
    return dot(high_left, high) + dot(high_left, low) + dot(low_left, high)


def times_kernel(finish, extras, x_ref, w_ref, *refs):
    more, outs, (high, low) = refs[:extras], refs[extras:-2], refs[-2:]

    @pl.when((pl.program_id(0) == 0) & (pl.program_id(1) == 0))
    def _():
        high[...], low[...] = halves(x_ref[...])

    weight = w_ref[...].reshape(w_ref.shape[-2], w_ref.shape[-1])
    finish(dot_three(high[...], low[...], weight, dot_plain), more, outs)


def times(x, w, which, finish, extras, outs):
    shards, depth, columns = w.shape[0], w.shape[-2], w.shape[-1]
    rows, wide = x.shape[0], min(WIDE, columns)
    if w.ndim == 4:
        w_spec = pl.BlockSpec((1, 1, depth, wide), lambda j, c: (j, which, 0, c))
    else:
        w_spec = pl.BlockSpec((1, depth, wide), lambda j, c: (j, 0, c))

    def spec(shape):
        return pl.BlockSpec((1, shape[1], wide), lambda j, c: (j, 0, c))

    results = pl.pallas_call(
        functools.partial(times_kernel, finish, len(extras)),
        grid=(shards, columns // wide),
        in_specs=[pl.BlockSpec((rows, depth), lambda j, c: (0, 0)), w_spec, *[spec(e.shape) for e in extras]],
        out_specs=[spec(shape) for shape in outs],
        out_shape=[jax.ShapeDtypeStruct(shape, jnp.float32) for shape in outs],
        scratch_shapes=[pltpu.VMEM((rows, depth), jnp.bfloat16)] * 2,
        compiler_params=pltpu.CompilerParams(vmem_limit_bytes=48 << 20),
        cost_estimate=pl.CostEstimate(flops=1, bytes_accessed=1024, transcendentals=0),
    )(x, w, *extras)
    return results


def keep_tile(tile, more, outs):
    outs[0][0] = tile


def add_row(tile, more, outs):
    outs[0][0] = tile + more[0][0]


def gelu_tile(tile, more, outs):
    outs[0][0], outs[1][0] = gelu_both(tile + more[0][0])


def scale_tile(tile, more, outs):
    tile = tile * more[0][0]
    outs[0][0] = tile
    outs[1][0] = jnp.sum(tile, axis=0, keepdims=True)


def project_kernel(count, x_ref, y_ref, wq_ref, wk_ref, wv_ref, bq_ref, bv_ref, q_ref, k_ref, v_ref, high, low):
    @pl.when(pl.program_id(0) == 0)
    def _():
        high[:count], low[:count] = halves(x_ref[...])
        high[count:], low[count:] = halves(y_ref[...])

    q_ref[0] = dot_three(high[:count], low[:count], wq_ref[0, 0], dot_plain) + bq_ref[0]
    k_ref[0] = dot_three(high[...], low[...], wk_ref[0, 0], dot_plain)
    v_ref[0] = dot_three(high[...], low[...], wv_ref[0, 0], dot_plain) + bv_ref[0]


def project(x, y, w, bias_q, bias_v):
    count, depth = x.shape
    rows = count + y.shape[0]
    shards, _, _, columns = w.shape

    def weight(which):
        return pl.BlockSpec((1, 1, depth, columns), lambda j: (j, which, 0, 0))

    def tile(height):
        return pl.BlockSpec((1, height, columns), lambda j: (j, 0, 0))

    return pl.pallas_call(
        functools.partial(project_kernel, count),
        grid=(shards,),
        in_specs=[
            pl.BlockSpec(x.shape, lambda j: (0, 0)),
            pl.BlockSpec(y.shape, lambda j: (0, 0)),
            *[weight(which) for which in range(3)],
            tile(1),
            tile(1),
        ],
        out_specs=[tile(count), tile(rows), tile(rows)],
        out_shape=[jax.ShapeDtypeStruct((shards, n, columns), jnp.float32) for n in (count, rows, rows)],
        scratch_shapes=[pltpu.VMEM((rows, depth), jnp.bfloat16)] * 2,
        compiler_params=pltpu.CompilerParams(vmem_limit_bytes=48 << 20),
        cost_estimate=pl.CostEstimate(flops=1, bytes_accessed=1024, transcendentals=0),
    )(x, y, w, w, w, bias_q, bias_v)


def gather_back_kernel(count, base_ref, *refs):
    out = refs[-1]

    @pl.when((pl.program_id(0) == 0) & (pl.program_id(1) == 0))
    def _():
        filled = base_ref.shape[0]
        out[:filled] = base_ref[...]
        if filled < out.shape[0]:
            out[filled:] = jnp.zeros((out.shape[0] - filled, out.shape[1]), jnp.float32)

    for a_ref, w_ref in zip(refs[:count], refs[count : 2 * count]):
        high, low = halves(a_ref[0])
        weight = w_ref[...].reshape(w_ref.shape[-2], w_ref.shape[-1])
        rows = pl.ds(0, a_ref.shape[1])
        out[rows] += dot_three(high, low, weight, dot_rows)


def gather_back(base, terms):
    arrays = [array for array, _, _ in terms]
    shards, _, columns = arrays[0].shape
    wide = min(WIDE, columns)
    total = (max(array.shape[1] for array in arrays), base.shape[1])

    def w_spec(w, which):
        if w.ndim == 4:
            return pl.BlockSpec((1, 1, w.shape[-2], wide), lambda j, c: (j, which, 0, c))
        return pl.BlockSpec((1, w.shape[-2], wide), lambda j, c: (j, 0, c))

    return pl.pallas_call(
        functools.partial(gather_back_kernel, len(terms)),
        grid=(shards, columns // wide),
        in_specs=[
            pl.BlockSpec(base.shape, lambda j, c: (0, 0)),
            *[pl.BlockSpec((1, a.shape[1], wide), lambda j, c: (j, 0, c)) for a in arrays],
            *[w_spec(w, which) for _, w, which in terms],
        ],
        out_specs=pl.BlockSpec(total, lambda j, c: (0, 0)),
        out_shape=jax.ShapeDtypeStruct(total, jnp.float32),
        compiler_params=pltpu.CompilerParams(vmem_limit_bytes=48 << 20),
        cost_estimate=pl.CostEstimate(flops=1, bytes_accessed=1024, transcendentals=0),
    )(base, *arrays, *[w for _, w, _ in terms])


def outer_kernel(x_ref, d_ref, *refs):
    out, high, low = refs[-3:]

    @pl.when((pl.program_id(0) == 0) & (pl.program_id(1) == 0))
    def _():
        high[...], low[...] = halves(x_ref[...].T)

    out[0] = dot_three(high[...], low[...], d_ref[0], dot_plain)


def outer(x, d, rows, at, into=None):
    tokens, depth = x.shape
    shards, _, columns = d.shape
    wide = min(WIDE, columns)
    held = [] if into is None else [into]
    return pl.pallas_call(
        outer_kernel,
        grid=(shards, columns // wide),
        in_specs=[
            pl.BlockSpec((tokens, depth), lambda j, c: (0, 0)),
            pl.BlockSpec((1, tokens, wide), lambda j, c: (j, 0, c)),
            *[pl.BlockSpec(memory_space=pl.ANY) for _ in held],
        ],
        out_specs=pl.BlockSpec((1, depth, wide), lambda j, c: (j, at, c)),
        out_shape=jax.ShapeDtypeStruct((shards, rows, columns), jnp.float32),
        scratch_shapes=[pltpu.VMEM((depth, tokens), jnp.bfloat16)] * 2,
        input_output_aliases={2: 0} if held else {},
        compiler_params=pltpu.CompilerParams(vmem_limit_bytes=48 << 20),
        cost_estimate=pl.CostEstimate(flops=1, bytes_accessed=1024, transcendentals=0),
    )(x, d, *held)


def outer_three_kernel(count, x_ref, y_ref, q_ref, k_ref, v_ref, out, high, low):
    @pl.when(pl.program_id(0) == 0)
    def _():
        high[:, :count], low[:, :count] = halves(x_ref[...].T)
        high[:, count:], low[:, count:] = halves(y_ref[...].T)

    depth = high.shape[0]
    out[0, pl.ds(0, depth)] = dot_three(high[:, :count], low[:, :count], q_ref[0], dot_plain)
    out[0, pl.ds(depth, depth)] = dot_three(high[...], low[...], k_ref[0], dot_plain)
    out[0, pl.ds(2 * depth, depth)] = dot_three(high[...], low[...], v_ref[0], dot_plain)


def outer_three(x, y, back_q, back_k, back_v, rows):
    shards, tokens, columns = back_k.shape
    count, depth = x.shape

    def tile(height):
        return pl.BlockSpec((1, height, columns), lambda j: (j, 0, 0))

    return pl.pallas_call(
        functools.partial(outer_three_kernel, count),
        grid=(shards,),
        in_specs=[
            pl.BlockSpec(x.shape, lambda j: (0, 0)),
            pl.BlockSpec(y.shape, lambda j: (0, 0)),
            tile(count),
            tile(tokens),
            tile(tokens),
        ],
        out_specs=tile(3 * depth),
        out_shape=jax.ShapeDtypeStruct((shards, rows, columns), jnp.float32),
        scratch_shapes=[pltpu.VMEM((depth, tokens), jnp.bfloat16)] * 2,
        compiler_params=pltpu.CompilerParams(vmem_limit_bytes=48 << 20),
        cost_estimate=pl.CostEstimate(flops=1, bytes_accessed=1024, transcendentals=0),
    )(x, y, back_q, back_k, back_v)


def thirds(array):
    high, rest = array.astype(jnp.bfloat16), None
    rest = array - high.astype(jnp.float32)
    middle = rest.astype(jnp.bfloat16)
    return high, middle, (rest - middle.astype(jnp.float32)).astype(jnp.bfloat16)


def select_rows(column, row, block):
    chosen = jnp.where(column == row, 1.0, 0.0).astype(jnp.bfloat16)
    high, middle, low = thirds(block)
    return dot_plain(chosen, high) + dot_plain(chosen, middle) + dot_plain(chosen, low)


def pack_kernel(wanted_ref, ids_ref, x_ref, o_ref):
    o_ref[...] = select_rows(wanted_ref[...], ids_ref[...], x_ref[...]).reshape(o_ref.shape)


def pack(wanted, ids, rows, groups, shards):
    cols = rows.shape[1] // shards
    return pl.pallas_call(
        pack_kernel,
        grid=(shards,),
        in_specs=[
            pl.BlockSpec((wanted.shape[0], 1), lambda j: (0, 0)),
            pl.BlockSpec((1, ids.shape[0]), lambda j: (0, 0)),
            pl.BlockSpec((ids.shape[0], cols), lambda j: (0, j)),
        ],
        out_specs=pl.BlockSpec((groups, 1, CAPACITY, cols), lambda j: (0, j, 0, 0)),
        out_shape=jax.ShapeDtypeStruct((groups, shards, CAPACITY, cols), jnp.float32),
        compiler_params=pltpu.CompilerParams(vmem_limit_bytes=32 << 20),
    )(wanted[:, None], ids[None, :], rows)


def expand_kernel(ids_ref, wanted_ref, x_ref, o_ref):
    block = x_ref[...].reshape(wanted_ref.shape[1], x_ref.shape[-1])
    o_ref[...] = select_rows(ids_ref[...], wanted_ref[...], block)


def expand_rows(ids, wanted, landed):
    groups, shards, _, cols = landed.shape
    return pl.pallas_call(
        expand_kernel,
        grid=(shards,),
        in_specs=[
            pl.BlockSpec((ids.shape[0], 1), lambda j: (0, 0)),
            pl.BlockSpec((1, wanted.shape[0]), lambda j: (0, 0)),
            pl.BlockSpec((groups, 1, CAPACITY, cols), lambda j: (0, j, 0, 0)),
        ],
        out_specs=pl.BlockSpec((ids.shape[0], cols), lambda j: (0, j)),
        out_shape=jax.ShapeDtypeStruct((ids.shape[0], shards * cols), jnp.float32),
        compiler_params=pltpu.CompilerParams(vmem_limit_bytes=32 << 20),
    )(ids[:, None], wanted[None, :], landed)


def normalise(values):
    center = values - jnp.mean(values, axis=-1, keepdims=True)
    scale = lax.rsqrt(jnp.mean(center * center, axis=-1, keepdims=True) + EPS)
    return center * scale, scale


def normalise_back(back, gain, unit, scale):
    inner = back * gain
    grad = scale * (
        inner
        - jnp.mean(inner, axis=-1, keepdims=True)
        - unit * jnp.mean(inner * unit, axis=-1, keepdims=True)
    )
    return grad, jnp.sum(back * unit, axis=0), jnp.sum(back, axis=0)


def gelu_both(values):
    cdf = 0.5 * (1.0 + lax.erf(values * math.sqrt(0.5)))
    pdf = jnp.exp(-0.5 * values * values) * (1.0 / math.sqrt(2.0 * math.pi))
    return values * cdf, cdf + values * pdf


def product(subscripts, left, right):
    return jnp.einsum(subscripts, left, right, precision=PRODUCT)


def request_lists(ids, vocab_rows, owners):
    count = ids.shape[0]
    index = lax.broadcasted_iota(jnp.int32, (count,), 0)
    earlier = index[None, :] < index[:, None]
    same = (ids[None, :] == ids[:, None]) & earlier
    first = jnp.logical_not(jnp.any(same, axis=1))
    owner = ids // vocab_rows
    ahead = (owner[None, :] == owner[:, None]) & earlier & first[None, :]
    rank = jnp.sum(ahead.astype(jnp.int32), axis=1)
    return owner, jnp.where(first, rank, -1)


def round_list(ids, owner, rank, round_index, owners):
    place = rank - round_index * CAPACITY
    inside = (rank >= 0) & (place >= 0) & (place < CAPACITY)
    place = jnp.where(inside, owner * CAPACITY + place, -1)
    wanted = lax.broadcasted_iota(jnp.int32, (owners * CAPACITY, 1), 0)
    return jnp.sum(jnp.where(place[None, :] == wanted, ids[None, :] + 1, 0), axis=1) - 1


def trade(block):
    return lax.all_to_all(block, ("dp", "tensor"), 0, 0, tiled=True)


def fast_on_device(
    token_ids, lengths, partners, embedding, positions, attn_weights, ffn_weights, bias_qv, bias_up, norms,
    head_first, head_second, head_bias, mom_embedding, mom_positions, mom_attn, ffn_momentum, mom_bias_qv,
    mom_bias_up, mom_norms, mom_head_first, mom_head_second, mom_head_bias, *, groups, shards
):
    seqs, slots = token_ids.shape
    half = slots // 2
    vocab_rows, cols = embedding.shape
    width = cols * shards
    devices = groups * shards
    hidden = bias_up.shape[0]
    heads = width // HEAD_DIM
    dp_rank = lax.axis_index("dp")
    tp_rank = lax.axis_index("tensor")
    pair = tp_rank // 2
    side = tp_rank % 2
    base = dp_rank * vocab_rows

    whole_seq = 3 * pair + 2 * side
    split_seq = 3 * pair + 1
    whole_ids = lax.dynamic_index_in_dim(token_ids, whole_seq, 0, keepdims=False)
    split_ids = lax.dynamic_index_in_dim(token_ids, split_seq, 0, keepdims=False)
    ids = jnp.concatenate([whole_ids, lax.dynamic_slice_in_dim(split_ids, side * half, half)])
    count = ids.shape[0]
    whole_length = lax.dynamic_index_in_dim(lengths, whole_seq, 0, keepdims=False)
    split_length = lax.dynamic_index_in_dim(lengths, split_seq, 0, keepdims=False)

    all_attn = lax.all_gather(attn_weights, "tensor")
    parts_shape = (shards, count, hidden)
    all_ffn_down = lax.all_gather(ffn_weights[1], "tensor")
    small = jnp.concatenate([positions[2 : slots + 2], bias_qv, bias_up.reshape(-1, cols)], axis=0)
    small = jnp.pad(small, ((0, -small.shape[0] % 8), (0, 0)))
    swap = [(i, i ^ 1) for i in range(shards)]
    owner, rank = request_lists(ids, vocab_rows, groups)
    rounds_here = jnp.max(rank) // CAPACITY + 1

    def serve(round_index):
        wanted = round_list(ids, owner, rank, round_index, groups)
        lists = jnp.broadcast_to(wanted.reshape(groups, 1, CAPACITY), (groups, shards, CAPACITY))
        lists = lists.reshape(devices, CAPACITY)
        tail = jnp.broadcast_to(rounds_here, (devices, 1)).astype(jnp.int32)
        lists = jnp.concatenate([lists, tail, jnp.zeros((devices, 127 - CAPACITY), jnp.int32)], axis=1)
        asked = trade(lists)
        rows = asked[:, :CAPACITY].reshape(-1) - base
        rounds = jnp.max(asked[:, CAPACITY])
        return wanted, rows, rounds

    def find(rows):
        return jnp.take(embedding, rows, axis=0, mode="clip")

    def expand(wanted, landed):
        return expand_rows(ids, wanted, landed.reshape(groups, shards, CAPACITY, cols))

    wanted_first, rows_first, rounds = serve(0)
    found, up_weights = lax.optimization_barrier((find(rows_first), ffn_weights[0]))
    all_ffn_up, all_small = spread(up_weights, small, groups, 6)
    landed, all_small = lax.optimization_barrier((trade(found), all_small))
    all_positions = all_small[:, :slots].transpose(1, 0, 2).reshape(slots, width)
    all_bias_up = all_small[:, slots + 2 : slots + 2 + hidden // cols].reshape(-1)
    tokens = expand(wanted_first, landed)

    def more(state):
        return state[0] < rounds

    def fetch_more(state):
        round_index, total = state
        wanted, rows, _ = serve(round_index)
        return round_index + 1, total + expand(wanted, trade(find(rows)))

    _, tokens = lax.while_loop(more, fetch_more, (jnp.int32(1), tokens))
    own_positions = jnp.concatenate(
        [all_positions, lax.dynamic_slice_in_dim(all_positions, side * half, half)], axis=0
    )
    embedded = tokens + own_positions
    unit_zero, scale_zero = normalise(embedded)
    h_zero = unit_zero * norms[0] + norms[1]

    h_other = lax.ppermute(h_zero[slots:], "tensor", swap)
    bias_q, bias_v = all_small[:, slots], all_small[:, slots + 1]
    queries, keys_all, values = project(h_zero, h_other, all_attn, bias_q[:, None, :], bias_v[:, None, :])
    key_index = lax.broadcasted_iota(jnp.int32, (slots,), 0)
    own_first = jnp.where(
        key_index < half, side * half + key_index, (1 - side) * half + key_index - half
    )
    counted = jnp.concatenate([key_index < whole_length, own_first < split_length])
    key_bias = jnp.where(counted, 0.0, -1e30).astype(jnp.float32)[:, None]
    mixed, lse = attend_call(
        attend_kernel,
        slots,
        (queries, keys_all, values, key_bias),
        (queries.shape, (heads // 2, 2, count)),
    )
    x_one = gather_back(h_zero + norms[6], [(mixed, all_attn, 3)])
    unit_one, scale_one = normalise(x_one)
    h_one = unit_one * norms[2] + norms[3]

    bias_tiles = all_bias_up.reshape(shards, 1, hidden)
    act, act_slope = times(h_one, all_ffn_up, 0, gelu_tile, [bias_tiles], [parts_shape, parts_shape])
    x_two = gather_back(h_one + norms[7], [(act, all_ffn_down, 0)])
    unit_two, scale_two = normalise(x_two)
    h_two = unit_two * norms[4] + norms[5]

    slot = lax.broadcasted_iota(jnp.int32, (count,), 0)
    in_whole = slot < slots
    place = jnp.where(in_whole, slot, slot - slots + side * half)
    keep = place < jnp.where(in_whole, whole_length, split_length)
    weight_whole = jnp.where(keep & in_whole, 1.0 / whole_length.astype(jnp.float32), 0.0)
    weight_split = jnp.where(keep & ~in_whole, 1.0 / split_length.astype(jnp.float32), 0.0)
    sums = jnp.stack(
        [jnp.sum(h_two * weight_whole[:, None], axis=0), jnp.sum(h_two * weight_split[:, None], axis=0)]
    )
    all_sums = meet(sums.reshape(-1, 128), groups, shards, 5).reshape(groups * shards // 2, 2, 2, width)
    all_pooled = jnp.stack(
        [all_sums[:, 0, 0], all_sums[:, 0, 1] + all_sums[:, 1, 1], all_sums[:, 1, 0]], axis=1
    ).reshape(groups * seqs, width)
    loss, head_pull = jax.vjp(
        lambda rows, first_w, second_w, bias_w: contrast(rows, first_w, second_w, bias_w, partners),
        all_pooled,
        head_first,
        head_second,
        head_bias,
    )
    back_pooled, grad_head_first, grad_head_second, grad_head_bias = head_pull(jnp.ones_like(loss))
    first_row = dp_rank * seqs
    back_whole = lax.dynamic_index_in_dim(back_pooled, first_row + whole_seq, 0, keepdims=False)
    back_split = lax.dynamic_index_in_dim(back_pooled, first_row + split_seq, 0, keepdims=False)
    back_h_two = weight_whole[:, None] * back_whole[None, :] + weight_split[:, None] * back_split[None, :]

    back_x_two, grad_gain_two, grad_shift_two = normalise_back(back_h_two, norms[4], unit_two, scale_two)
    grad_down = outer(back_x_two, act, width, 0)
    sum_down = lax.psum_scatter(grad_down, "tensor", scatter_dimension=0, tiled=False)
    back_up, grad_bias_up = times(
        back_x_two, all_ffn_down, 0, scale_tile, [act_slope], [parts_shape, bias_tiles.shape]
    )
    grad_up = outer(h_one, back_up, width, 0)
    back_up, grad_up = lax.optimization_barrier((back_up, grad_up))
    sum_up = lax.psum_scatter(grad_up, "tensor", scatter_dimension=0, tiled=False)
    back_h_one = gather_back(back_x_two, [(back_up, all_ffn_up, 0)])
    back_x_one, grad_gain_one, grad_shift_one = normalise_back(back_h_one, norms[2], unit_one, scale_one)

    (back_mixed,) = times(back_x_one, all_attn, 3, keep_tile, [], [mixed.shape])
    back_q, back_k, back_v = attend_call(
        attend_back_kernel,
        slots,
        (queries, keys_all, values, key_bias, mixed, lse, back_mixed),
        (queries.shape, keys_all.shape, values.shape),
    )
    back_keys = gather_back(
        back_x_one, [(back_q, all_attn, 0), (back_k, all_attn, 1), (back_v, all_attn, 2)]
    )
    back_other = lax.ppermute(back_keys[count:], "tensor", swap)
    back_h_zero = back_keys[:count]
    back_h_zero = back_h_zero + jnp.pad(back_other, ((slots, 0), (0, 0)))
    back_embedded, grad_gain_zero, grad_shift_zero = normalise_back(back_h_zero, norms[0], unit_zero, scale_zero)

    def send_back(wanted):
        return pack(wanted, ids, back_embedded, groups, shards).reshape(devices * CAPACITY, cols)

    def add_rows(landed, rows, total):
        target = jnp.where(rows >= 0, rows, vocab_rows)
        return total.at[target].add(landed, mode="drop")

    leaving, back_q, back_k, back_v, back_x_one = lax.optimization_barrier(
        (send_back(wanted_first), back_q, back_k, back_v, back_x_one)
    )
    landed_first = trade(leaving)
    part_rows = 4 * width + slots + SMALL_ROWS
    parts_attn = outer_three(h_zero, h_other, back_q, back_k, back_v, part_rows)
    parts_attn = outer(back_x_one, mixed, part_rows, 3, parts_attn)
    grad_small = jnp.concatenate(
        [
            jnp.stack(
                [
                    grad_gain_zero,
                    grad_shift_zero,
                    grad_gain_one,
                    grad_shift_one,
                    grad_gain_two,
                    grad_shift_two,
                    jnp.sum(back_x_one, axis=0),
                    jnp.sum(back_x_two, axis=0),
                    jnp.sum(back_q, axis=1).reshape(-1),
                    jnp.sum(back_v, axis=1).reshape(-1),
                ]
            ),
            grad_bias_up.reshape(-1, width),
        ],
        axis=0,
    )
    half_rows = jnp.where(side == 0, 1.0, 0.0) * back_embedded[slots:]
    other_rows = back_embedded[slots:] - half_rows
    grad_pos_full = back_embedded[:slots] + jnp.concatenate([half_rows, other_rows], axis=0)
    grad_pos_parts = grad_pos_full.reshape(slots, shards, cols)
    grad_pos_parts = grad_pos_parts.transpose(1, 0, 2)
    small_size = grad_small.size
    small_rows = jnp.pad(grad_small.reshape(-1), (0, SMALL_ROWS * cols - small_size)).reshape(1, SMALL_ROWS, cols)
    small_rows = jnp.broadcast_to(small_rows, (shards, SMALL_ROWS, cols))
    parts_attn = lax.dynamic_update_slice(parts_attn, grad_pos_parts, (0, 4 * width, 0))
    parts_attn = lax.dynamic_update_slice(parts_attn, small_rows, (0, 4 * width + slots, 0))
    first_all = (dp_rank == 0).astype(jnp.float32) * (tp_rank == 0).astype(jnp.float32)
    head_squares = first_all * (squares(grad_head_first) + squares(grad_head_second) + squares(grad_head_bias))
    landed_first, parts_attn, head_squares = lax.optimization_barrier((landed_first, parts_attn, head_squares))
    sum_attn = lax.psum_scatter(parts_attn, "tensor", scatter_dimension=0, tiled=False)
    corner = (lax.broadcasted_iota(jnp.int32, (8, 128), 0) + lax.broadcasted_iota(jnp.int32, (8, 128), 1)) == 0
    tile = jnp.where(corner, head_squares, 0.0)
    (sum_down,), tile = ring_sum([sum_down], tile, groups, shards, 2, 0, 1)
    (sum_up,), squared = ring_sum([sum_up], tile, groups, shards, 2, 0, 3)
    landed_first, sum_up = lax.optimization_barrier((landed_first, sum_up))
    zero_table = jnp.zeros((vocab_rows, cols), jnp.float32)
    grad_embedding = add_rows(landed_first, rows_first, zero_table)

    def give_more(state):
        round_index, total = state
        wanted, rows, _ = serve(round_index)
        return round_index + 1, add_rows(trade(send_back(wanted)), rows, total)

    _, grad_embedding = lax.while_loop(more, give_more, (jnp.int32(1), grad_embedding))

    squared = squared + jnp.where(corner, squares(grad_embedding), 0.0)
    sum_attn, grad_embedding = lax.optimization_barrier((sum_attn, grad_embedding))
    (sum_attn,), squared = ring_sum([sum_attn], squared, groups, shards, 2, SMALL_ROWS, 2)
    sum_small = sum_attn[-SMALL_ROWS:].reshape(-1)[:small_size].reshape(grad_small.shape)
    grad_norms = sum_small[:8]
    grad_bias_qv = lax.dynamic_slice_in_dim(sum_small[8:10], tp_rank * cols, cols, 1)
    grad_bias_up = lax.dynamic_slice_in_dim(sum_small[10:].reshape(-1), tp_rank * hidden, hidden)
    grad_attn = sum_attn[: 4 * width].reshape(4, width, cols)
    grad_ffn_up, grad_ffn_down = sum_up, sum_down
    grad_pos = sum_attn[4 * width : -SMALL_ROWS]

    grad_norm = jnp.sqrt(jnp.sum(squared))
    factor = jnp.minimum(1.0, CLIP_SCALE * math.sqrt(PARAMS) / (grad_norm + 1e-06))
    grad_positions = jnp.pad(grad_pos, ((2, positions.shape[0] - slots - 2), (0, 0)))
    grad_ffn = jnp.stack([grad_ffn_up, grad_ffn_down])
    new_embedding, next_embedding = advance(embedding, mom_embedding, grad_embedding, factor)
    new_positions, next_positions = advance(positions, mom_positions, grad_positions, factor)
    new_attn, next_attn = advance(attn_weights, mom_attn, grad_attn, factor)
    new_ffn, next_ffn = advance(ffn_weights, ffn_momentum, grad_ffn, factor)
    new_bias_qv, next_bias_qv = advance(bias_qv, mom_bias_qv, grad_bias_qv, factor)
    new_bias_up, next_bias_up = advance(bias_up, mom_bias_up, grad_bias_up, factor)
    new_norms, next_norms = advance(norms, mom_norms, grad_norms, factor)
    new_head_first, next_head_first = advance(head_first, mom_head_first, grad_head_first, factor)
    new_head_second, next_head_second = advance(head_second, mom_head_second, grad_head_second, factor)
    new_head_bias, next_head_bias = advance(head_bias, mom_head_bias, grad_head_bias, factor)
    return (
        new_embedding, new_positions, new_attn, new_ffn, new_bias_qv, new_bias_up, new_norms, new_head_first,
        new_head_second, new_head_bias, next_embedding, next_positions, next_attn, next_ffn, next_bias_qv,
        next_bias_up, next_norms, next_head_first, next_head_second, next_head_bias, loss, grad_norm,
    )


def solution(mesh):
    in_specs = (
        P("dp", None),
        P("dp"),
        P(),
        P("dp", "tensor"),
        P(None, "tensor"),
        P(None, None, "tensor"),
        P(None, None, "tensor"),
        P(None, "tensor"),
        P("tensor"),
        P(),
        P(),
        P(),
        P(),
        P("dp", "tensor"),
        P(None, "tensor"),
        P(None, None, "tensor"),
        P(None, None, "tensor"),
        P(None, "tensor"),
        P("tensor"),
        P(),
        P(),
        P(),
        P(),
    )
    out_specs = (
        P("dp", "tensor"),
        P(None, "tensor"),
        P(None, None, "tensor"),
        P(None, None, "tensor"),
        P(None, "tensor"),
        P("tensor"),
        P(),
        P(),
        P(),
        P(),
        P("dp", "tensor"),
        P(None, "tensor"),
        P(None, None, "tensor"),
        P(None, None, "tensor"),
        P(None, "tensor"),
        P("tensor"),
        P(),
        P(),
        P(),
        P(),
        P(),
        P(),
    )
    groups, shards = mesh.shape["dp"], mesh.shape["tensor"]

    def run(*arrays):
        body = on_device
        if 2 * (arrays[0].shape[0] // groups) == 3 * shards:
            body = functools.partial(fast_on_device, groups=groups, shards=shards)
        return jax.shard_map(
            body, mesh=mesh, in_specs=in_specs, out_specs=out_specs, check_vma=False
        )(*arrays)

    return run
```
